32 devices in a mesh: ctx: 16 (over z, x, core), head: 2 (over y).
Axes of the slice: x: 2, y: 2, z: 4, core: 2. Of those that a mesh axis runs over, the one named last changes fastest.
Arguments:
- queries: bfloat16 [4096, 4096], P('ctx', 'head')
- keys: bfloat16 [4096, 1024], P(('ctx', 'head'))
- values: bfloat16 [4096, 1024], P(('ctx', 'head')), may hold values from -6 to 6
- selected: int32 [32, 8, 3], P('ctx', 'head'), may hold values from 0 to 6, as said below
Outputs:
- attended: bfloat16 [4096, 4096], P('ctx', 'head')
The draws below stay inside these ranges and needn't reach their ends.
Inputs may be any that keep to these rules, and one draw needn't show every extreme that they name: selected[t, g, :] names 3 different blocks of 512 positions that lie before the block of tile t; where fewer than 3 such blocks exist, the remaining entries equal the tile's own block and name nothing more.
All inputs are finite; a program needn't handle non-finite values.
Results may differ from the reference program's by a relative error of at most 0.0041.
Values may be sent and summed in bfloat16 or wider, within the bound.
No kernel may reach another device: no remote copies, remote signals or barrier semaphores. Data moves between devices by JAX's collectives and lax.ppermute only.
A program may use at most 64 MiB of HBM per device.

```python
import jax
import jax.numpy as jnp
from jax import lax

HD = 128
QH = 32
KVH = 8
BLK = 512
TILE = 128
TOPK = 3
SEQ = 4096
NB = 8
NT = 32


def draw_queries(key, part):
    result = jax.random.normal(jax.random.fold_in(key, 1), (SEQ, QH * HD), jnp.float32)
    return result.astype(jnp.bfloat16)


def draw_keys(key, part):
    result = jax.random.normal(jax.random.fold_in(key, 2), (SEQ, KVH * HD), jnp.float32)
    return result.astype(jnp.bfloat16)


def draw_selected(key, part):
    tile_ids = jnp.arange(NT, dtype=jnp.int32)
    own_block = tile_ids * TILE // BLK
    width_all = NB + TOPK
    candidate = jnp.arange(width_all, dtype=jnp.int32)
    random_part = jax.random.randint(key, (NT, KVH, width_all), 0, 1048576)
    ranking = random_part * width_all + candidate[None, None, :]
    earlier = candidate[None, None, :] < own_block[:, None, None]
    ranking = jnp.where(earlier, ranking, -1 - candidate[None, None, :])
    forced = (tile_ids == NT - 1)[:, None, None] & (candidate == NB - 2)[None, None, :]
    ranking = jnp.where(forced, 1048576 * width_all + width_all, ranking)
    unused, picked = lax.top_k(ranking, TOPK)
    picked = jnp.where(picked < own_block[:, None, None], picked, own_block[:, None, None])
    return picked.astype(jnp.int32)


def shard_levels(stream_key, shape, split, least, high):
    level = 1.0
    for dim, shards_of in split:
        heights = jax.random.uniform(jax.random.fold_in(jax.random.fold_in(stream_key, 6), dim), (shards_of,), jnp.float32, least / len(split), high / len(split))
        level = level * jnp.repeat(jnp.exp(heights), shape[dim] // shards_of).reshape((-1,) + (1,) * (len(shape) - 1 - dim))
    return level


def gaussian(key, dims, deviation, reach, cuts=(), held_as=jnp.bfloat16):
    gain = shard_levels(key, dims, cuts, -0.22, 0.18) if cuts else 1.0
    drawn = jax.random.normal(key, dims, jnp.float32) * deviation * gain
    return jnp.minimum(jnp.maximum(drawn, -reach), reach).astype(held_as)


def setup_inputs(seed: int = 0) -> dict:
    splits = jax.random.split(jax.random.key(seed), 5)
    return {
        "queries": draw_queries(jax.random.fold_in(splits[4], 71), 0),
        "keys": draw_keys(jax.random.fold_in(splits[4], 71), 0),
        "values": gaussian(splits[2], (SEQ, KVH * HD), 1.0, 6.0, ((0, 32),)),
        "selected": draw_selected(jax.random.fold_in(splits[4], 71), 0),
    }


def reference(queries, keys, values, selected):
    seq_len = queries.shape[0]
    per_group = QH // KVH
    score_scale = HD ** -0.5
    query_tiles = queries.reshape(NT, TILE, KVH, per_group, HD)
    key_heads = keys.reshape(seq_len, KVH, HD)
    value_heads = values.reshape(seq_len, KVH, HD)
    group_ids = jnp.arange(KVH, dtype=jnp.int32)
    offsets = jnp.arange(BLK, dtype=jnp.int32)
    slot_ids = jnp.arange((TOPK + 1) * BLK, dtype=jnp.int32) // BLK

    def one_tile(tile):
        tile_queries = lax.dynamic_index_in_dim(query_tiles, tile, 0, keepdims=False)
        own_block = (tile * TILE) // BLK
        chosen = lax.dynamic_index_in_dim(selected, tile, 0, keepdims=False)
        own_column = jnp.zeros((KVH, 1), jnp.int32) + own_block
        blocks = jnp.concatenate([chosen.astype(jnp.int32), own_column.astype(jnp.int32)], axis=1)
        key_pos = (blocks[:, :, None] * BLK + offsets[None, None, :]).reshape(KVH, (TOPK + 1) * BLK)
        tile_keys = key_heads[key_pos, group_ids[:, None]]
        tile_values = value_heads[key_pos, group_ids[:, None]]
        query_pos = tile * TILE + jnp.arange(TILE, dtype=jnp.int32)
        slot_block = blocks[:, slot_ids]
        from_list = (slot_ids < TOPK)[None, :] & (slot_block != own_block)
        causal = (slot_ids == TOPK)[None, None, :] & (key_pos[:, None, :] <= query_pos[None, :, None])
        allowed = from_list[:, None, :] | causal
        scores = jnp.einsum('qgjd,gkd->gjqk', tile_queries.astype(jnp.float32), tile_keys.astype(jnp.float32)) * score_scale
        scores = jnp.where(allowed[:, None], scores, -jnp.inf)
        row_max = jnp.max(scores, axis=-1, keepdims=True)
        raw_weights = jnp.exp(scores - row_max)
        totals = jnp.sum(raw_weights, axis=-1)
        rounded = lax.optimization_barrier(raw_weights.astype(jnp.bfloat16)).astype(jnp.float32)
        mixed = jnp.einsum('gjqk,gkd->gjqd', rounded, tile_values.astype(jnp.float32)) / totals[..., None]
        return jnp.transpose(mixed, (2, 0, 1, 3)).reshape(TILE, QH * HD).astype(jnp.bfloat16)

    tiles_out = lax.map(one_tile, jnp.arange(NT, dtype=jnp.int32))
    return tiles_out.reshape(seq_len, QH * HD)
```

```python
import functools
import math

import jax
import jax.numpy as jnp
from jax import lax
from jax.experimental import pallas as pl
from jax.experimental.pallas import tpu as pltpu
from jax.sharding import Mesh, PartitionSpec as P

HD = 128
QH = 32
KVH = 8
BLK = 512
TILE = 128
TOPK = 3
PER = QH // KVH
QW = PER * HD

FLOOR = -1e30
SCALE = HD ** -0.5 * math.log2(math.e)
NONE = -100000
F32 = jnp.float32
BF16 = jnp.bfloat16


def dot_nt(a, b):
    return lax.dot_general(a, b, (((1,), (1,)), ((), ())), preferred_element_type=F32)


def dot_nn(a, b):
    return lax.dot_general(a, b, (((1,), (0,)), ((), ())), preferred_element_type=F32)


def attention(levels, first, last, flipped, bases_of, queries, sel, sources, state):
    parts, rows = queries.shape[0], queries.shape[1] // TILE * TILE
    tiles = parts * rows // TILE
    tiles_in_part = rows // TILE
    chunk_rows = sources[0].shape[2]
    per_block = BLK // chunk_rows
    n_src = len(sources)

    def kernel(*refs):
        sel_ref, q_ref = refs[:2]
        src = refs[2 : 2 + n_src]
        rest = refs[2 + n_src :]
        if not first:
            m_in, l_in, acc_in = rest[:3]
            rest = rest[3:]
        if last:
            out_ref, m_ref, l_ref, acc_ref = rest
        else:
            m_ref, l_ref, acc_ref = rest
        level = lax.axis_index("lev")
        bases = bases_of(level)

        def key_rows(ref, block, count):
            part = ref[pl.ds(block * per_block, count // chunk_rows), 0]
            return part.reshape(count, HD)

        def value_columns(ref, block, count):
            n = count // chunk_rows
            if flipped:
                pieces = [ref[block * per_block + i, 1] for i in range(n)]
                return jnp.concatenate(pieces, axis=1) if n > 1 else pieces[0]
            part = ref[pl.ds(block * per_block, n), 1]
            return part.reshape(count, HD).T

        def one_tile(t, carry):
            slot = 0 if last else t
            part, at = t // tiles_in_part, lax.rem(t, tiles_in_part) * TILE
            tile = level * tiles + t
            own = tile * TILE // BLK
            rows4 = q_ref[part, pl.ds(pl.multiple_of(at, TILE), TILE), :]
            q = jnp.concatenate([rows4[:, j * HD : (j + 1) * HD] for j in range(PER)], axis=0)

            def own_part(pieces):
                count = pieces * TILE
                block = own - bases[0]
                s = dot_nt(key_rows(src[0], block, count), q)
                key_at = lax.broadcasted_iota(jnp.int32, s.shape, 0)
                query_at = lax.rem(lax.broadcasted_iota(jnp.int32, s.shape, 1), TILE)
                s = jnp.where(key_at <= query_at + (count - TILE), s, FLOOR)
                m = jnp.max(s, axis=0, keepdims=True)
                p = jnp.exp2((s - m) * SCALE)
                m_ref[slot] = m
                l_ref[slot] = jnp.sum(p, axis=0, keepdims=True)
                acc_ref[slot] = dot_nn(value_columns(src[0], block, count), p.astype(BF16))

            if first:
                for pieces in range(1, BLK // TILE + 1):
                    pl.when(lax.rem(tile, BLK // TILE) == pieces - 1)(
                        functools.partial(own_part, pieces)
                    )
            else:
                m_ref[slot] = m_in[t]
                l_ref[slot] = l_in[t]
                acc_ref[slot] = acc_in[t]

            def other(e, carry):
                block = sel_ref[t * TOPK + e]
                for ref, base in zip(src, bases):
                    blocks = ref.shape[0] // per_block

                    @pl.when((block != own) & (block >= base) & (block < base + blocks))
                    def _():
                        s = dot_nt(key_rows(ref, block - base, BLK), q)
                        old = m_ref[slot]
                        m = jnp.maximum(old, jnp.max(s, axis=0, keepdims=True))
                        p = jnp.exp2((s - m) * SCALE)
                        fade = jnp.exp2((old - m) * SCALE)
                        m_ref[slot] = m
                        l_ref[slot] = l_ref[slot] * fade + jnp.sum(p, axis=0, keepdims=True)
                        acc_ref[slot] = acc_ref[slot] * fade + dot_nn(
                            value_columns(ref, block - base, BLK), p.astype(BF16)
                        )

                return carry

            lax.fori_loop(0, TOPK, other, 0)
            if last:
                mixed = acc_ref[0] / l_ref[0]
                for j in range(PER):
                    out_ref[part, pl.ds(pl.multiple_of(at, TILE), TILE), j * HD : (j + 1) * HD] = (
                        mixed[:, j * HD : (j + 1) * HD].T.astype(BF16)
                    )
            return carry

        lax.fori_loop(0, tiles, one_tile, 0)

    kept = (
        jax.ShapeDtypeStruct((tiles, 1, QW), F32),
        jax.ShapeDtypeStruct((tiles, 1, QW), F32),
        jax.ShapeDtypeStruct((tiles, HD, QW), F32),
    )
    vmem = pl.BlockSpec(memory_space=pltpu.VMEM)
    return pl.pallas_call(
        kernel,
        in_specs=[pl.BlockSpec(memory_space=pltpu.SMEM)] + [vmem] * (1 + n_src + len(state)),
        out_shape=jax.ShapeDtypeStruct((parts, rows, QW), BF16) if last else kept,
        out_specs=vmem if last else (vmem,) * 3,
        scratch_shapes=[
            pltpu.VMEM((1, 1, QW), F32),
            pltpu.VMEM((1, 1, QW), F32),
            pltpu.VMEM((1, HD, QW), F32),
        ]
        if last
        else [],
        compiler_params=pltpu.CompilerParams(vmem_limit_bytes=50 * 1024 * 1024),
        cost_estimate=pl.CostEstimate(
            flops=4 * n_src * tiles * QW * BLK * HD,
            transcendentals=n_src * tiles * QW * BLK,
            bytes_accessed=8 * 1024 * 1024,
        ),
    )(sel, queries, *sources, *state)


def body(levels, subs, heads, queries, keys, values, selected):
    rows = queries.shape[0]
    r = keys.shape[0]
    tiles_here = selected.shape[0]
    flipped = r == HD

    def by_owner(a, flip):
        a = a.reshape(r, heads, subs, HD)
        a = jnp.transpose(a, (2, 1, 3, 0) if flip else (2, 1, 0, 3))
        return a.reshape(subs * heads, 1, r, HD)

    packed = jnp.concatenate([by_owner(keys, False), by_owner(values, flipped)], axis=1)
    own = lax.all_to_all(packed, ("sub", "head"), 0, 0, tiled=True)

    picks = jnp.transpose(selected, (1, 0, 2)).reshape(subs, 1, tiles_here * TOPK).astype(BF16)
    picks = jnp.pad(picks, ((0, 0), (0, 15), (0, QW - tiles_here * TOPK)))
    q = jnp.transpose(queries.reshape(rows, subs, QW), (1, 0, 2))
    q = jnp.concatenate([q, picks], axis=1)
    if subs > 1:
        q = lax.all_to_all(q, "sub", 0, 0, tiled=True)
    sel = q[:, rows, : tiles_here * TOPK].astype(jnp.int32).reshape(-1)

    level_blocks = subs * rows // BLK
    if levels == 4 and subs * rows % BLK == 0:
        level = lax.axis_index("lev")
        p1 = lax.ppermute(own, "lev", [(0, 2), (2, 3)])
        p2 = lax.ppermute(own, "lev", [(1, 3), (0, 1)])
        p3 = lax.ppermute(jnp.where(level == 2, p1, own), "lev", [(2, 3), (1, 2)])

        def at(level, *which):
            base = jnp.int32(NONE)
            for here, holds in which:
                base = jnp.where(level == here, holds * level_blocks, base)
            return base

        def early(level):
            return (level * level_blocks, at(level, (2, 0), (3, 2)), at(level, (1, 0), (3, 1)))

        def late(level):
            return (at(level, (2, 1), (3, 0)),)

        state = attention(levels, True, False, flipped, early, q, sel, (own, p1, p2), ())
        out = attention(levels, False, True, flipped, late, q, sel, (p3,), state)
    else:
        whole = lax.all_gather(own, "lev", axis=0, tiled=True)
        out = attention(
            levels, True, True, flipped, lambda level: (0,), q, sel, (whole,), ()
        )
    if subs > 1:
        out = lax.all_to_all(out, "sub", 0, 0, tiled=True)
    return jnp.transpose(out, (1, 0, 2)).reshape(rows, subs * QW)


def solution(mesh):
    ctx, heads = mesh.shape["ctx"], mesh.shape["head"]
    subs = math.gcd(KVH // heads, ctx)
    if subs * heads != KVH:
        raise ValueError("unsupported mesh")
    levels = ctx // subs
    split = Mesh(mesh.devices.reshape(levels, subs, heads), ("lev", "sub", "head"))
    placed = (
        P(("lev", "sub"), "head"),
        P(("lev", "sub", "head"), None),
        P(("lev", "sub", "head"), None),
        P(("lev", "sub"), "head", None),
    )
    return jax.shard_map(
        functools.partial(body, levels, subs, heads),
        mesh=split,
        in_specs=placed,
        out_specs=P(("lev", "sub"), "head"),
        check_vma=False,
    )
```

```python
import functools
import math

import jax
import jax.numpy as jnp
from jax import lax
from jax.experimental import pallas as pl
from jax.experimental.pallas import tpu as pltpu
from jax.sharding import Mesh, PartitionSpec as P

HD = 128
QH = 32
KVH = 8
BLK = 512
TILE = 128
TOPK = 3
PER = QH // KVH
QW = PER * HD
EXTRA = 16

FLOOR = -1e30
SCALE = HD ** -0.5 * math.log2(math.e)
NONE = -100000
F32 = jnp.float32
BF16 = jnp.bfloat16
VMEM = pl.BlockSpec(memory_space=pltpu.VMEM)
SMEM = pl.BlockSpec(memory_space=pltpu.SMEM)
MIB = 1024 * 1024


def dot_nt(a, b):
    return lax.dot_general(a, b, (((1,), (1,)), ((), ())), preferred_element_type=F32)


def dot_nn(a, b):
    return lax.dot_general(a, b, (((1,), (0,)), ((), ())), preferred_element_type=F32)


def copy_cost(bytes_moved):
    return pl.CostEstimate(flops=0, transcendentals=0, bytes_accessed=bytes_moved)


def pack_keys_values(subs, heads, keys, values):
    r = keys.shape[0]

    def kernel(k_ref, v_ref, out_ref):
        for sub in range(subs):
            for head in range(heads):
                at = (head * subs + sub) * HD
                out_ref[sub * heads + head, 0] = k_ref[:, at : at + HD]
                out_ref[sub * heads + head, 1] = v_ref[:, at : at + HD]

    return pl.pallas_call(
        kernel,
        in_specs=[VMEM, VMEM],
        out_specs=VMEM,
        out_shape=jax.ShapeDtypeStruct((subs * heads, 2, r, HD), BF16),
        cost_estimate=copy_cost(4 * keys.size * 2),
        compiler_params=pltpu.CompilerParams(vmem_limit_bytes=8 * MIB),
        name="pack_kv",
    )(keys, values)


def pack_queries(subs, queries, selected):
    rows = queries.shape[0]
    tiles_here = selected.shape[0]

    def kernel(sel_ref, q_ref, *outs):
        sub = lax.axis_index("sub") if subs > 1 else 0
        lane = lax.broadcasted_iota(jnp.int32, (EXTRA, QW), 1)
        for k, out_ref in enumerate(outs):
            head = sub ^ k
            out_ref[:rows] = q_ref[:, pl.ds(pl.multiple_of(head * QW, QW), QW)]
            row = jnp.zeros((EXTRA, QW), jnp.int32)
            for t in range(tiles_here):
                for e in range(TOPK):
                    row = jnp.where(lane == t * TOPK + e, sel_ref[t, head, e], row)
            out_ref[rows:] = row.astype(F32).astype(BF16)

    return pl.pallas_call(
        kernel,
        in_specs=[SMEM, VMEM],
        out_specs=(VMEM,) * subs,
        out_shape=(jax.ShapeDtypeStruct((rows + EXTRA, QW), BF16),) * subs,
        cost_estimate=copy_cost(2 * queries.size * 2),
        compiler_params=pltpu.CompilerParams(vmem_limit_bytes=8 * MIB),
        name="pack_q",
    )(selected, queries)


def unpack_output(subs, pieces):
    rows = pieces[0].shape[0]

    def kernel(*refs):
        sub = lax.axis_index("sub")
        for k in range(subs):
            at = pl.multiple_of((sub ^ k) * QW, QW)
            refs[subs][:, pl.ds(at, QW)] = refs[k][...]

    return pl.pallas_call(
        kernel,
        in_specs=[VMEM] * subs,
        out_specs=VMEM,
        out_shape=jax.ShapeDtypeStruct((rows, subs * QW), BF16),
        cost_estimate=copy_cost(4 * subs * rows * QW),
        compiler_params=pltpu.CompilerParams(vmem_limit_bytes=8 * MIB),
        name="unpack",
    )(*pieces)


def attention(name, first, last, partners, bases_of, queries, sel, sources, state):
    parts, rows = len(queries), queries[0].shape[0] - EXTRA
    tiles_in_part = rows // TILE
    tiles = parts * tiles_in_part
    r = sources[0].shape[2]
    per_block = BLK // r
    n_src = len(sources)
    slots = [src.shape[0] // per_block for src in sources]
    most = min(TOPK, sum(slots))
    n_q = len(partners)
    n_out = len(partners) if last else 2

    def kernel(*refs):
        sel_ref, q_refs = refs[0], refs[1 : 1 + n_q]
        src = refs[1 + n_q : 1 + n_q + n_src]
        rest = refs[1 + n_q + n_src :]
        m_in, acc_in = (None, None) if first else rest[:2]
        rest = rest if first else rest[2:]
        outs, k_buf, v_buf, m_tmp, acc_tmp, q_buf = rest[:n_out], *rest[n_out:]
        level = lax.axis_index("lev")
        sub = lax.axis_index("sub") if parts > 1 else 0
        for i, q_ref in enumerate(q_refs):
            q_buf[i] = q_ref[:rows]
        bases = bases_of(level)

        v_buf[:, HD:] = jnp.ones((sum(slots) * BLK, HD), BF16)
        start = 0
        for ref, base, n in zip(src, bases, slots):

            def fill(ref=ref, start=start, n=n):
                if n * per_block <= 8:
                    k_buf[start * BLK : (start + n) * BLK] = ref[:, 0].reshape(n * BLK, HD)
                    v_buf[start * BLK : (start + n) * BLK, :HD] = ref[:, 1].reshape(n * BLK, HD)
                else:

                    def chunk(i, carry):
                        at = pl.ds(pl.multiple_of(start * BLK + i * r, r), r)
                        k_buf[at] = ref[i, 0]
                        v_buf[at, :HD] = ref[i, 1]
                        return carry

                    lax.fori_loop(0, n * per_block, chunk, 0)

            if isinstance(base, int):
                fill()
            else:
                pl.when(base >= 0)(fill)
            start += n

        def one_tile(k, part, i, out_ref, out_at):
            t = k * tiles_in_part + i
            tile = level * tiles + (sub ^ k) * tiles_in_part + i
            own = tile * TILE // BLK
            q_rows = pl.ds(pl.multiple_of(i * TILE, TILE), TILE)
            m_old, acc_old, at_old = (m_tmp, acc_tmp, 0) if first else (m_in, acc_in, t)

            def finish(j, acc):
                out_ref[out_at, j * HD : (j + 1) * HD] = (acc[:, :HD] / acc[:, HD:]).astype(BF16)

            def keep(j, m, acc):
                outs[0][t, j * TILE : (j + 1) * TILE] = m
                outs[1][t, j * TILE : (j + 1) * TILE] = acc

            def own_part(pieces):
                count = pieces * TILE
                at = pl.ds(pl.multiple_of((own - bases[0]) * BLK, BLK), count)
                key_at = lax.broadcasted_iota(jnp.int32, (TILE, TILE), 1)
                query_at = lax.broadcasted_iota(jnp.int32, (TILE, TILE), 0)
                for j in range(PER):
                    s = dot_nt(q_buf[part, q_rows, j * HD : (j + 1) * HD], k_buf[at])
                    edge = jnp.where(key_at <= query_at, s[:, count - TILE :], FLOOR)
                    s = jnp.concatenate([s[:, : count - TILE], edge], axis=1) if pieces > 1 else edge
                    m = jnp.max(s, axis=1, keepdims=True)
                    p = jnp.exp2((s - m) * SCALE).astype(BF16)
                    m_tmp[0, j * TILE : (j + 1) * TILE] = jnp.broadcast_to(m, (TILE, HD))
                    acc_tmp[0, j * TILE : (j + 1) * TILE] = dot_nn(p, v_buf[at])

            if first:
                for pieces in range(1, BLK // TILE + 1):
                    pl.when(lax.rem(tile, BLK // TILE) == pieces - 1)(
                        functools.partial(own_part, pieces)
                    )

            found = jnp.int32(0)
            where = [jnp.int32(0)] * most
            for e in range(TOPK):
                block = sel_ref[t * TOPK + e]
                start = 0
                for base, n in zip(bases, slots):
                    hit = (block != own) & (block >= base) & (block < base + n)
                    where = [
                        jnp.where(hit & (found == i), start + block - base, w)
                        for i, w in enumerate(where)
                    ]
                    found = found + hit.astype(jnp.int32)
                    start += n

            def others(n):
                at = [pl.ds(pl.multiple_of(w * BLK, BLK), BLK) for w in where[:n]]
                for j in range(PER):
                    here = slice(j * TILE, (j + 1) * TILE)
                    old = m_old[at_old, here]
                    acc = acc_old[at_old, here]
                    if n:
                        q = q_buf[part, q_rows, j * HD : (j + 1) * HD]
                        s = [dot_nt(q, k_buf[a]) for a in at]
                        s = jnp.concatenate(s, axis=1) if n > 1 else s[0]
                        m = jnp.maximum(old, jnp.max(s, axis=1, keepdims=True))
                        p = jnp.exp2((s - jnp.tile(m, (1, n * BLK // HD))) * SCALE).astype(BF16)
                        fade = jnp.exp2((old - m) * SCALE)
                        acc = acc * jnp.tile(fade, (1, 2))
                        for i, a in enumerate(at):
                            acc = acc + dot_nn(p[:, i * BLK : (i + 1) * BLK], v_buf[a])
                        old = m
                    if last:
                        finish(j, acc)
                    else:
                        keep(j, old, acc)

            for n in range(most + 1):
                pl.when(found == n)(functools.partial(others, n))

        if last:
            for part, (out_ref, k) in enumerate(zip(outs, partners)):

                def step(i, carry, out_ref=out_ref, k=k, part=part):
                    out_at = pl.ds(pl.multiple_of(i * TILE, TILE), TILE)
                    one_tile(k, part, i, out_ref, out_at)
                    return carry

                lax.fori_loop(0, tiles_in_part, step, 0)
        else:

            def step(t, carry):
                k = t // tiles_in_part
                one_tile(k, k, lax.rem(t, tiles_in_part), None, None)
                return carry

            lax.fori_loop(0, tiles, step, 0)

    if last:
        out_shape = tuple(jax.ShapeDtypeStruct((rows, QW), BF16) for _ in partners)
    else:
        out_shape = (
            jax.ShapeDtypeStruct((tiles, QW, HD), F32),
            jax.ShapeDtypeStruct((tiles, QW, 2 * HD), F32),
        )
    work = (tiles if not last else len(partners) * tiles_in_part) * QW * BLK * (1 + n_src) // 2
    return pl.pallas_call(
        kernel,
        in_specs=[SMEM] + [VMEM] * (n_q + n_src + len(state)),
        out_shape=out_shape,
        out_specs=(VMEM,) * n_out,
        scratch_shapes=[
            pltpu.VMEM((sum(slots) * BLK, HD), BF16),
            pltpu.VMEM((sum(slots) * BLK, 2 * HD), BF16),
            pltpu.VMEM((1, QW, HD), F32),
            pltpu.VMEM((1, QW, 2 * HD), F32),
            pltpu.VMEM((n_q, rows, QW), BF16),
        ],
        compiler_params=pltpu.CompilerParams(
            vmem_limit_bytes=(24 if sum(slots) <= 16 else 56) * MIB
        ),
        cost_estimate=pl.CostEstimate(
            flops=8 * work * HD, transcendentals=work, bytes_accessed=4 * MIB
        ),
        name=name,
    )(sel, *[queries[k] for k in partners], *sources, *state)


def body(levels, subs, heads, queries, keys, values, selected):
    rows = queries.shape[0]
    tiles_here = selected.shape[0]
    level_blocks = subs * rows // BLK
    by_levels = levels == 4 and subs * rows % BLK == 0

    def exchange(pieces):
        return tuple(
            lax.ppermute(piece, "sub", [(i, i ^ k) for i in range(subs)]) if k else piece
            for k, piece in enumerate(pieces)
        )

    packed = pack_keys_values(subs, heads, keys, values)
    if by_levels:
        p1 = lax.ppermute(packed, "lev", [(0, 2), (2, 3)])
    own = lax.all_to_all(packed, ("sub", "head"), 0, 0, tiled=True)
    q = pack_queries(subs, queries, selected)
    q = exchange(q)
    sel = jnp.concatenate([piece[rows, : tiles_here * TOPK] for piece in q]).astype(jnp.int32)

    everyone = tuple(range(subs))
    if by_levels:
        p1 = lax.all_to_all(p1, ("sub", "head"), 0, 0, tiled=True)
        p2 = lax.ppermute(own, "lev", [(1, 3), (0, 1)])
        later, p1 = lax.optimization_barrier((own, p1))
        p3 = lax.ppermute(p1, "lev", [(2, 3)])
        p4 = lax.ppermute(later, "lev", [(1, 2)])

        def at(level, *which):
            base = jnp.int32(NONE)
            for here, holds in which:
                base = jnp.where(level == here, holds * level_blocks, base)
            return base

        def early(level):
            return (level * level_blocks, at(level, (2, 0), (3, 2)), at(level, (1, 0), (3, 1)))

        def late(level):
            return (at(level, (3, 0)), at(level, (2, 1)))

        state = attention(
            "early", True, False, everyone, early, q, sel, (own, p1, p2), ()
        )
        far, near = everyone[subs // 2 :], everyone[: subs // 2]
        out_far = attention("late_far", False, True, far, late, q, sel, (p3, p4), state)
        out_near = attention("late_near", False, True, near, late, q, sel, (p3, p4), state)
        out = out_near + out_far
    else:
        whole = lax.all_gather(own, "lev", axis=0, tiled=True)
        out = attention(
            "all", True, True, everyone, lambda level: (0,), q, sel, (whole,), ()
        )
    out = exchange(out)
    return unpack_output(subs, out) if subs > 1 else out[0]


def solution(mesh):
    ctx, heads = mesh.shape["ctx"], mesh.shape["head"]
    subs = math.gcd(KVH // heads, ctx)
    if subs * heads != KVH:
        raise ValueError("unsupported mesh")
    levels = ctx // subs
    split = Mesh(mesh.devices.reshape(levels, subs, heads), ("lev", "sub", "head"))
    placed = (
        P(("lev", "sub"), "head"),
        P(("lev", "sub", "head"), None),
        P(("lev", "sub", "head"), None),
        P(("lev", "sub"), "head", None),
    )
    return jax.shard_map(
        functools.partial(body, levels, subs, heads),
        mesh=split,
        in_specs=placed,
        out_specs=P(("lev", "sub"), "head"),
        check_vma=False,
    )
```

```python
import functools
import math

import jax
import jax.numpy as jnp
from jax import lax
from jax.experimental import pallas as pl
from jax.experimental.pallas import tpu as pltpu
from jax.sharding import Mesh, PartitionSpec as P

HD = 128
QH = 32
KVH = 8
BLK = 512
TILE = 128
TOPK = 3
PER = QH // KVH
QW = PER * HD
EXTRA = 16

FLOOR = -1e30
SCALE = HD ** -0.5 * math.log2(math.e)
NONE = -100000
F32 = jnp.float32
BF16 = jnp.bfloat16
VMEM = pl.BlockSpec(memory_space=pltpu.VMEM)
SMEM = pl.BlockSpec(memory_space=pltpu.SMEM)
HBM = pl.BlockSpec(memory_space=pltpu.HBM)
MIB = 1024 * 1024


def dot_nt(a, b):
    return lax.dot_general(a, b, (((1,), (1,)), ((), ())), preferred_element_type=F32)


def dot_nn(a, b):
    return lax.dot_general(a, b, (((1,), (0,)), ((), ())), preferred_element_type=F32)


def copy_cost(bytes_moved):
    return pl.CostEstimate(flops=0, transcendentals=0, bytes_accessed=bytes_moved)


def pack_keys_values(subs, heads, keys, values):
    r = keys.shape[0]

    def kernel(k_ref, v_ref, out_ref, sems):
        copies = []
        for sub in range(subs):
            for head in range(heads):
                at = pl.ds((head * subs + sub) * HD, HD)
                chunk = sub * heads + head
                for i, ref in enumerate((k_ref, v_ref)):
                    copies.append(
                        pltpu.make_async_copy(
                            ref.at[:, at], out_ref.at[chunk, i], sems.at[2 * chunk + i]
                        )
                    )
        for copy in copies:
            copy.start()
        for copy in copies:
            copy.wait()

    return pl.pallas_call(
        kernel,
        in_specs=[HBM, HBM],
        out_specs=HBM,
        out_shape=jax.ShapeDtypeStruct((subs * heads, 2, r, HD), BF16),
        scratch_shapes=[pltpu.SemaphoreType.DMA((2 * subs * heads,))],
        cost_estimate=copy_cost(4 * keys.size * 2),
        name="pack_kv",
    )(keys, values)


def pack_queries(subs, queries, selected):
    rows = queries.shape[0]
    tiles_here = selected.shape[0]

    def kernel(sel_ref, q_ref, *outs):
        sub = lax.axis_index("sub") if subs > 1 else 0
        lane = lax.broadcasted_iota(jnp.int32, (EXTRA, QW), 1)
        for k, out_ref in enumerate(outs):
            head = sub ^ k
            out_ref[:rows] = q_ref[:, pl.ds(pl.multiple_of(head * QW, QW), QW)]
            row = jnp.zeros((EXTRA, QW), jnp.int32)
            for t in range(tiles_here):
                for e in range(TOPK):
                    row = jnp.where(lane == t * TOPK + e, sel_ref[t, head, e], row)
            out_ref[rows:] = row.astype(F32).astype(BF16)

    return pl.pallas_call(
        kernel,
        in_specs=[SMEM, VMEM],
        out_specs=(VMEM,) * subs,
        out_shape=(jax.ShapeDtypeStruct((rows + EXTRA, QW), BF16),) * subs,
        cost_estimate=copy_cost(2 * queries.size * 2),
        compiler_params=pltpu.CompilerParams(vmem_limit_bytes=8 * MIB),
        name="pack_q",
    )(selected, queries)


def unpack_output(subs, pieces):
    rows = pieces[0].shape[0]

    def kernel(*refs):
        sub = lax.axis_index("sub")
        for k in range(subs):
            at = pl.multiple_of((sub ^ k) * QW, QW)
            refs[subs][:, pl.ds(at, QW)] = refs[k][...]

    return pl.pallas_call(
        kernel,
        in_specs=[VMEM] * subs,
        out_specs=VMEM,
        out_shape=jax.ShapeDtypeStruct((rows, subs * QW), BF16),
        cost_estimate=copy_cost(4 * subs * rows * QW),
        compiler_params=pltpu.CompilerParams(vmem_limit_bytes=8 * MIB),
        name="unpack",
    )(*pieces)


def attention(name, first, last, partners, bases_of, queries, sel, sources, state):
    parts, rows = len(queries), queries[0].shape[0] - EXTRA
    tiles_in_part = rows // TILE
    tiles = parts * tiles_in_part
    r = sources[0].shape[2]
    per_block = BLK // r
    n_src = len(sources)
    slots = [src.shape[0] // per_block for src in sources]
    most = min(TOPK, sum(slots))
    n_q = len(partners)
    n_out = len(partners) if last else 2

    def kernel(*refs):
        sel_ref, q_refs = refs[0], refs[1 : 1 + n_q]
        src = refs[1 + n_q : 1 + n_q + n_src]
        rest = refs[1 + n_q + n_src :]
        m_in, acc_in = (None, None) if first else rest[:2]
        rest = rest if first else rest[2:]
        outs, k_buf, v_buf, m_tmp, acc_tmp, q_buf = rest[:n_out], *rest[n_out:]
        level = lax.axis_index("lev")
        sub = lax.axis_index("sub") if parts > 1 else 0
        for i, q_ref in enumerate(q_refs):
            q_buf[i] = q_ref[:rows]
        bases = bases_of(level)

        v_buf[:, HD:] = jnp.ones((sum(slots) * BLK, HD), BF16)
        start = 0
        for ref, base, n in zip(src, bases, slots):

            def fill(ref=ref, start=start, n=n):
                if n * per_block <= 8:
                    k_buf[start * BLK : (start + n) * BLK] = ref[:, 0].reshape(n * BLK, HD)
                    v_buf[start * BLK : (start + n) * BLK, :HD] = ref[:, 1].reshape(n * BLK, HD)
                else:

                    def chunk(i, carry):
                        at = pl.ds(pl.multiple_of(start * BLK + i * r, r), r)
                        k_buf[at] = ref[i, 0]
                        v_buf[at, :HD] = ref[i, 1]
                        return carry

                    lax.fori_loop(0, n * per_block, chunk, 0)

            if isinstance(base, int):
                fill()
            else:
                pl.when(base >= 0)(fill)
            start += n

        def one_tile(k, part, i, out_ref, out_at):
            t = k * tiles_in_part + i
            tile = level * tiles + (sub ^ k) * tiles_in_part + i
            own = tile * TILE // BLK
            q_rows = pl.ds(pl.multiple_of(i * TILE, TILE), TILE)
            m_old, acc_old, at_old = (m_tmp, acc_tmp, 0) if first else (m_in, acc_in, t)

            def finish(j, acc):
                out_ref[out_at, j * HD : (j + 1) * HD] = (acc[:, :HD] / acc[:, HD:]).astype(BF16)

            def keep(j, m, acc):
                outs[0][t, j * TILE : (j + 1) * TILE] = m
                outs[1][t, j * TILE : (j + 1) * TILE] = acc

            def own_part(pieces):
                count = pieces * TILE
                at = pl.ds(pl.multiple_of((own - bases[0]) * BLK, BLK), count)
                key_at = lax.broadcasted_iota(jnp.int32, (TILE, TILE), 1)
                query_at = lax.broadcasted_iota(jnp.int32, (TILE, TILE), 0)
                for j in range(PER):
                    s = dot_nt(q_buf[part, q_rows, j * HD : (j + 1) * HD], k_buf[at])
                    edge = jnp.where(key_at <= query_at, s[:, count - TILE :], FLOOR)
                    s = jnp.concatenate([s[:, : count - TILE], edge], axis=1) if pieces > 1 else edge
                    m = jnp.max(s, axis=1, keepdims=True)
                    p = jnp.exp2((s - m) * SCALE).astype(BF16)
                    m_tmp[0, j * TILE : (j + 1) * TILE] = jnp.broadcast_to(m, (TILE, HD))
                    acc_tmp[0, j * TILE : (j + 1) * TILE] = dot_nn(p, v_buf[at])

            if first:
                for pieces in range(1, BLK // TILE + 1):
                    pl.when(lax.rem(tile, BLK // TILE) == pieces - 1)(
                        functools.partial(own_part, pieces)
                    )

            found = jnp.int32(0)
            where = [jnp.int32(0)] * most
            for e in range(TOPK):
                block = sel_ref[t * TOPK + e]
                start = 0
                for base, n in zip(bases, slots):
                    hit = (block != own) & (block >= base) & (block < base + n)
                    where = [
                        jnp.where(hit & (found == i), start + block - base, w)
                        for i, w in enumerate(where)
                    ]
                    found = found + hit.astype(jnp.int32)
                    start += n

            def others(n):
                at = [pl.ds(pl.multiple_of(w * BLK, BLK), BLK) for w in where[:n]]
                for j in range(PER):
                    here = slice(j * TILE, (j + 1) * TILE)
                    old = m_old[at_old, here]
                    acc = acc_old[at_old, here]
                    if n:
                        q = q_buf[part, q_rows, j * HD : (j + 1) * HD]
                        s = [dot_nt(q, k_buf[a]) for a in at]
                        s = jnp.concatenate(s, axis=1) if n > 1 else s[0]
                        m = jnp.maximum(old, jnp.max(s, axis=1, keepdims=True))
                        p = jnp.exp2((s - jnp.tile(m, (1, n * BLK // HD))) * SCALE).astype(BF16)
                        fade = jnp.exp2((old - m) * SCALE)
                        acc = acc * jnp.tile(fade, (1, 2))
                        for i, a in enumerate(at):
                            acc = acc + dot_nn(p[:, i * BLK : (i + 1) * BLK], v_buf[a])
                        old = m
                    if last:
                        finish(j, acc)
                    else:
                        keep(j, old, acc)

            for n in range(most + 1):
                pl.when(found == n)(functools.partial(others, n))

        if last:
            for part, (out_ref, k) in enumerate(zip(outs, partners)):

                def step(i, carry, out_ref=out_ref, k=k, part=part):
                    out_at = pl.ds(pl.multiple_of(i * TILE, TILE), TILE)
                    one_tile(k, part, i, out_ref, out_at)
                    return carry

                lax.fori_loop(0, tiles_in_part, step, 0)
        else:

            def step(t, carry):
                k = t // tiles_in_part
                one_tile(k, k, lax.rem(t, tiles_in_part), None, None)
                return carry

            lax.fori_loop(0, tiles, step, 0)

    if last:
        out_shape = tuple(jax.ShapeDtypeStruct((rows, QW), BF16) for _ in partners)
    else:
        out_shape = (
            jax.ShapeDtypeStruct((tiles, QW, HD), F32),
            jax.ShapeDtypeStruct((tiles, QW, 2 * HD), F32),
        )
    work = (tiles if not last else len(partners) * tiles_in_part) * QW * BLK * (1 + n_src) // 2
    return pl.pallas_call(
        kernel,
        in_specs=[SMEM] + [VMEM] * (n_q + n_src + len(state)),
        out_shape=out_shape,
        out_specs=(VMEM,) * n_out,
        scratch_shapes=[
            pltpu.VMEM((sum(slots) * BLK, HD), BF16),
            pltpu.VMEM((sum(slots) * BLK, 2 * HD), BF16),
            pltpu.VMEM((1, QW, HD), F32),
            pltpu.VMEM((1, QW, 2 * HD), F32),
            pltpu.VMEM((n_q, rows, QW), BF16),
        ],
        compiler_params=pltpu.CompilerParams(
            vmem_limit_bytes=(24 if sum(slots) <= 16 else 56) * MIB
        ),
        cost_estimate=pl.CostEstimate(
            flops=8 * work * HD, transcendentals=work, bytes_accessed=4 * MIB
        ),
        name=name,
    )(sel, *[queries[k] for k in partners], *sources, *state)


def body(levels, subs, heads, queries, keys, values, selected):
    rows = queries.shape[0]
    tiles_here = selected.shape[0]
    level_blocks = subs * rows // BLK
    by_levels = levels == 4 and subs * rows % BLK == 0

    def exchange(pieces):
        return tuple(
            lax.ppermute(piece, "sub", [(i, i ^ k) for i in range(subs)]) if k else piece
            for k, piece in enumerate(pieces)
        )

    packed = pack_keys_values(subs, heads, keys, values)
    if by_levels:
        raw = lax.ppermute(packed, "lev", [(1, 3), (0, 1)])
    own = lax.all_to_all(packed, ("sub", "head"), 0, 0, tiled=True)
    q = pack_queries(subs, queries, selected)
    q = exchange(q)
    sel = jnp.concatenate([piece[rows, : tiles_here * TOPK] for piece in q]).astype(jnp.int32)

    everyone = tuple(range(subs))
    if by_levels:
        own, raw = lax.optimization_barrier((own, raw))
        pa = lax.ppermute(own, "lev", [(0, 2), (2, 3)])
        p2 = lax.all_to_all(raw, ("sub", "head"), 0, 0, tiled=True)
        pf = lax.ppermute(pa, "lev", [(2, 3)])
        later, pa = lax.optimization_barrier((own, pa))
        po = lax.ppermute(later, "lev", [(1, 2)])

        def at(level, *which):
            base = jnp.int32(NONE)
            for here, holds in which:
                base = jnp.where(level == here, holds * level_blocks, base)
            return base

        def early(level):
            return (level * level_blocks, at(level, (2, 0), (3, 2)), at(level, (1, 0), (3, 1)))

        def late(level):
            return (at(level, (3, 0)), at(level, (2, 1)))

        state = attention(
            "early", True, False, everyone, early, q, sel, (own, pa, p2), ()
        )
        far, near = everyone[subs // 2 :], everyone[: subs // 2]
        out_far = attention("late_far", False, True, far, late, q, sel, (pf, po), state)
        out_near = attention("late_near", False, True, near, late, q, sel, (pf, po), state)
        out = out_near + out_far
    else:
        whole = lax.all_gather(own, "lev", axis=0, tiled=True)
        out = attention(
            "all", True, True, everyone, lambda level: (0,), q, sel, (whole,), ()
        )
    out = exchange(out)
    return unpack_output(subs, out) if subs > 1 else out[0]


def solution(mesh):
    ctx, heads = mesh.shape["ctx"], mesh.shape["head"]
    subs = math.gcd(KVH // heads, ctx)
    if subs * heads != KVH:
        raise ValueError("unsupported mesh")
    levels = ctx // subs
    split = Mesh(mesh.devices.reshape(levels, subs, heads), ("lev", "sub", "head"))
    placed = (
        P(("lev", "sub"), "head"),
        P(("lev", "sub", "head"), None),
        P(("lev", "sub", "head"), None),
        P(("lev", "sub"), "head", None),
    )
    return jax.shard_map(
        functools.partial(body, levels, subs, heads),
        mesh=split,
        in_specs=placed,
        out_specs=P(("lev", "sub"), "head"),
        check_vma=False,
    )
```

```python
import functools
import math

import jax
import jax.numpy as jnp
from jax import lax
from jax.experimental import pallas as pl
from jax.experimental.pallas import tpu as pltpu
from jax.sharding import Mesh, PartitionSpec as P

HD = 128
QH = 32
KVH = 8
BLK = 512
TILE = 128
TOPK = 3
PER = QH // KVH
QW = PER * HD
EXTRA = 16

FLOOR = -1e30
SCALE = HD ** -0.5 * math.log2(math.e)
NONE = -100000
F32 = jnp.float32
BF16 = jnp.bfloat16
VMEM = pl.BlockSpec(memory_space=pltpu.VMEM)
SMEM = pl.BlockSpec(memory_space=pltpu.SMEM)
MIB = 1024 * 1024


def dot_nt(a, b):
    return lax.dot_general(a, b, (((1,), (1,)), ((), ())), preferred_element_type=F32)


def dot_nn(a, b):
    return lax.dot_general(a, b, (((1,), (0,)), ((), ())), preferred_element_type=F32)


def copy_cost(bytes_moved):
    return pl.CostEstimate(flops=0, transcendentals=0, bytes_accessed=bytes_moved)


def pack_keys_values(subs, heads, keys, values):
    r = keys.shape[0]

    def kernel(k_ref, v_ref, out_ref):
        for sub in range(subs):
            for head in range(heads):
                at = (head * subs + sub) * HD
                out_ref[sub * heads + head, 0] = k_ref[:, at : at + HD]
                out_ref[sub * heads + head, 1] = v_ref[:, at : at + HD]

    return pl.pallas_call(
        kernel,
        in_specs=[VMEM, VMEM],
        out_specs=VMEM,
        out_shape=jax.ShapeDtypeStruct((subs * heads, 2, r, HD), BF16),
        cost_estimate=copy_cost(4 * keys.size * 2),
        name="pack_kv",
    )(keys, values)


def pack_queries(subs, queries, selected):
    rows = queries.shape[0]
    tiles_here = selected.shape[0]

    def kernel(sel_ref, q_ref, *outs):
        sub = lax.axis_index("sub") if subs > 1 else 0
        lane = lax.broadcasted_iota(jnp.int32, (EXTRA, QW), 1)
        for k, out_ref in enumerate(outs):
            head = sub ^ k
            out_ref[:rows] = q_ref[:, pl.ds(pl.multiple_of(head * QW, QW), QW)]
            row = jnp.zeros((EXTRA, QW), jnp.int32)
            for t in range(tiles_here):
                for e in range(TOPK):
                    row = jnp.where(lane == t * TOPK + e, sel_ref[t, head, e], row)
            out_ref[rows:] = row.astype(F32).astype(BF16)

    return pl.pallas_call(
        kernel,
        in_specs=[SMEM, VMEM],
        out_specs=(VMEM,) * subs,
        out_shape=(jax.ShapeDtypeStruct((rows + EXTRA, QW), BF16),) * subs,
        cost_estimate=copy_cost(2 * queries.size * 2),
        compiler_params=pltpu.CompilerParams(vmem_limit_bytes=8 * MIB),
        name="pack_q",
    )(selected, queries)


def unpack_output(subs, pieces):
    rows = pieces[0].shape[0]

    def kernel(*refs):
        sub = lax.axis_index("sub")
        for k in range(subs):
            at = pl.multiple_of((sub ^ k) * QW, QW)
            refs[subs][:, pl.ds(at, QW)] = refs[k][...]

    return pl.pallas_call(
        kernel,
        in_specs=[VMEM] * subs,
        out_specs=VMEM,
        out_shape=jax.ShapeDtypeStruct((rows, subs * QW), BF16),
        cost_estimate=copy_cost(4 * subs * rows * QW),
        compiler_params=pltpu.CompilerParams(vmem_limit_bytes=8 * MIB),
        name="unpack",
    )(*pieces)


def attention(name, first, last, partners, bases_of, queries, sel, sources, state):
    parts, rows = len(queries), queries[0].shape[0] - EXTRA
    tiles_in_part = rows // TILE
    tiles = parts * tiles_in_part
    r = sources[0].shape[2]
    per_block = BLK // r
    n_src = len(sources)
    slots = [src.shape[0] // per_block for src in sources]
    most = min(TOPK, sum(slots))
    n_q = len(partners)
    n_out = len(partners) if last else 2

    def kernel(*refs):
        sel_ref, q_refs = refs[0], refs[1 : 1 + n_q]
        src = refs[1 + n_q : 1 + n_q + n_src]
        rest = refs[1 + n_q + n_src :]
        m_in, acc_in = (None, None) if first else rest[:2]
        rest = rest if first else rest[2:]
        outs, k_buf, v_buf, m_tmp, acc_tmp, q_buf = rest[:n_out], *rest[n_out:]
        level = lax.axis_index("lev")
        sub = lax.axis_index("sub") if parts > 1 else 0
        for i, q_ref in enumerate(q_refs):
            q_buf[i] = q_ref[:rows]
        bases = bases_of(level)

        v_buf[:, HD:] = jnp.ones((sum(slots) * BLK, HD), BF16)
        start = 0
        for ref, base, n in zip(src, bases, slots):

            def fill(ref=ref, start=start, n=n):
                if n * per_block <= 8:
                    k_buf[start * BLK : (start + n) * BLK] = ref[:, 0].reshape(n * BLK, HD)
                    v_buf[start * BLK : (start + n) * BLK, :HD] = ref[:, 1].reshape(n * BLK, HD)
                else:

                    def chunk(i, carry):
                        at = pl.ds(pl.multiple_of(start * BLK + i * r, r), r)
                        k_buf[at] = ref[i, 0]
                        v_buf[at, :HD] = ref[i, 1]
                        return carry

                    lax.fori_loop(0, n * per_block, chunk, 0)

            if isinstance(base, int):
                fill()
            else:
                pl.when(base >= 0)(fill)
            start += n

        def one_tile(k, part, i, out_ref, out_at):
            t = k * tiles_in_part + i
            tile = level * tiles + (sub ^ k) * tiles_in_part + i
            own = tile * TILE // BLK
            q_rows = pl.ds(pl.multiple_of(i * TILE, TILE), TILE)
            m_old, acc_old, at_old = (m_tmp, acc_tmp, 0) if first else (m_in, acc_in, t)

            def finish(j, acc):
                out_ref[out_at, j * HD : (j + 1) * HD] = (acc[:, :HD] / acc[:, HD:]).astype(BF16)

            def keep(j, m, acc):
                outs[0][t, j * TILE : (j + 1) * TILE] = m
                outs[1][t, j * TILE : (j + 1) * TILE] = acc

            def own_part(pieces):
                count = pieces * TILE
                at = pl.ds(pl.multiple_of((own - bases[0]) * BLK, BLK), count)
                key_at = lax.broadcasted_iota(jnp.int32, (TILE, TILE), 1)
                query_at = lax.broadcasted_iota(jnp.int32, (TILE, TILE), 0)
                for j in range(PER):
                    s = dot_nt(q_buf[part, q_rows, j * HD : (j + 1) * HD], k_buf[at])
                    edge = jnp.where(key_at <= query_at, s[:, count - TILE :], FLOOR)
                    s = jnp.concatenate([s[:, : count - TILE], edge], axis=1) if pieces > 1 else edge
                    m = jnp.max(s, axis=1, keepdims=True)
                    p = jnp.exp2((s - m) * SCALE).astype(BF16)
                    m_tmp[0, j * TILE : (j + 1) * TILE] = jnp.broadcast_to(m, (TILE, HD))
                    acc_tmp[0, j * TILE : (j + 1) * TILE] = dot_nn(p, v_buf[at])

            if first:
                for pieces in range(1, BLK // TILE + 1):
                    pl.when(lax.rem(tile, BLK // TILE) == pieces - 1)(
                        functools.partial(own_part, pieces)
                    )

            found = jnp.int32(0)
            where = [jnp.int32(0)] * most
            for e in range(TOPK):
                block = sel_ref[t * TOPK + e]
                start = 0
                for base, n in zip(bases, slots):
                    hit = (block != own) & (block >= base) & (block < base + n)
                    where = [
                        jnp.where(hit & (found == i), start + block - base, w)
                        for i, w in enumerate(where)
                    ]
                    found = found + hit.astype(jnp.int32)
                    start += n

            def others(n):
                at = [pl.ds(pl.multiple_of(w * BLK, BLK), BLK) for w in where[:n]]
                for j in range(PER):
                    here = slice(j * TILE, (j + 1) * TILE)
                    old = m_old[at_old, here]
                    acc = acc_old[at_old, here]
                    if n:
                        q = q_buf[part, q_rows, j * HD : (j + 1) * HD]
                        s = [dot_nt(q, k_buf[a]) for a in at]
                        s = jnp.concatenate(s, axis=1) if n > 1 else s[0]
                        m = jnp.maximum(old, jnp.max(s, axis=1, keepdims=True))
                        p = jnp.exp2((s - jnp.tile(m, (1, n * BLK // HD))) * SCALE).astype(BF16)
                        fade = jnp.exp2((old - m) * SCALE)
                        acc = acc * jnp.tile(fade, (1, 2))
                        for i, a in enumerate(at):
                            acc = acc + dot_nn(p[:, i * BLK : (i + 1) * BLK], v_buf[a])
                        old = m
                    if last:
                        finish(j, acc)
                    else:
                        keep(j, old, acc)

            for n in range(most + 1):
                pl.when(found == n)(functools.partial(others, n))

        if last:
            for part, (out_ref, k) in enumerate(zip(outs, partners)):

                def step(i, carry, out_ref=out_ref, k=k, part=part):
                    out_at = pl.ds(pl.multiple_of(i * TILE, TILE), TILE)
                    one_tile(k, part, i, out_ref, out_at)
                    return carry

                lax.fori_loop(0, tiles_in_part, step, 0)
        else:

            def step(t, carry):
                k = t // tiles_in_part
                one_tile(k, k, lax.rem(t, tiles_in_part), None, None)
                return carry

            lax.fori_loop(0, tiles, step, 0)

    if last:
        out_shape = tuple(jax.ShapeDtypeStruct((rows, QW), BF16) for _ in partners)
    else:
        out_shape = (
            jax.ShapeDtypeStruct((tiles, QW, HD), F32),
            jax.ShapeDtypeStruct((tiles, QW, 2 * HD), F32),
        )
    work = (tiles if not last else len(partners) * tiles_in_part) * QW * BLK * (1 + n_src) // 2
    return pl.pallas_call(
        kernel,
        in_specs=[SMEM] + [VMEM] * (n_q + n_src + len(state)),
        out_shape=out_shape,
        out_specs=(VMEM,) * n_out,
        scratch_shapes=[
            pltpu.VMEM((sum(slots) * BLK, HD), BF16),
            pltpu.VMEM((sum(slots) * BLK, 2 * HD), BF16),
            pltpu.VMEM((1, QW, HD), F32),
            pltpu.VMEM((1, QW, 2 * HD), F32),
            pltpu.VMEM((n_q, rows, QW), BF16),
        ],
        compiler_params=pltpu.CompilerParams(
            vmem_limit_bytes=(24 if sum(slots) <= 16 else 56) * MIB
        ),
        cost_estimate=pl.CostEstimate(
            flops=8 * work * HD, transcendentals=work, bytes_accessed=4 * MIB
        ),
        name=name,
    )(sel, *[queries[k] for k in partners], *sources, *state)


def body(levels, subs, heads, queries, keys, values, selected):
    rows = queries.shape[0]
    tiles_here = selected.shape[0]
    level_blocks = subs * rows // BLK
    by_levels = levels == 4 and subs * rows % BLK == 0

    def exchange(pieces):
        return tuple(
            lax.ppermute(piece, "sub", [(i, i ^ k) for i in range(subs)]) if k else piece
            for k, piece in enumerate(pieces)
        )

    packed = pack_keys_values(subs, heads, keys, values)
    if by_levels:
        raw = lax.ppermute(packed, "lev", [(1, 3), (0, 1)])
    own = lax.all_to_all(packed, ("sub", "head"), 0, 0, tiled=True)
    q = pack_queries(subs, queries, selected)
    q = exchange(q)
    sel = jnp.concatenate([piece[rows, : tiles_here * TOPK] for piece in q]).astype(jnp.int32)

    everyone = tuple(range(subs))
    if by_levels:
        own, raw = lax.optimization_barrier((own, raw))
        pa = lax.ppermute(own, "lev", [(0, 2), (2, 3)])
        p2 = lax.all_to_all(raw, ("sub", "head"), 0, 0, tiled=True)
        pf = lax.ppermute(pa, "lev", [(2, 3)])
        later, pa = lax.optimization_barrier((own, pa))
        po = lax.ppermute(later, "lev", [(1, 2)])

        def at(level, *which):
            base = jnp.int32(NONE)
            for here, holds in which:
                base = jnp.where(level == here, holds * level_blocks, base)
            return base

        def early(level):
            return (level * level_blocks, at(level, (2, 0), (3, 2)), at(level, (1, 0), (3, 1)))

        def late(level):
            return (at(level, (3, 0)), at(level, (2, 1)))

        state = attention(
            "early", True, False, everyone, early, q, sel, (own, pa, p2), ()
        )
        far, near = everyone[subs // 2 :], everyone[: subs // 2]
        out_far = attention("late_far", False, True, far, late, q, sel, (pf, po), state)
        out_near = attention("late_near", False, True, near, late, q, sel, (pf, po), state)
        out = out_near + out_far
    else:
        whole = lax.all_gather(own, "lev", axis=0, tiled=True)
        out = attention(
            "all", True, True, everyone, lambda level: (0,), q, sel, (whole,), ()
        )
    out = exchange(out)
    return unpack_output(subs, out) if subs > 1 else out[0]


def solution(mesh):
    ctx, heads = mesh.shape["ctx"], mesh.shape["head"]
    subs = math.gcd(KVH // heads, ctx)
    if subs * heads != KVH:
        raise ValueError("unsupported mesh")
    levels = ctx // subs
    split = Mesh(mesh.devices.reshape(levels, subs, heads), ("lev", "sub", "head"))
    placed = (
        P(("lev", "sub"), "head"),
        P(("lev", "sub", "head"), None),
        P(("lev", "sub", "head"), None),
        P(("lev", "sub"), "head", None),
    )
    return jax.shard_map(
        functools.partial(body, levels, subs, heads),
        mesh=split,
        in_specs=placed,
        out_specs=P(("lev", "sub"), "head"),
        check_vma=False,
    )
```

```python
import functools
import math

import jax
import jax.numpy as jnp
from jax import lax
from jax.experimental import pallas as pl
from jax.experimental.pallas import tpu as pltpu
from jax.sharding import Mesh, PartitionSpec as P

HD = 128
QH = 32
KVH = 8
BLK = 512
TILE = 128
TOPK = 3
PER = QH // KVH
QW = PER * HD
EXTRA = 16

FLOOR = -1e30
SCALE = HD ** -0.5 * math.log2(math.e)
NONE = -100000
F32 = jnp.float32
BF16 = jnp.bfloat16
VMEM = pl.BlockSpec(memory_space=pltpu.VMEM)
SMEM = pl.BlockSpec(memory_space=pltpu.SMEM)
ANY = pl.BlockSpec(memory_space=pl.ANY)
MIB = 1024 * 1024


def dot_nt(a, b):
    return lax.dot_general(a, b, (((1,), (1,)), ((), ())), preferred_element_type=F32)


def dot_nn(a, b):
    return lax.dot_general(a, b, (((1,), (0,)), ((), ())), preferred_element_type=F32)


def copy_cost(bytes_moved):
    return pl.CostEstimate(flops=0, transcendentals=0, bytes_accessed=bytes_moved)


def pack_keys_values(subs, heads, keys, values):
    r = keys.shape[0]

    def kernel(k_ref, v_ref, out_ref):
        for sub in range(subs):
            for head in range(heads):
                at = (head * subs + sub) * HD
                out_ref[sub * heads + head, 0] = k_ref[:, at : at + HD]
                out_ref[sub * heads + head, 1] = v_ref[:, at : at + HD]

    return pl.pallas_call(
        kernel,
        in_specs=[VMEM, VMEM],
        out_specs=VMEM,
        out_shape=jax.ShapeDtypeStruct((subs * heads, 2, r, HD), BF16),
        cost_estimate=copy_cost(4 * keys.size * 2),
        name="pack_kv",
    )(keys, values)


def pack_queries(subs, queries, selected):
    rows = queries.shape[0]
    tiles_here = selected.shape[0]

    def kernel(sel_ref, q_ref, *outs):
        sub = lax.axis_index("sub") if subs > 1 else 0
        lane = lax.broadcasted_iota(jnp.int32, (EXTRA, QW), 1)
        for k, out_ref in enumerate(outs):
            head = sub ^ k
            out_ref[:rows] = q_ref[:, pl.ds(pl.multiple_of(head * QW, QW), QW)]
            row = jnp.zeros((EXTRA, QW), jnp.int32)
            for t in range(tiles_here):
                for e in range(TOPK):
                    row = jnp.where(lane == t * TOPK + e, sel_ref[t, head, e], row)
            out_ref[rows:] = row.astype(F32).astype(BF16)

    return pl.pallas_call(
        kernel,
        in_specs=[SMEM, VMEM],
        out_specs=(VMEM,) * subs,
        out_shape=(jax.ShapeDtypeStruct((rows + EXTRA, QW), BF16),) * subs,
        cost_estimate=copy_cost(2 * queries.size * 2),
        compiler_params=pltpu.CompilerParams(vmem_limit_bytes=8 * MIB),
        name="pack_q",
    )(selected, queries)


def unpack_output(name, subs, pieces, ks, begun):
    rows = pieces[0].shape[0]
    n = len(pieces)

    def kernel(*refs):
        out_ref, sems = refs[-2:]
        sub = lax.axis_index("sub")
        copies = []
        for i, k in enumerate(ks):
            at = pl.ds(pl.multiple_of((sub ^ k) * QW, QW), QW)
            copies.append(pltpu.make_async_copy(refs[i], out_ref.at[:, at], sems.at[i]))
        for copy in copies:
            copy.start()
        for copy in copies:
            copy.wait()

    return pl.pallas_call(
        kernel,
        in_specs=[VMEM] * n + [ANY] * len(begun),
        out_specs=ANY,
        out_shape=jax.ShapeDtypeStruct((rows, subs * QW), BF16),
        scratch_shapes=[pltpu.SemaphoreType.DMA((n,))],
        input_output_aliases={n: 0} if begun else {},
        cost_estimate=copy_cost(4 * n * rows * QW),
        compiler_params=pltpu.CompilerParams(vmem_limit_bytes=8 * MIB),
        name=name,
    )(*pieces, *begun)


def attention(name, first, last, partners, bases_of, queries, sel, sources, state):
    parts, rows = len(queries), queries[0].shape[0] - EXTRA
    tiles_in_part = rows // TILE
    tiles_here = len(partners) * tiles_in_part
    r = sources[0].shape[2]
    per_block = BLK // r
    n_src = len(sources)
    slots = [src.shape[0] // per_block for src in sources]
    most = min(TOPK, sum(slots))
    n_q = len(partners)
    n_out = len(partners) if last else 2

    def kernel(*refs):
        sel_ref, q_refs = refs[0], refs[1 : 1 + n_q]
        src = refs[1 + n_q : 1 + n_q + n_src]
        rest = refs[1 + n_q + n_src :]
        m_in, acc_in = (None, None) if first else rest[:2]
        rest = rest if first else rest[2:]
        outs, k_buf, v_buf, m_tmp, acc_tmp, q_buf = rest[:n_out], *rest[n_out:]
        level = lax.axis_index("lev")
        sub = lax.axis_index("sub") if parts > 1 else 0
        for i, q_ref in enumerate(q_refs):
            q_buf[i] = q_ref[:rows]
        bases = bases_of(level)

        v_buf[:, HD:] = jnp.ones((sum(slots) * BLK, HD), BF16)
        start = 0
        for ref, base, n in zip(src, bases, slots):

            def fill(ref=ref, start=start, n=n):
                if n * per_block <= 8:
                    k_buf[start * BLK : (start + n) * BLK] = ref[:, 0].reshape(n * BLK, HD)
                    v_buf[start * BLK : (start + n) * BLK, :HD] = ref[:, 1].reshape(n * BLK, HD)
                else:

                    def chunk(i, carry):
                        at = pl.ds(pl.multiple_of(start * BLK + i * r, r), r)
                        k_buf[at] = ref[i, 0]
                        v_buf[at, :HD] = ref[i, 1]
                        return carry

                    lax.fori_loop(0, n * per_block, chunk, 0)

            if isinstance(base, int):
                fill()
            else:
                pl.when(base >= 0)(fill)
            start += n

        def one_tile(k, part, i, out_ref, out_at):
            t = part * tiles_in_part + i
            tile = (level * parts + (sub ^ k)) * tiles_in_part + i
            own = tile * TILE // BLK
            q_rows = pl.ds(pl.multiple_of(i * TILE, TILE), TILE)
            m_old, acc_old, at_old = (m_tmp, acc_tmp, 0) if first else (m_in, acc_in, t)

            def finish(j, acc):
                out_ref[out_at, j * HD : (j + 1) * HD] = (acc[:, :HD] / acc[:, HD:]).astype(BF16)

            def keep(j, m, acc):
                outs[0][t, j * TILE : (j + 1) * TILE] = m
                outs[1][t, j * TILE : (j + 1) * TILE] = acc

            def own_part(pieces):
                count = pieces * TILE
                at = pl.ds(pl.multiple_of((own - bases[0]) * BLK, BLK), count)
                key_at = lax.broadcasted_iota(jnp.int32, (TILE, TILE), 1)
                query_at = lax.broadcasted_iota(jnp.int32, (TILE, TILE), 0)
                for j in range(PER):
                    s = dot_nt(q_buf[part, q_rows, j * HD : (j + 1) * HD], k_buf[at])
                    edge = jnp.where(key_at <= query_at, s[:, count - TILE :], FLOOR)
                    s = jnp.concatenate([s[:, : count - TILE], edge], axis=1) if pieces > 1 else edge
                    m = jnp.max(s, axis=1, keepdims=True)
                    p = jnp.exp2((s - m) * SCALE).astype(BF16)
                    m_tmp[0, j * TILE : (j + 1) * TILE] = jnp.broadcast_to(m, (TILE, HD))
                    acc_tmp[0, j * TILE : (j + 1) * TILE] = dot_nn(p, v_buf[at])

            if first:
                for pieces in range(1, BLK // TILE + 1):
                    pl.when(lax.rem(tile, BLK // TILE) == pieces - 1)(
                        functools.partial(own_part, pieces)
                    )

            found = jnp.int32(0)
            where = [jnp.int32(0)] * most
            for e in range(TOPK):
                block = sel_ref[(k * tiles_in_part + i) * TOPK + e]
                start = 0
                for base, n in zip(bases, slots):
                    hit = (block != own) & (block >= base) & (block < base + n)
                    where = [
                        jnp.where(hit & (found == i), start + block - base, w)
                        for i, w in enumerate(where)
                    ]
                    found = found + hit.astype(jnp.int32)
                    start += n

            def others(n):
                at = [pl.ds(pl.multiple_of(w * BLK, BLK), BLK) for w in where[:n]]
                for j in range(PER):
                    here = slice(j * TILE, (j + 1) * TILE)
                    old = m_old[at_old, here]
                    acc = acc_old[at_old, here]
                    if n:
                        q = q_buf[part, q_rows, j * HD : (j + 1) * HD]
                        s = [dot_nt(q, k_buf[a]) for a in at]
                        s = jnp.concatenate(s, axis=1) if n > 1 else s[0]
                        m = jnp.maximum(old, jnp.max(s, axis=1, keepdims=True))
                        p = jnp.exp2((s - jnp.tile(m, (1, n * BLK // HD))) * SCALE).astype(BF16)
                        fade = jnp.exp2((old - m) * SCALE)
                        acc = acc * jnp.tile(fade, (1, 2))
                        for i, a in enumerate(at):
                            acc = acc + dot_nn(p[:, i * BLK : (i + 1) * BLK], v_buf[a])
                        old = m
                    if last:
                        finish(j, acc)
                    else:
                        keep(j, old, acc)

            for n in range(most + 1):
                pl.when(found == n)(functools.partial(others, n))

        if last:
            for part, (out_ref, k) in enumerate(zip(outs, partners)):

                def step(i, carry, out_ref=out_ref, k=k, part=part):
                    out_at = pl.ds(pl.multiple_of(i * TILE, TILE), TILE)
                    one_tile(k, part, i, out_ref, out_at)
                    return carry

                lax.fori_loop(0, tiles_in_part, step, 0)
        else:

            def step(t, carry):
                part = t // tiles_in_part
                one_tile(partners[0] + part, part, lax.rem(t, tiles_in_part), None, None)
                return carry

            lax.fori_loop(0, tiles_here, step, 0)

    if last:
        out_shape = tuple(jax.ShapeDtypeStruct((rows, QW), BF16) for _ in partners)
    else:
        out_shape = (
            jax.ShapeDtypeStruct((tiles_here, QW, HD), F32),
            jax.ShapeDtypeStruct((tiles_here, QW, 2 * HD), F32),
        )
    work = tiles_here * QW * BLK * 3 // 2
    return pl.pallas_call(
        kernel,
        in_specs=[SMEM] + [VMEM] * (n_q + n_src + len(state)),
        out_shape=out_shape,
        out_specs=(VMEM,) * n_out,
        scratch_shapes=[
            pltpu.VMEM((sum(slots) * BLK, HD), BF16),
            pltpu.VMEM((sum(slots) * BLK, 2 * HD), BF16),
            pltpu.VMEM((1, QW, HD), F32),
            pltpu.VMEM((1, QW, 2 * HD), F32),
            pltpu.VMEM((n_q, rows, QW), BF16),
        ],
        compiler_params=pltpu.CompilerParams(
            vmem_limit_bytes=(24 if sum(slots) <= 16 else 56) * MIB
        ),
        cost_estimate=pl.CostEstimate(
            flops=8 * work * HD, transcendentals=work, bytes_accessed=4 * MIB
        ),
        name=name,
    )(sel, *[queries[k] for k in partners], *sources, *state)


def body(levels, subs, heads, queries, keys, values, selected):
    rows = queries.shape[0]
    tiles_here = selected.shape[0]
    level_blocks = subs * rows // BLK
    by_levels = levels == 4 and subs * rows % BLK == 0

    def exchange(pieces, ks):
        return tuple(
            lax.ppermute(piece, "sub", [(i, i ^ k) for i in range(subs)]) if k else piece
            for k, piece in zip(ks, pieces)
        )

    everyone = tuple(range(subs))
    packed = pack_keys_values(subs, heads, keys, values)
    if by_levels:
        raw = lax.ppermute(packed, "lev", [(1, 3), (0, 1)])
    own = lax.all_to_all(packed, ("sub", "head"), 0, 0, tiled=True)
    q = pack_queries(subs, queries, selected)
    q = exchange(q, everyone)
    sel = jnp.concatenate([piece[rows, : tiles_here * TOPK] for piece in q]).astype(jnp.int32)

    if by_levels:
        own, raw, first_piece = lax.optimization_barrier((own, raw, q[1]))
        q = (q[0], first_piece, *q[2:])
        pa = lax.ppermute(own, "lev", [(0, 2), (2, 3)])
        p2 = lax.all_to_all(raw, ("sub", "head"), 0, 0, tiled=True)
        pf = lax.ppermute(pa, "lev", [(2, 3)])
        later, pa = lax.optimization_barrier((own, pa))
        po = lax.ppermute(later, "lev", [(1, 2)])

        def at(level, *which):
            base = jnp.int32(NONE)
            for here, holds in which:
                base = jnp.where(level == here, holds * level_blocks, base)
            return base

        def early(level):
            return (level * level_blocks, at(level, (2, 0), (3, 2)), at(level, (1, 0), (3, 1)))

        def late(level):
            return (at(level, (3, 0)), at(level, (2, 1)))

        def whole_range(level):
            return early(level) + late(level)

        far, near = everyone[subs // 2 :], everyone[: subs // 2]
        state = attention(
            "far_early", True, False, far, early, q, sel, (own, pa, p2), ()
        )
        out_far = attention("far_late", False, True, far, late, q, sel, (pf, po), state)
        q_near, _ = lax.optimization_barrier((q[: subs // 2], out_far))
        q = tuple(q_near) + q[subs // 2 :]
        out_near = attention(
            "near", True, True, near, whole_range, q, sel, (own, pa, p2, pf, po), ()
        )
        begun = unpack_output("unpack_far", subs, exchange(out_far, far), far, ())
        return unpack_output("unpack_near", subs, exchange(out_near, near), near, (begun,))
    whole = lax.all_gather(own, "lev", axis=0, tiled=True)
    out = attention("all", True, True, everyone, lambda level: (0,), q, sel, (whole,), ())
    if subs == 1:
        return out[0]
    return unpack_output("unpack", subs, exchange(out, everyone), everyone, ())


def solution(mesh):
    ctx, heads = mesh.shape["ctx"], mesh.shape["head"]
    subs = math.gcd(KVH // heads, ctx)
    if subs * heads != KVH:
        raise ValueError("unsupported mesh")
    levels = ctx // subs
    split = Mesh(mesh.devices.reshape(levels, subs, heads), ("lev", "sub", "head"))
    placed = (
        P(("lev", "sub"), "head"),
        P(("lev", "sub", "head"), None),
        P(("lev", "sub", "head"), None),
        P(("lev", "sub"), "head", None),
    )
    return jax.shard_map(
        functools.partial(body, levels, subs, heads),
        mesh=split,
        in_specs=placed,
        out_specs=P(("lev", "sub"), "head"),
        check_vma=False,
    )
```

```python
import functools
import math

import jax
import jax.numpy as jnp
from jax import lax
from jax.experimental import pallas as pl
from jax.experimental.pallas import tpu as pltpu
from jax.sharding import Mesh, PartitionSpec as P

HD = 128
QH = 32
KVH = 8
BLK = 512
TILE = 128
TOPK = 3
PER = QH // KVH
QW = PER * HD
EXTRA = 16

FLOOR = -1e30
SCALE = HD ** -0.5 * math.log2(math.e)
NONE = -100000
F32 = jnp.float32
BF16 = jnp.bfloat16
VMEM = pl.BlockSpec(memory_space=pltpu.VMEM)
SMEM = pl.BlockSpec(memory_space=pltpu.SMEM)
ANY = pl.BlockSpec(memory_space=pl.ANY)
MIB = 1024 * 1024


def dot_nt(a, b):
    return lax.dot_general(a, b, (((1,), (1,)), ((), ())), preferred_element_type=F32)


def dot_nn(a, b):
    return lax.dot_general(a, b, (((1,), (0,)), ((), ())), preferred_element_type=F32)


def copy_cost(bytes_moved):
    return pl.CostEstimate(flops=0, transcendentals=0, bytes_accessed=bytes_moved)


def pack_keys_values(subs, heads, keys, values):
    r = keys.shape[0]

    def kernel(k_ref, v_ref, out_ref):
        for sub in range(subs):
            for head in range(heads):
                at = (head * subs + sub) * HD
                out_ref[sub * heads + head, 0] = k_ref[:, at : at + HD]
                out_ref[sub * heads + head, 1] = v_ref[:, at : at + HD]

    return pl.pallas_call(
        kernel,
        in_specs=[VMEM, VMEM],
        out_specs=VMEM,
        out_shape=jax.ShapeDtypeStruct((subs * heads, 2, r, HD), BF16),
        cost_estimate=copy_cost(4 * keys.size * 2),
        name="pack_kv",
    )(keys, values)


def pack_queries(subs, queries, selected):
    rows = queries.shape[0]
    tiles_here = selected.shape[0]

    def kernel(sel_ref, q_ref, *outs):
        sub = lax.axis_index("sub") if subs > 1 else 0
        lane = lax.broadcasted_iota(jnp.int32, (EXTRA, QW), 1)
        for k, out_ref in enumerate(outs):
            head = sub ^ k
            out_ref[:rows] = q_ref[:, pl.ds(pl.multiple_of(head * QW, QW), QW)]
            row = jnp.zeros((EXTRA, QW), jnp.int32)
            for t in range(tiles_here):
                for e in range(TOPK):
                    row = jnp.where(lane == t * TOPK + e, sel_ref[t, head, e], row)
            out_ref[rows:] = row.astype(F32).astype(BF16)

    return pl.pallas_call(
        kernel,
        in_specs=[SMEM, VMEM],
        out_specs=(VMEM,) * subs,
        out_shape=(jax.ShapeDtypeStruct((rows + EXTRA, QW), BF16),) * subs,
        cost_estimate=copy_cost(2 * queries.size * 2),
        compiler_params=pltpu.CompilerParams(vmem_limit_bytes=8 * MIB),
        name="pack_q",
    )(selected, queries)


def unpack_output(name, subs, pieces, ks, begun):
    rows = pieces[0].shape[0]
    n = len(pieces)

    def kernel(*refs):
        out_ref, sems = refs[-2:]
        sub = lax.axis_index("sub")
        copies = []
        for i, k in enumerate(ks):
            at = pl.ds(pl.multiple_of((sub ^ k) * QW, QW), QW)
            copies.append(pltpu.make_async_copy(refs[i], out_ref.at[:, at], sems.at[i]))
        for copy in copies:
            copy.start()
        for copy in copies:
            copy.wait()

    return pl.pallas_call(
        kernel,
        in_specs=[VMEM] * n + [ANY] * len(begun),
        out_specs=ANY,
        out_shape=jax.ShapeDtypeStruct((rows, subs * QW), BF16),
        scratch_shapes=[pltpu.SemaphoreType.DMA((n,))],
        input_output_aliases={n: 0} if begun else {},
        cost_estimate=copy_cost(4 * n * rows * QW),
        compiler_params=pltpu.CompilerParams(vmem_limit_bytes=8 * MIB),
        name=name,
    )(*pieces, *begun)


def attention(name, first, last, partners, bases_of, queries, sel, sources, state):
    parts, rows = len(queries), queries[0].shape[0] - EXTRA
    tiles_in_part = rows // TILE
    tiles_here = len(partners) * tiles_in_part
    r = sources[0].shape[2]
    per_block = BLK // r
    n_src = len(sources)
    slots = [src.shape[0] // per_block for src in sources]
    most = min(TOPK, sum(slots))
    n_q = len(partners)
    n_out = len(partners) if last else 2

    def kernel(*refs):
        sel_ref, q_refs = refs[0], refs[1 : 1 + n_q]
        src = refs[1 + n_q : 1 + n_q + n_src]
        rest = refs[1 + n_q + n_src :]
        m_in, acc_in = (None, None) if first else rest[:2]
        rest = rest if first else rest[2:]
        outs, k_buf, v_buf, m_tmp, acc_tmp, q_buf = rest[:n_out], *rest[n_out:]
        level = lax.axis_index("lev")
        sub = lax.axis_index("sub") if parts > 1 else 0
        for i, q_ref in enumerate(q_refs):
            q_buf[i] = q_ref[:rows]
        bases = bases_of(level)

        v_buf[:, HD:] = jnp.ones((sum(slots) * BLK, HD), BF16)
        start = 0
        for ref, base, n in zip(src, bases, slots):

            def fill(ref=ref, start=start, n=n):
                if n * per_block <= 8:
                    k_buf[start * BLK : (start + n) * BLK] = ref[:, 0].reshape(n * BLK, HD)
                    v_buf[start * BLK : (start + n) * BLK, :HD] = ref[:, 1].reshape(n * BLK, HD)
                else:

                    def chunk(i, carry):
                        at = pl.ds(pl.multiple_of(start * BLK + i * r, r), r)
                        k_buf[at] = ref[i, 0]
                        v_buf[at, :HD] = ref[i, 1]
                        return carry

                    lax.fori_loop(0, n * per_block, chunk, 0)

            if isinstance(base, int):
                fill()
            else:
                pl.when(base >= 0)(fill)
            start += n

        def one_tile(k, part, i, out_ref, out_at):
            t = part * tiles_in_part + i
            tile = (level * parts + (sub ^ k)) * tiles_in_part + i
            own = tile * TILE // BLK
            q_rows = pl.ds(pl.multiple_of(i * TILE, TILE), TILE)
            m_old, acc_old, at_old = (m_tmp, acc_tmp, 0) if first else (m_in, acc_in, t)

            def finish(j, acc):
                out_ref[out_at, j * HD : (j + 1) * HD] = (acc[:, :HD] / acc[:, HD:]).astype(BF16)

            def keep(j, m, acc):
                outs[0][t, j * TILE : (j + 1) * TILE] = m
                outs[1][t, j * TILE : (j + 1) * TILE] = acc

            def own_part(pieces):
                count = pieces * TILE
                at = pl.ds(pl.multiple_of((own - bases[0]) * BLK, BLK), count)
                key_at = lax.broadcasted_iota(jnp.int32, (TILE, TILE), 1)
                query_at = lax.broadcasted_iota(jnp.int32, (TILE, TILE), 0)
                for j in range(PER):
                    s = dot_nt(q_buf[part, q_rows, j * HD : (j + 1) * HD], k_buf[at])
                    edge = jnp.where(key_at <= query_at, s[:, count - TILE :], FLOOR)
                    s = jnp.concatenate([s[:, : count - TILE], edge], axis=1) if pieces > 1 else edge
                    m = jnp.max(s, axis=1, keepdims=True)
                    p = jnp.exp2((s - m) * SCALE).astype(BF16)
                    m_tmp[0, j * TILE : (j + 1) * TILE] = jnp.broadcast_to(m, (TILE, HD))
                    acc_tmp[0, j * TILE : (j + 1) * TILE] = dot_nn(p, v_buf[at])

            if first:
                for pieces in range(1, BLK // TILE + 1):
                    pl.when(lax.rem(tile, BLK // TILE) == pieces - 1)(
                        functools.partial(own_part, pieces)
                    )

            found = jnp.int32(0)
            where = [jnp.int32(0)] * most
            for e in range(TOPK):
                block = sel_ref[(k * tiles_in_part + i) * TOPK + e]
                start = 0
                for base, n in zip(bases, slots):
                    hit = (block != own) & (block >= base) & (block < base + n)
                    where = [
                        jnp.where(hit & (found == i), start + block - base, w)
                        for i, w in enumerate(where)
                    ]
                    found = found + hit.astype(jnp.int32)
                    start += n

            def others(n):
                at = [pl.ds(pl.multiple_of(w * BLK, BLK), BLK) for w in where[:n]]
                for j in range(PER):
                    here = slice(j * TILE, (j + 1) * TILE)
                    old = m_old[at_old, here]
                    acc = acc_old[at_old, here]
                    if n:
                        q = q_buf[part, q_rows, j * HD : (j + 1) * HD]
                        s = [dot_nt(q, k_buf[a]) for a in at]
                        s = jnp.concatenate(s, axis=1) if n > 1 else s[0]
                        m = jnp.maximum(old, jnp.max(s, axis=1, keepdims=True))
                        p = jnp.exp2((s - jnp.tile(m, (1, n * BLK // HD))) * SCALE).astype(BF16)
                        fade = jnp.exp2((old - m) * SCALE)
                        acc = acc * jnp.tile(fade, (1, 2))
                        for i, a in enumerate(at):
                            acc = acc + dot_nn(p[:, i * BLK : (i + 1) * BLK], v_buf[a])
                        old = m
                    if last:
                        finish(j, acc)
                    else:
                        keep(j, old, acc)

            for n in range(most + 1):
                pl.when(found == n)(functools.partial(others, n))

        if last:
            for part, (out_ref, k) in enumerate(zip(outs, partners)):

                def step(i, carry, out_ref=out_ref, k=k, part=part):
                    out_at = pl.ds(pl.multiple_of(i * TILE, TILE), TILE)
                    one_tile(k, part, i, out_ref, out_at)
                    return carry

                lax.fori_loop(0, tiles_in_part, step, 0)
        else:

            def step(t, carry):
                part = t // tiles_in_part
                one_tile(partners[0] + part, part, lax.rem(t, tiles_in_part), None, None)
                return carry

            lax.fori_loop(0, tiles_here, step, 0)

    if last:
        out_shape = tuple(jax.ShapeDtypeStruct((rows, QW), BF16) for _ in partners)
    else:
        out_shape = (
            jax.ShapeDtypeStruct((tiles_here, QW, HD), F32),
            jax.ShapeDtypeStruct((tiles_here, QW, 2 * HD), F32),
        )
    work = tiles_here * QW * BLK * 3 // 2
    return pl.pallas_call(
        kernel,
        in_specs=[SMEM] + [VMEM] * (n_q + n_src + len(state)),
        out_shape=out_shape,
        out_specs=(VMEM,) * n_out,
        scratch_shapes=[
            pltpu.VMEM((sum(slots) * BLK, HD), BF16),
            pltpu.VMEM((sum(slots) * BLK, 2 * HD), BF16),
            pltpu.VMEM((1, QW, HD), F32),
            pltpu.VMEM((1, QW, 2 * HD), F32),
            pltpu.VMEM((n_q, rows, QW), BF16),
        ],
        compiler_params=pltpu.CompilerParams(
            vmem_limit_bytes=(24 if sum(slots) <= 16 else 56) * MIB
        ),
        cost_estimate=pl.CostEstimate(
            flops=8 * work * HD, transcendentals=work, bytes_accessed=4 * MIB
        ),
        name=name,
    )(sel, *[queries[k] for k in partners], *sources, *state)


def body(levels, subs, heads, queries, keys, values, selected):
    rows = queries.shape[0]
    tiles_here = selected.shape[0]
    level_blocks = subs * rows // BLK
    by_levels = levels == 4 and subs * rows % (2 * BLK) == 0

    def exchange(pieces, ks):
        return tuple(
            lax.ppermute(piece, "sub", [(i, i ^ k) for i in range(subs)]) if k else piece
            for k, piece in zip(ks, pieces)
        )

    everyone = tuple(range(subs))
    packed = pack_keys_values(subs, heads, keys, values)
    if by_levels:
        raw = lax.ppermute(packed, "lev", [(1, 3), (0, 1)])
    own = lax.all_to_all(packed, ("sub", "head"), 0, 0, tiled=True)
    q = pack_queries(subs, queries, selected)
    hop = subs // 2
    if hop > 1:
        over = exchange(q[hop:], [hop] * hop)
        q = exchange(q[:hop], range(hop)) + exchange(over, range(hop))
    else:
        q = exchange(q, everyone)
    if by_levels:
        own, raw = lax.optimization_barrier((own, raw))
        half = own.shape[0] // 2
        halves = lax.optimization_barrier((own[:half], own[half:]))
        up = [lax.ppermute(piece, "lev", [(0, 2), (2, 3)]) for piece in halves]
        p2 = lax.all_to_all(raw, ("sub", "head"), 0, 0, tiled=True)
        q, _ = lax.optimization_barrier((q, up))
        sel = jnp.concatenate([piece[rows, : tiles_here * TOPK] for piece in q]).astype(jnp.int32)
        forwards = lax.axis_index("lev") == 2
        last_up = [
            lax.ppermute(jnp.where(forwards, a, b), "lev", [(2, 3), (1, 2)])
            for a, b in zip(up, halves)
        ]

        def at(level, *which):
            base = jnp.int32(NONE)
            for here, holds in which:
                base = jnp.where(level == here, holds * level_blocks, base)
            return base

        def in_halves(base):
            return (base, base + level_blocks // 2)

        def early(level):
            return (
                level * level_blocks,
                *in_halves(at(level, (2, 0), (3, 2))),
                at(level, (1, 0), (3, 1)),
            )

        def late(level):
            return in_halves(at(level, (2, 1), (3, 0)))

        def whole_range(level):
            return early(level) + late(level)

        far, near = everyone[subs // 2 :], everyone[: subs // 2]
        state = attention(
            "far_early", True, False, far, early, q, sel, (own, *up, p2), ()
        )
        out_far = attention("far_late", False, True, far, late, q, sel, tuple(last_up), state)
        q_near, _ = lax.optimization_barrier((q[: subs // 2], out_far))
        q = tuple(q_near) + tuple(q[subs // 2 :])
        out_near = attention(
            "near", True, True, near, whole_range, q, sel, (own, *up, p2, *last_up), ()
        )
        begun = unpack_output("unpack_far", subs, exchange(out_far, far), far, ())
        return unpack_output("unpack_near", subs, exchange(out_near, near), near, (begun,))
    sel = jnp.concatenate([piece[rows, : tiles_here * TOPK] for piece in q]).astype(jnp.int32)
    whole = lax.all_gather(own, "lev", axis=0, tiled=True)
    out = attention("all", True, True, everyone, lambda level: (0,), q, sel, (whole,), ())
    if subs == 1:
        return out[0]
    return unpack_output("unpack", subs, exchange(out, everyone), everyone, ())


def solution(mesh):
    ctx, heads = mesh.shape["ctx"], mesh.shape["head"]
    subs = math.gcd(KVH // heads, ctx)
    if subs * heads != KVH:
        raise ValueError("unsupported mesh")
    levels = ctx // subs
    split = Mesh(mesh.devices.reshape(levels, subs, heads), ("lev", "sub", "head"))
    placed = (
        P(("lev", "sub"), "head"),
        P(("lev", "sub", "head"), None),
        P(("lev", "sub", "head"), None),
        P(("lev", "sub"), "head", None),
    )
    return jax.shard_map(
        functools.partial(body, levels, subs, heads),
        mesh=split,
        in_specs=placed,
        out_specs=P(("lev", "sub"), "head"),
        check_vma=False,
    )
```

```python
import functools
import math

import jax
import jax.numpy as jnp
from jax import lax
from jax.experimental import pallas as pl
from jax.experimental.pallas import tpu as pltpu
from jax.sharding import Mesh, PartitionSpec as P

HD = 128
QH = 32
KVH = 8
BLK = 512
TILE = 128
TOPK = 3
PER = QH // KVH
QW = PER * HD
EXTRA = 16

FLOOR = -1e30
SCALE = HD ** -0.5 * math.log2(math.e)
NONE = -100000
F32 = jnp.float32
BF16 = jnp.bfloat16
VMEM = pl.BlockSpec(memory_space=pltpu.VMEM)
SMEM = pl.BlockSpec(memory_space=pltpu.SMEM)
ANY = pl.BlockSpec(memory_space=pl.ANY)
MIB = 1024 * 1024


def dot_nt(a, b):
    return lax.dot_general(a, b, (((1,), (1,)), ((), ())), preferred_element_type=F32)


def dot_nn(a, b):
    return lax.dot_general(a, b, (((1,), (0,)), ((), ())), preferred_element_type=F32)


def copy_cost(bytes_moved):
    return pl.CostEstimate(flops=0, transcendentals=0, bytes_accessed=bytes_moved)


def pack_keys_values(subs, heads, keys, values):
    r = keys.shape[0]

    def kernel(k_ref, v_ref, out_ref):
        for sub in range(subs):
            for head in range(heads):
                at = (head * subs + sub) * HD
                out_ref[sub * heads + head, 0] = k_ref[:, at : at + HD]
                out_ref[sub * heads + head, 1] = v_ref[:, at : at + HD]

    return pl.pallas_call(
        kernel,
        in_specs=[VMEM, VMEM],
        out_specs=VMEM,
        out_shape=jax.ShapeDtypeStruct((subs * heads, 2, r, HD), BF16),
        cost_estimate=copy_cost(4 * keys.size * 2),
        name="pack_kv",
    )(keys, values)


def pack_queries(subs, queries, selected):
    rows = queries.shape[0]
    tiles_here = selected.shape[0]

    def kernel(sel_ref, q_ref, *outs):
        sub = lax.axis_index("sub") if subs > 1 else 0
        lane = lax.broadcasted_iota(jnp.int32, (EXTRA, QW), 1)
        for k, out_ref in enumerate(outs):
            head = sub ^ k
            out_ref[:rows] = q_ref[:, pl.ds(pl.multiple_of(head * QW, QW), QW)]
            row = jnp.zeros((EXTRA, QW), jnp.int32)
            for t in range(tiles_here):
                for e in range(TOPK):
                    row = jnp.where(lane == t * TOPK + e, sel_ref[t, head, e], row)
            out_ref[rows:] = row.astype(F32).astype(BF16)

    return pl.pallas_call(
        kernel,
        in_specs=[SMEM, VMEM],
        out_specs=(VMEM,) * subs,
        out_shape=(jax.ShapeDtypeStruct((rows + EXTRA, QW), BF16),) * subs,
        cost_estimate=copy_cost(2 * queries.size * 2),
        compiler_params=pltpu.CompilerParams(vmem_limit_bytes=8 * MIB),
        name="pack_q",
    )(selected, queries)


def unpack_output(name, subs, pieces, ks, begun):
    rows = pieces[0].shape[0]
    n = len(pieces)

    def kernel(*refs):
        out_ref, sems = refs[-2:]
        sub = lax.axis_index("sub")
        copies = []
        for i, k in enumerate(ks):
            at = pl.ds(pl.multiple_of((sub ^ k) * QW, QW), QW)
            copies.append(pltpu.make_async_copy(refs[i], out_ref.at[:, at], sems.at[i]))
        for copy in copies:
            copy.start()
        for copy in copies:
            copy.wait()

    return pl.pallas_call(
        kernel,
        in_specs=[VMEM] * n + [ANY] * len(begun),
        out_specs=ANY,
        out_shape=jax.ShapeDtypeStruct((rows, subs * QW), BF16),
        scratch_shapes=[pltpu.SemaphoreType.DMA((n,))],
        input_output_aliases={n: 0} if begun else {},
        cost_estimate=copy_cost(4 * n * rows * QW),
        compiler_params=pltpu.CompilerParams(vmem_limit_bytes=8 * MIB),
        name=name,
    )(*pieces, *begun)


def attention(name, first, last, partners, bases_of, queries, sel, sources, state):
    parts, rows = len(queries), queries[0].shape[0] - EXTRA
    tiles_in_part = rows // TILE
    tiles_here = len(partners) * tiles_in_part
    in_block = BLK // TILE
    r = sources[0].shape[2]
    per_block = BLK // r
    n_src = len(sources)
    slots = [src.shape[0] // per_block for src in sources]
    n_slots = sum(slots)
    n_q = len(partners)
    n_out = n_q if last else 2
    one_block = parts > 1 and len(partners) * rows == BLK

    def kernel(*refs):
        sel_ref, q_refs = refs[0], refs[1 : 1 + n_q]
        src = refs[1 + n_q : 1 + n_q + n_src]
        rest = refs[1 + n_q + n_src :]
        m_in, acc_in = (None, None) if first else rest[:2]
        rest = rest if first else rest[2:]
        outs, k_buf, v_buf, q_buf, item_tile, item_slot = rest[:n_out], *rest[n_out : n_out + 5]
        m_ref, acc_ref = rest[n_out + 5 :] if last else outs
        level = lax.axis_index("lev")
        sub = lax.axis_index("sub") if parts > 1 else 0
        for i, q_ref in enumerate(q_refs):
            q_buf[i] = q_ref[:rows]
        if not first:
            m_ref[:tiles_here] = m_in[:tiles_here]
            acc_ref[:tiles_here] = acc_in[:tiles_here]
        bases = bases_of(level)

        v_buf[:, HD:] = jnp.ones((n_slots * BLK, HD), BF16)
        start = 0
        for ref, base, n in zip(src, bases, slots):

            def fill(ref=ref, start=start, n=n):
                if n * per_block <= 8:
                    k_buf[start * BLK : (start + n) * BLK] = ref[:, 0].reshape(n * BLK, HD)
                    v_buf[start * BLK : (start + n) * BLK, :HD] = ref[:, 1].reshape(n * BLK, HD)
                else:

                    def chunk(i, carry):
                        at = pl.ds(pl.multiple_of(start * BLK + i * r, r), r)
                        k_buf[at] = ref[i, 0]
                        v_buf[at, :HD] = ref[i, 1]
                        return carry

                    lax.fori_loop(0, n * per_block, chunk, 0)

            if isinstance(base, int):
                fill()
            else:
                pl.when(base >= 0)(fill)
            start += n

        def tile_of(t):
            k = partners[0] + t // tiles_in_part
            return (level * parts + (sub ^ k)) * tiles_in_part + lax.rem(t, tiles_in_part)

        def q_of(t, j):
            at = pl.ds(pl.multiple_of(lax.rem(t, tiles_in_part) * TILE, TILE), TILE)
            return q_buf[t // tiles_in_part, at, j * HD : (j + 1) * HD]

        def heads_rows(j):
            return slice(j * TILE, (j + 1) * TILE)

        def slot_rows(slot, count=BLK):
            return pl.ds(pl.multiple_of(slot * BLK, BLK), count)

        def own_part(t, slot, pieces):
            count = pieces * TILE
            at = slot_rows(slot, count)
            key_at = lax.broadcasted_iota(jnp.int32, (TILE, TILE), 1)
            query_at = lax.broadcasted_iota(jnp.int32, (TILE, TILE), 0)
            for j in range(PER):
                s = dot_nt(q_of(t, j), k_buf[at])
                edge = jnp.where(key_at <= query_at, s[:, count - TILE :], FLOOR)
                s = jnp.concatenate([s[:, : count - TILE], edge], axis=1) if pieces > 1 else edge
                m = jnp.max(s, axis=1, keepdims=True)
                p = jnp.exp2((s - m) * SCALE).astype(BF16)
                m_ref[t, heads_rows(j)] = jnp.broadcast_to(m, (TILE, HD))
                acc_ref[t, heads_rows(j)] = dot_nn(p, v_buf[at])

        if first and one_block:
            own = tile_of(0) // in_block
            for i in range(in_block):
                part = own * (in_block // tiles_in_part) + i // tiles_in_part - level * parts
                t = ((part ^ sub) - partners[0]) * tiles_in_part + i % tiles_in_part
                own_part(t, own - bases[0], i + 1)
        elif first:

            def own_tile(t, carry):
                tile = tile_of(t)
                for pieces in range(1, in_block + 1):
                    pl.when(lax.rem(tile, in_block) == pieces - 1)(
                        functools.partial(own_part, t, tile // in_block - bases[0], pieces)
                    )
                return carry

            lax.fori_loop(0, tiles_here, own_tile, 0)

        picks = [
            [sel_ref[(partners[0] * tiles_in_part + t) * TOPK + e] for e in range(TOPK)]
            for t in range(tiles_here)
        ]
        owns = [tile_of(jnp.int32(t)) // in_block for t in range(tiles_here)]

        def list_slot(slot, block, carry):
            count, before = carry
            for t in range(tiles_here):
                hit = functools.reduce(jnp.logical_or, [pick == block for pick in picks[t]])
                hit = hit & (block != owns[t]) & (block >= 0)
                clash = hit & (before == t) & (lax.rem(count, 2) == 1)
                item_tile[count] = tiles_here
                item_slot[count] = slot
                put = jnp.where(clash, count + 1, count)
                item_tile[put] = t
                item_slot[put] = slot
                count = jnp.where(hit, put + 1, count)
                before = jnp.where(hit, t, before)
            return count, before

        carry = (jnp.int32(0), jnp.int32(-1))
        start = 0
        for base, n in zip(bases, slots):
            if n <= 2:
                for i in range(n):
                    carry = list_slot(start + i, base + i, carry)
            else:
                carry = lax.fori_loop(
                    0,
                    n,
                    lambda i, c, start=start, base=base: list_slot(start + i, base + i, c),
                    carry,
                )
            start += n
        count = carry[0]
        item_tile[count] = tiles_here
        item_slot[count] = 0

        def two_items(i, carry):
            pair = [(item_tile[2 * i + x], item_slot[2 * i + x]) for x in range(2)]
            olds = [[m_ref[t, heads_rows(j)] for j in range(PER)] for t, _ in pair]
            for j in range(PER):
                for (t, slot), old in zip(pair, olds):
                    at = slot_rows(slot)
                    s = dot_nt(q_of(jnp.minimum(t, tiles_here - 1), j), k_buf[at])
                    m = jnp.maximum(old[j], jnp.max(s, axis=1, keepdims=True))
                    p = jnp.exp2((s - jnp.tile(m, (1, BLK // HD))) * SCALE).astype(BF16)
                    fade = jnp.exp2((old[j] - m) * SCALE)
                    m_ref[t, heads_rows(j)] = m
                    acc_ref[t, heads_rows(j)] = acc_ref[t, heads_rows(j)] * jnp.tile(
                        fade, (1, 2)
                    ) + dot_nn(p, v_buf[at])
            return carry

        lax.fori_loop(0, (count + 1) // 2, two_items, 0)

        if last:
            for t in range(tiles_here):
                at = slice(t % tiles_in_part * TILE, (t % tiles_in_part + 1) * TILE)
                for j in range(PER):
                    acc = acc_ref[t, heads_rows(j)]
                    outs[t // tiles_in_part][at, j * HD : (j + 1) * HD] = (
                        acc[:, :HD] / acc[:, HD:]
                    ).astype(BF16)

    kept = [(tiles_here + 1, QW, HD), (tiles_here + 1, QW, 2 * HD)]
    if last:
        out_shape = tuple(jax.ShapeDtypeStruct((rows, QW), BF16) for _ in partners)
    else:
        out_shape = tuple(jax.ShapeDtypeStruct(shape, F32) for shape in kept)
    items = 2 * tiles_here * TOPK + 4
    work = tiles_here * QW * BLK * 3 // 2
    return pl.pallas_call(
        kernel,
        in_specs=[SMEM] + [VMEM] * (n_q + n_src + len(state)),
        out_shape=out_shape,
        out_specs=(VMEM,) * n_out,
        scratch_shapes=[
            pltpu.VMEM((n_slots * BLK, HD), BF16),
            pltpu.VMEM((n_slots * BLK, 2 * HD), BF16),
            pltpu.VMEM((n_q, rows, QW), BF16),
            pltpu.SMEM((items,), jnp.int32),
            pltpu.SMEM((items,), jnp.int32),
        ]
        + ([pltpu.VMEM(shape, F32) for shape in kept] if last else []),
        compiler_params=pltpu.CompilerParams(
            vmem_limit_bytes=(24 if n_slots <= 16 else 56) * MIB
        ),
        cost_estimate=pl.CostEstimate(
            flops=8 * work * HD, transcendentals=work, bytes_accessed=4 * MIB
        ),
        name=name,
    )(sel, *[queries[k] for k in partners], *sources, *state)


def body(levels, subs, heads, queries, keys, values, selected):
    rows = queries.shape[0]
    tiles_here = selected.shape[0]
    level_blocks = subs * rows // BLK
    by_levels = levels == 4 and subs * rows % (2 * BLK) == 0

    def exchange(pieces, ks):
        return tuple(
            lax.ppermute(piece, "sub", [(i, i ^ k) for i in range(subs)]) if k else piece
            for k, piece in zip(ks, pieces)
        )

    everyone = tuple(range(subs))
    packed = pack_keys_values(subs, heads, keys, values)
    if by_levels:
        raw = lax.ppermute(packed, "lev", [(1, 3), (0, 1)])
    own = lax.all_to_all(packed, ("sub", "head"), 0, 0, tiled=True)
    q = pack_queries(subs, queries, selected)
    hop = subs // 2
    if hop > 1:
        over = exchange(q[hop:], [hop] * hop)
        q = exchange(q[:hop], range(hop)) + exchange(over, range(hop))
    else:
        q = exchange(q, everyone)
    if by_levels:
        own, raw = lax.optimization_barrier((own, raw))
        half = own.shape[0] // 2
        halves = lax.optimization_barrier((own[:half], own[half:]))
        up = [lax.ppermute(piece, "lev", [(0, 2), (2, 3)]) for piece in halves]
        p2 = lax.all_to_all(raw, ("sub", "head"), 0, 0, tiled=True)
        q, _ = lax.optimization_barrier((q, up))
        sel = jnp.concatenate([piece[rows, : tiles_here * TOPK] for piece in q]).astype(jnp.int32)
        forwards = lax.axis_index("lev") == 2
        last_up = [
            lax.ppermute(jnp.where(forwards, a, b), "lev", [(2, 3), (1, 2)])
            for a, b in zip(up, halves)
        ]

        def at(level, *which):
            base = jnp.int32(NONE)
            for here, holds in which:
                base = jnp.where(level == here, holds * level_blocks, base)
            return base

        def in_halves(base):
            return (base, base + level_blocks // 2)

        def early(level):
            return (
                level * level_blocks,
                *in_halves(at(level, (2, 0), (3, 2))),
                at(level, (1, 0), (3, 1)),
            )

        def late(level):
            return in_halves(at(level, (2, 1), (3, 0)))

        def whole_range(level):
            return early(level) + late(level)

        far, near = everyone[subs // 2 :], everyone[: subs // 2]
        state = attention(
            "far_early", True, False, far, early, q, sel, (own, *up, p2), ()
        )
        out_far = attention("far_late", False, True, far, late, q, sel, tuple(last_up), state)
        q_near, _ = lax.optimization_barrier((q[: subs // 2], out_far))
        q = tuple(q_near) + tuple(q[subs // 2 :])
        out_near = attention(
            "near", True, True, near, whole_range, q, sel, (own, *up, p2, *last_up), ()
        )
        begun = unpack_output("unpack_far", subs, exchange(out_far, far), far, ())
        return unpack_output("unpack_near", subs, exchange(out_near, near), near, (begun,))
    sel = jnp.concatenate([piece[rows, : tiles_here * TOPK] for piece in q]).astype(jnp.int32)
    whole = lax.all_gather(own, "lev", axis=0, tiled=True)
    out = attention("all", True, True, everyone, lambda level: (0,), q, sel, (whole,), ())
    if subs == 1:
        return out[0]
    return unpack_output("unpack", subs, exchange(out, everyone), everyone, ())


def solution(mesh):
    ctx, heads = mesh.shape["ctx"], mesh.shape["head"]
    subs = math.gcd(KVH // heads, ctx)
    if subs * heads != KVH:
        raise ValueError("unsupported mesh")
    levels = ctx // subs
    split = Mesh(mesh.devices.reshape(levels, subs, heads), ("lev", "sub", "head"))
    placed = (
        P(("lev", "sub"), "head"),
        P(("lev", "sub", "head"), None),
        P(("lev", "sub", "head"), None),
        P(("lev", "sub"), "head", None),
    )
    return jax.shard_map(
        functools.partial(body, levels, subs, heads),
        mesh=split,
        in_specs=placed,
        out_specs=P(("lev", "sub"), "head"),
        check_vma=False,
    )
```

```python
import functools
import math

import jax
import jax.numpy as jnp
from jax import lax
from jax.experimental import pallas as pl
from jax.experimental.pallas import tpu as pltpu
from jax.sharding import Mesh, PartitionSpec as P

HD = 128
QH = 32
KVH = 8
BLK = 512
TILE = 128
TOPK = 3
PER = QH // KVH
QW = PER * HD
EXTRA = 16

FLOOR = -1e30
SCALE = HD ** -0.5 * math.log2(math.e)
NONE = -100000
F32 = jnp.float32
BF16 = jnp.bfloat16
VMEM = pl.BlockSpec(memory_space=pltpu.VMEM)
SMEM = pl.BlockSpec(memory_space=pltpu.SMEM)
ANY = pl.BlockSpec(memory_space=pl.ANY)
MIB = 1024 * 1024


def dot_nt(a, b):
    return lax.dot_general(a, b, (((1,), (1,)), ((), ())), preferred_element_type=F32)


def dot_nn(a, b):
    return lax.dot_general(a, b, (((1,), (0,)), ((), ())), preferred_element_type=F32)


def copy_cost(bytes_moved):
    return pl.CostEstimate(flops=0, transcendentals=0, bytes_accessed=bytes_moved)


def pack_keys_values(subs, heads, keys, values):
    r = keys.shape[0]

    def kernel(k_ref, v_ref, out_ref):
        for sub in range(subs):
            for head in range(heads):
                at = (head * subs + sub) * HD
                out_ref[sub * heads + head, 0] = k_ref[:, at : at + HD]
                out_ref[sub * heads + head, 1] = v_ref[:, at : at + HD]

    return pl.pallas_call(
        kernel,
        in_specs=[VMEM, VMEM],
        out_specs=VMEM,
        out_shape=jax.ShapeDtypeStruct((subs * heads, 2, r, HD), BF16),
        cost_estimate=copy_cost(4 * keys.size * 2),
        name="pack_kv",
    )(keys, values)


def pack_queries(subs, queries, selected):
    rows = queries.shape[0]
    tiles_here = selected.shape[0]

    def kernel(sel_ref, q_ref, *outs):
        sub = lax.axis_index("sub") if subs > 1 else 0
        lane = lax.broadcasted_iota(jnp.int32, (EXTRA, QW), 1)
        for k, out_ref in enumerate(outs):
            head = sub ^ k
            out_ref[:rows] = q_ref[:, pl.ds(pl.multiple_of(head * QW, QW), QW)]
            row = jnp.zeros((EXTRA, QW), jnp.int32)
            for t in range(tiles_here):
                for e in range(TOPK):
                    row = jnp.where(lane == t * TOPK + e, sel_ref[t, head, e], row)
            out_ref[rows:] = row.astype(F32).astype(BF16)

    return pl.pallas_call(
        kernel,
        in_specs=[SMEM, VMEM],
        out_specs=(VMEM,) * subs,
        out_shape=(jax.ShapeDtypeStruct((rows + EXTRA, QW), BF16),) * subs,
        cost_estimate=copy_cost(2 * queries.size * 2),
        compiler_params=pltpu.CompilerParams(vmem_limit_bytes=8 * MIB),
        name="pack_q",
    )(selected, queries)


def unpack_output(name, subs, pieces, ks, begun):
    rows = pieces[0].shape[0]
    n = len(pieces)

    def kernel(*refs):
        out_ref, sems = refs[-2:]
        sub = lax.axis_index("sub")
        copies = []
        for i, k in enumerate(ks):
            at = pl.ds(pl.multiple_of((sub ^ k) * QW, QW), QW)
            copies.append(pltpu.make_async_copy(refs[i], out_ref.at[:, at], sems.at[i]))
        for copy in copies:
            copy.start()
        for copy in copies:
            copy.wait()

    return pl.pallas_call(
        kernel,
        in_specs=[VMEM] * n + [ANY] * len(begun),
        out_specs=ANY,
        out_shape=jax.ShapeDtypeStruct((rows, subs * QW), BF16),
        scratch_shapes=[pltpu.SemaphoreType.DMA((n,))],
        input_output_aliases={n: 0} if begun else {},
        cost_estimate=copy_cost(4 * n * rows * QW),
        compiler_params=pltpu.CompilerParams(vmem_limit_bytes=8 * MIB),
        name=name,
    )(*pieces, *begun)


def attention(
    name, first, last, partners, bases_of, queries, sel, sources, state, state_from=0
):
    parts, rows = len(queries), queries[0].shape[0] - EXTRA
    tiles_in_part = rows // TILE
    tiles_here = len(partners) * tiles_in_part
    r = sources[0].shape[2]
    per_block = BLK // r
    n_src = len(sources)
    slots = [src.shape[0] // per_block for src in sources]
    most = min(TOPK, sum(slots))
    n_q = len(partners)
    n_out = len(partners) if last else 2
    in_block = BLK // TILE
    one_block = parts > 1 and len(partners) * rows == BLK

    def kernel(*refs):
        sel_ref, q_refs = refs[0], refs[1 : 1 + n_q]
        src = refs[1 + n_q : 1 + n_q + n_src]
        rest = refs[1 + n_q + n_src :]
        m_in, acc_in = (None, None) if first else rest[:2]
        rest = rest if first else rest[2:]
        outs, k_buf, v_buf, m_tmp, acc_tmp, q_buf = rest[:n_out], *rest[n_out:]
        level = lax.axis_index("lev")
        sub = lax.axis_index("sub") if parts > 1 else 0
        for i, q_ref in enumerate(q_refs):
            q_buf[i] = q_ref[:rows]
        bases = bases_of(level)

        v_buf[:, HD:] = jnp.ones((sum(slots) * BLK, HD), BF16)
        start = 0
        for ref, base, n in zip(src, bases, slots):

            def fill(ref=ref, start=start, n=n):
                if n * per_block <= 8:
                    k_buf[start * BLK : (start + n) * BLK] = ref[:, 0].reshape(n * BLK, HD)
                    v_buf[start * BLK : (start + n) * BLK, :HD] = ref[:, 1].reshape(n * BLK, HD)
                else:

                    def chunk(i, carry):
                        at = pl.ds(pl.multiple_of(start * BLK + i * r, r), r)
                        k_buf[at] = ref[i, 0]
                        v_buf[at, :HD] = ref[i, 1]
                        return carry

                    lax.fori_loop(0, n * per_block, chunk, 0)

            if isinstance(base, int):
                fill()
            else:
                pl.when(base >= 0)(fill)
            start += n

        def own_part(t, part, at, slot, own, pieces):
            count = pieces * TILE
            keys_at = pl.ds(pl.multiple_of((own - bases[0]) * BLK, BLK), count)
            q_rows = pl.ds(pl.multiple_of(at, TILE), TILE)
            key_at = lax.broadcasted_iota(jnp.int32, (TILE, TILE), 1)
            query_at = lax.broadcasted_iota(jnp.int32, (TILE, TILE), 0)
            for j in range(PER):
                here = slice(j * TILE, (j + 1) * TILE)
                s = dot_nt(q_buf[part, q_rows, j * HD : (j + 1) * HD], k_buf[keys_at])
                edge = jnp.where(key_at <= query_at, s[:, count - TILE :], FLOOR)
                s = jnp.concatenate([s[:, : count - TILE], edge], axis=1) if pieces > 1 else edge
                m = jnp.max(s, axis=1, keepdims=True)
                p = jnp.exp2((s - m) * SCALE).astype(BF16)
                m_tmp[slot, here] = jnp.broadcast_to(m, (TILE, HD))
                acc_tmp[slot, here] = dot_nn(p, v_buf[keys_at])

        if first and one_block:
            first_part = level * parts
            own = (first_part + (sub ^ partners[0])) * tiles_in_part // in_block
            for i in range(in_block):
                part = own * (in_block // tiles_in_part) + i // tiles_in_part - first_part
                local = (part ^ sub) - partners[0]
                t = local * tiles_in_part + i % tiles_in_part
                own_part(t, local, i % tiles_in_part * TILE, t, own, i + 1)

        def one_tile(k, part, i, out_ref, out_at):
            t = part * tiles_in_part + i
            tile = (level * parts + (sub ^ k)) * tiles_in_part + i
            own = tile // in_block
            q_rows = pl.ds(pl.multiple_of(i * TILE, TILE), TILE)
            if first:
                m_old, acc_old, at_old = m_tmp, acc_tmp, t if one_block else 0
            else:
                m_old, acc_old, at_old = m_in, acc_in, t + (partners[0] - state_from) * tiles_in_part

            def finish(j, acc):
                out_ref[out_at, j * HD : (j + 1) * HD] = (acc[:, :HD] / acc[:, HD:]).astype(BF16)

            def keep(j, m, acc):
                outs[0][t, j * TILE : (j + 1) * TILE] = m
                outs[1][t, j * TILE : (j + 1) * TILE] = acc

            if first and not one_block:
                for pieces in range(1, in_block + 1):
                    pl.when(lax.rem(tile, in_block) == pieces - 1)(
                        functools.partial(own_part, t, part, i * TILE, 0, own, pieces)
                    )

            found = jnp.int32(0)
            where = [jnp.int32(0)] * most
            for e in range(TOPK):
                block = sel_ref[(k * tiles_in_part + i) * TOPK + e]
                start = 0
                for base, n in zip(bases, slots):
                    hit = (block != own) & (block >= base) & (block < base + n)
                    where = [
                        jnp.where(hit & (found == i), start + block - base, w)
                        for i, w in enumerate(where)
                    ]
                    found = found + hit.astype(jnp.int32)
                    start += n

            def others(n):
                at = [pl.ds(pl.multiple_of(w * BLK, BLK), BLK) for w in where[:n]]
                for j in range(PER):
                    here = slice(j * TILE, (j + 1) * TILE)
                    old = m_old[at_old, here]
                    acc = acc_old[at_old, here]
                    if n:
                        q = q_buf[part, q_rows, j * HD : (j + 1) * HD]
                        s = [dot_nt(q, k_buf[a]) for a in at]
                        s = jnp.concatenate(s, axis=1) if n > 1 else s[0]
                        m = jnp.maximum(old, jnp.max(s, axis=1, keepdims=True))
                        p = jnp.exp2((s - jnp.tile(m, (1, n * BLK // HD))) * SCALE).astype(BF16)
                        fade = jnp.exp2((old - m) * SCALE)
                        acc = acc * jnp.tile(fade, (1, 2))
                        for i, a in enumerate(at):
                            acc = acc + dot_nn(p[:, i * BLK : (i + 1) * BLK], v_buf[a])
                        old = m
                    if last:
                        finish(j, acc)
                    else:
                        keep(j, old, acc)

            for n in range(most + 1):
                pl.when(found == n)(functools.partial(others, n))

        if last:
            for part, (out_ref, k) in enumerate(zip(outs, partners)):

                def step(i, carry, out_ref=out_ref, k=k, part=part):
                    out_at = pl.ds(pl.multiple_of(i * TILE, TILE), TILE)
                    one_tile(k, part, i, out_ref, out_at)
                    return carry

                lax.fori_loop(0, tiles_in_part, step, 0)
        else:

            def step(t, carry):
                part = t // tiles_in_part
                one_tile(partners[0] + part, part, lax.rem(t, tiles_in_part), None, None)
                return carry

            lax.fori_loop(0, tiles_here, step, 0)

    if last:
        out_shape = tuple(jax.ShapeDtypeStruct((rows, QW), BF16) for _ in partners)
    else:
        out_shape = (
            jax.ShapeDtypeStruct((tiles_here, QW, HD), F32),
            jax.ShapeDtypeStruct((tiles_here, QW, 2 * HD), F32),
        )
    work = tiles_here * QW * BLK * 3 // 2
    return pl.pallas_call(
        kernel,
        in_specs=[SMEM] + [VMEM] * (n_q + n_src + len(state)),
        out_shape=out_shape,
        out_specs=(VMEM,) * n_out,
        scratch_shapes=[
            pltpu.VMEM((sum(slots) * BLK, HD), BF16),
            pltpu.VMEM((sum(slots) * BLK, 2 * HD), BF16),
            pltpu.VMEM((tiles_here if one_block else 1, QW, HD), F32),
            pltpu.VMEM((tiles_here if one_block else 1, QW, 2 * HD), F32),
            pltpu.VMEM((n_q, rows, QW), BF16),
        ],
        compiler_params=pltpu.CompilerParams(
            vmem_limit_bytes=(24 if sum(slots) <= 16 else 56) * MIB
        ),
        cost_estimate=pl.CostEstimate(
            flops=8 * work * HD, transcendentals=work, bytes_accessed=4 * MIB
        ),
        name=name,
    )(sel, *[queries[k] for k in partners], *sources, *state)


def body(levels, subs, heads, queries, keys, values, selected):
    rows = queries.shape[0]
    tiles_here = selected.shape[0]
    level_blocks = subs * rows // BLK
    by_levels = levels == 4 and subs * rows % (2 * BLK) == 0

    def exchange(pieces, ks):
        return tuple(
            lax.ppermute(piece, "sub", [(i, i ^ k) for i in range(subs)]) if k else piece
            for k, piece in zip(ks, pieces)
        )

    everyone = tuple(range(subs))
    packed = pack_keys_values(subs, heads, keys, values)
    if by_levels:
        raw = lax.ppermute(packed, "lev", [(1, 3), (0, 1)])
    own = lax.all_to_all(packed, ("sub", "head"), 0, 0, tiled=True)
    q = pack_queries(subs, queries, selected)
    hop = subs // 2
    if hop > 1:
        over = exchange(q[hop:], [hop] * hop)
        q = exchange(q[:hop], range(hop)) + exchange(over, range(hop))
    else:
        q = exchange(q, everyone)
    if by_levels:
        own, raw = lax.optimization_barrier((own, raw))
        half = own.shape[0] // 2
        halves = lax.optimization_barrier((own[:half], own[half:]))
        up = [lax.ppermute(piece, "lev", [(0, 2), (2, 3)]) for piece in halves]
        p2 = lax.all_to_all(raw, ("sub", "head"), 0, 0, tiled=True)
        q, _ = lax.optimization_barrier((q, up))
        sel = jnp.concatenate([piece[rows, : tiles_here * TOPK] for piece in q]).astype(jnp.int32)
        forwards = lax.axis_index("lev") == 2
        last_up = [
            lax.ppermute(jnp.where(forwards, a, b), "lev", [(2, 3), (1, 2)])
            for a, b in zip(up, halves)
        ]

        def at(level, *which):
            base = jnp.int32(NONE)
            for here, holds in which:
                base = jnp.where(level == here, holds * level_blocks, base)
            return base

        def in_halves(base):
            return (base, base + level_blocks // 2)

        def early(level):
            return (
                level * level_blocks,
                *in_halves(at(level, (2, 0), (3, 2))),
                at(level, (1, 0), (3, 1)),
            )

        def late(level):
            return in_halves(at(level, (2, 1), (3, 0)))

        def whole_range(level):
            return early(level) + late(level)

        far, near = everyone[subs // 2 :], everyone[: subs // 2]
        state = attention(
            "far_early", True, False, far, early, q, sel, (own, *up, p2), ()
        )
        out_far = ()
        for k in far:
            out_far += attention(
                "far_late", False, True, (k,), late, q, sel, tuple(last_up), state, far[0]
            )
        q_near, _ = lax.optimization_barrier((q[: subs // 2], out_far))
        q = tuple(q_near) + tuple(q[subs // 2 :])
        out_near = attention(
            "near", True, True, near, whole_range, q, sel, (own, *up, p2, *last_up), ()
        )
        begun = unpack_output("unpack_far", subs, exchange(out_far, far), far, ())
        return unpack_output("unpack_near", subs, exchange(out_near, near), near, (begun,))
    sel = jnp.concatenate([piece[rows, : tiles_here * TOPK] for piece in q]).astype(jnp.int32)
    whole = lax.all_gather(own, "lev", axis=0, tiled=True)
    out = attention("all", True, True, everyone, lambda level: (0,), q, sel, (whole,), ())
    if subs == 1:
        return out[0]
    return unpack_output("unpack", subs, exchange(out, everyone), everyone, ())


def solution(mesh):
    ctx, heads = mesh.shape["ctx"], mesh.shape["head"]
    subs = math.gcd(KVH // heads, ctx)
    if subs * heads != KVH:
        raise ValueError("unsupported mesh")
    levels = ctx // subs
    split = Mesh(mesh.devices.reshape(levels, subs, heads), ("lev", "sub", "head"))
    placed = (
        P(("lev", "sub"), "head"),
        P(("lev", "sub", "head"), None),
        P(("lev", "sub", "head"), None),
        P(("lev", "sub"), "head", None),
    )
    return jax.shard_map(
        functools.partial(body, levels, subs, heads),
        mesh=split,
        in_specs=placed,
        out_specs=P(("lev", "sub"), "head"),
        check_vma=False,
    )
```

```python
import functools
import math

import jax
import jax.numpy as jnp
from jax import lax
from jax.experimental import pallas as pl
from jax.experimental.pallas import tpu as pltpu
from jax.sharding import Mesh, PartitionSpec as P

HD = 128
QH = 32
KVH = 8
BLK = 512
TILE = 128
TOPK = 3
PER = QH // KVH
QW = PER * HD
EXTRA = 16
TOGETHER = 2

FLOOR = -1e30
SCALE = HD ** -0.5 * math.log2(math.e)
NONE = -100000
F32 = jnp.float32
BF16 = jnp.bfloat16
VMEM = pl.BlockSpec(memory_space=pltpu.VMEM)
SMEM = pl.BlockSpec(memory_space=pltpu.SMEM)
ANY = pl.BlockSpec(memory_space=pl.ANY)
MIB = 1024 * 1024


def dot_nt(a, b):
    return lax.dot_general(a, b, (((1,), (1,)), ((), ())), preferred_element_type=F32)


def dot_nn(a, b):
    return lax.dot_general(a, b, (((1,), (0,)), ((), ())), preferred_element_type=F32)


def copy_cost(bytes_moved):
    return pl.CostEstimate(flops=0, transcendentals=0, bytes_accessed=bytes_moved)


def pack_keys_values(subs, heads, keys, values):
    r = keys.shape[0]

    def kernel(k_ref, v_ref, out_ref):
        for sub in range(subs):
            for head in range(heads):
                at = (head * subs + sub) * HD
                out_ref[sub * heads + head, 0] = k_ref[:, at : at + HD]
                out_ref[sub * heads + head, 1] = v_ref[:, at : at + HD]

    return pl.pallas_call(
        kernel,
        in_specs=[VMEM, VMEM],
        out_specs=VMEM,
        out_shape=jax.ShapeDtypeStruct((subs * heads, 2, r, HD), BF16),
        cost_estimate=copy_cost(4 * keys.size * 2),
        name="pack_kv",
    )(keys, values)


def pack_queries(subs, queries, selected):
    rows = queries.shape[0]
    tiles_here = selected.shape[0]

    def kernel(sel_ref, q_ref, *outs):
        sub = lax.axis_index("sub") if subs > 1 else 0
        lane = lax.broadcasted_iota(jnp.int32, (EXTRA, QW), 1)
        for k, out_ref in enumerate(outs):
            head = sub ^ k
            out_ref[:rows] = q_ref[:, pl.ds(pl.multiple_of(head * QW, QW), QW)]
            row = jnp.zeros((EXTRA, QW), jnp.int32)
            for t in range(tiles_here):
                for e in range(TOPK):
                    row = jnp.where(lane == t * TOPK + e, sel_ref[t, head, e], row)
            out_ref[rows:] = row.astype(F32).astype(BF16)

    return pl.pallas_call(
        kernel,
        in_specs=[SMEM, VMEM],
        out_specs=(VMEM,) * subs,
        out_shape=(jax.ShapeDtypeStruct((rows + EXTRA, QW), BF16),) * subs,
        cost_estimate=copy_cost(2 * queries.size * 2),
        compiler_params=pltpu.CompilerParams(vmem_limit_bytes=8 * MIB),
        name="pack_q",
    )(selected, queries)


def unpack_output(name, subs, pieces, ks, begun):
    rows = pieces[0].shape[0]
    n = len(pieces)

    def kernel(*refs):
        out_ref, sems = refs[-2:]
        sub = lax.axis_index("sub")
        copies = []
        for i, k in enumerate(ks):
            at = pl.ds(pl.multiple_of((sub ^ k) * QW, QW), QW)
            copies.append(pltpu.make_async_copy(refs[i], out_ref.at[:, at], sems.at[i]))
        for copy in copies:
            copy.start()
        for copy in copies:
            copy.wait()

    return pl.pallas_call(
        kernel,
        in_specs=[VMEM] * n + [ANY] * len(begun),
        out_specs=ANY,
        out_shape=jax.ShapeDtypeStruct((rows, subs * QW), BF16),
        scratch_shapes=[pltpu.SemaphoreType.DMA((n,))],
        input_output_aliases={n: 0} if begun else {},
        cost_estimate=copy_cost(4 * n * rows * QW),
        compiler_params=pltpu.CompilerParams(vmem_limit_bytes=8 * MIB),
        name=name,
    )(*pieces, *begun)


def attention(
    name, first, last, partners, bases_of, queries, sel, sources, state, state_from=0
):
    parts, rows = len(queries), queries[0].shape[0] - EXTRA
    tiles_in_part = rows // TILE
    tiles_here = len(partners) * tiles_in_part
    r = sources[0].shape[2]
    per_block = BLK // r
    n_src = len(sources)
    slots = [src.shape[0] // per_block for src in sources]
    most = min(TOPK, sum(slots))
    n_q = len(partners)
    n_out = len(partners) if last else 2
    in_block = BLK // TILE
    one_block = parts > 1 and len(partners) * rows == BLK

    def kernel(*refs):
        sel_ref, q_refs = refs[0], refs[1 : 1 + n_q]
        src = refs[1 + n_q : 1 + n_q + n_src]
        rest = refs[1 + n_q + n_src :]
        m_in, acc_in = (None, None) if first else rest[:2]
        rest = rest if first else rest[2:]
        outs, k_buf, v_buf, m_tmp, acc_tmp, q_buf = rest[:n_out], *rest[n_out:]
        level = lax.axis_index("lev")
        sub = lax.axis_index("sub") if parts > 1 else 0
        for i, q_ref in enumerate(q_refs):
            q_buf[i] = q_ref[:rows]
        bases = bases_of(level)

        v_buf[:, HD:] = jnp.ones((sum(slots) * BLK, HD), BF16)
        start = 0
        for ref, base, n in zip(src, bases, slots):

            def fill(ref=ref, start=start, n=n):
                if n * per_block <= 8:
                    k_buf[start * BLK : (start + n) * BLK] = ref[:, 0].reshape(n * BLK, HD)
                    v_buf[start * BLK : (start + n) * BLK, :HD] = ref[:, 1].reshape(n * BLK, HD)
                else:

                    def chunk(i, carry):
                        at = pl.ds(pl.multiple_of(start * BLK + i * r, r), r)
                        k_buf[at] = ref[i, 0]
                        v_buf[at, :HD] = ref[i, 1]
                        return carry

                    lax.fori_loop(0, n * per_block, chunk, 0)

            if isinstance(base, int):
                fill()
            else:
                pl.when(base >= 0)(fill)
            start += n

        def own_part(t, part, at, slot, own, pieces):
            count = pieces * TILE
            keys_at = pl.ds(pl.multiple_of((own - bases[0]) * BLK, BLK), count)
            q_rows = pl.ds(pl.multiple_of(at, TILE), TILE)
            key_at = lax.broadcasted_iota(jnp.int32, (TILE, TILE), 1)
            query_at = lax.broadcasted_iota(jnp.int32, (TILE, TILE), 0)
            for j in range(PER):
                here = slice(j * TILE, (j + 1) * TILE)
                s = dot_nt(q_buf[part, q_rows, j * HD : (j + 1) * HD], k_buf[keys_at])
                edge = jnp.where(key_at <= query_at, s[:, count - TILE :], FLOOR)
                s = jnp.concatenate([s[:, : count - TILE], edge], axis=1) if pieces > 1 else edge
                m = jnp.max(s, axis=1, keepdims=True)
                p = jnp.exp2((s - m) * SCALE).astype(BF16)
                m_tmp[slot, here] = jnp.broadcast_to(m, (TILE, HD))
                acc_tmp[slot, here] = dot_nn(p, v_buf[keys_at])

        if first and one_block:
            first_part = level * parts
            own = (first_part + (sub ^ partners[0])) * tiles_in_part // in_block
            for i in range(in_block):
                part = own * (in_block // tiles_in_part) + i // tiles_in_part - first_part
                local = (part ^ sub) - partners[0]
                t = local * tiles_in_part + i % tiles_in_part
                own_part(t, local, i % tiles_in_part * TILE, t, own, i + 1)

        def one_tile(k, part, i, out_ref, out_at):
            t = part * tiles_in_part + i
            tile = (level * parts + (sub ^ k)) * tiles_in_part + i
            own = tile // in_block
            q_rows = pl.ds(pl.multiple_of(i * TILE, TILE), TILE)
            if first:
                m_old, acc_old, at_old = m_tmp, acc_tmp, t if one_block else 0
            else:
                m_old, acc_old, at_old = m_in, acc_in, t + (partners[0] - state_from) * tiles_in_part

            def finish(j, acc):
                out_ref[out_at, j * HD : (j + 1) * HD] = (acc[:, :HD] / acc[:, HD:]).astype(BF16)

            def keep(j, m, acc):
                outs[0][t, j * TILE : (j + 1) * TILE] = m
                outs[1][t, j * TILE : (j + 1) * TILE] = acc

            if first and not one_block:
                for pieces in range(1, in_block + 1):
                    pl.when(lax.rem(tile, in_block) == pieces - 1)(
                        functools.partial(own_part, t, part, i * TILE, 0, own, pieces)
                    )

            found = jnp.int32(0)
            where = [jnp.int32(0)] * most
            for e in range(TOPK):
                block = sel_ref[(k * tiles_in_part + i) * TOPK + e]
                start = 0
                for base, n in zip(bases, slots):
                    hit = (block != own) & (block >= base) & (block < base + n)
                    where = [
                        jnp.where(hit & (found == i), start + block - base, w)
                        for i, w in enumerate(where)
                    ]
                    found = found + hit.astype(jnp.int32)
                    start += n

            def others(n):
                at = [pl.ds(pl.multiple_of(w * BLK, BLK), BLK) for w in where[:n]]

                def scores(c):
                    heads = range(c * TOGETHER, (c + 1) * TOGETHER)
                    q = [q_buf[part, q_rows, j * HD : (j + 1) * HD] for j in heads]
                    q = jnp.concatenate(q, axis=0)
                    s = [dot_nt(q, k_buf[a]) for a in at]
                    return jnp.concatenate(s, axis=1) if n > 1 else s[0]

                chains = range(PER // TOGETHER)
                ready = [scores(c) for c in chains] if n else None
                for c in chains:
                    here = slice(c * TOGETHER * TILE, (c + 1) * TOGETHER * TILE)
                    m = m_old[at_old, here]
                    acc = acc_old[at_old, here]
                    if n:
                        old, s = m, ready[c]
                        m = jnp.maximum(old, jnp.max(s, axis=1, keepdims=True))
                        p = jnp.exp2((s - jnp.tile(m, (1, n * BLK // HD))) * SCALE).astype(BF16)
                        acc = acc * jnp.tile(jnp.exp2((old - m) * SCALE), (1, 2))
                        for i, a in enumerate(at):
                            acc = acc + dot_nn(p[:, i * BLK : (i + 1) * BLK], v_buf[a])
                    for i in range(TOGETHER):
                        j, rows_of = c * TOGETHER + i, slice(i * TILE, (i + 1) * TILE)
                        if last:
                            finish(j, acc[rows_of])
                        else:
                            keep(j, m[rows_of], acc[rows_of])

            for n in range(most + 1):
                pl.when(found == n)(functools.partial(others, n))

        if last:
            for part, (out_ref, k) in enumerate(zip(outs, partners)):

                def step(i, carry, out_ref=out_ref, k=k, part=part):
                    out_at = pl.ds(pl.multiple_of(i * TILE, TILE), TILE)
                    one_tile(k, part, i, out_ref, out_at)
                    return carry

                lax.fori_loop(0, tiles_in_part, step, 0)
        else:

            def step(t, carry):
                part = t // tiles_in_part
                one_tile(partners[0] + part, part, lax.rem(t, tiles_in_part), None, None)
                return carry

            lax.fori_loop(0, tiles_here, step, 0)

    if last:
        out_shape = tuple(jax.ShapeDtypeStruct((rows, QW), BF16) for _ in partners)
    else:
        out_shape = (
            jax.ShapeDtypeStruct((tiles_here, QW, HD), F32),
            jax.ShapeDtypeStruct((tiles_here, QW, 2 * HD), F32),
        )
    work = tiles_here * QW * BLK * 3 // 2
    return pl.pallas_call(
        kernel,
        in_specs=[SMEM] + [VMEM] * (n_q + n_src + len(state)),
        out_shape=out_shape,
        out_specs=(VMEM,) * n_out,
        scratch_shapes=[
            pltpu.VMEM((sum(slots) * BLK, HD), BF16),
            pltpu.VMEM((sum(slots) * BLK, 2 * HD), BF16),
            pltpu.VMEM((tiles_here if one_block else 1, QW, HD), F32),
            pltpu.VMEM((tiles_here if one_block else 1, QW, 2 * HD), F32),
            pltpu.VMEM((n_q, rows, QW), BF16),
        ],
        compiler_params=pltpu.CompilerParams(
            vmem_limit_bytes=(24 if sum(slots) <= 16 else 56) * MIB
        ),
        cost_estimate=pl.CostEstimate(
            flops=8 * work * HD, transcendentals=work, bytes_accessed=4 * MIB
        ),
        name=name,
    )(sel, *[queries[k] for k in partners], *sources, *state)


def body(levels, subs, heads, queries, keys, values, selected):
    rows = queries.shape[0]
    tiles_here = selected.shape[0]
    level_blocks = subs * rows // BLK
    by_levels = levels == 4 and subs >= 4 and subs * rows % (2 * BLK) == 0

    def exchange(pieces, ks):
        return tuple(
            lax.ppermute(piece, "sub", [(i, i ^ k) for i in range(subs)]) if k else piece
            for k, piece in zip(ks, pieces)
        )

    everyone = tuple(range(subs))
    packed = pack_keys_values(subs, heads, keys, values)
    if by_levels:
        raw = lax.ppermute(packed, "lev", [(1, 3), (0, 1)])
    own = lax.all_to_all(packed, ("sub", "head"), 0, 0, tiled=True)
    q = pack_queries(subs, queries, selected)
    hop = subs // 2
    if hop > 1:
        over = exchange(q[hop:], [hop] * hop)
        q = exchange(q[:hop], range(hop)) + exchange(over, range(hop))
    else:
        q = exchange(q, everyone)
    if by_levels:
        own, raw = lax.optimization_barrier((own, raw))
        half = own.shape[0] // 2
        halves = lax.optimization_barrier((own[:half], own[half:]))
        up = [lax.ppermute(piece, "lev", [(0, 2), (2, 3)]) for piece in halves]
        p2 = lax.all_to_all(raw, ("sub", "head"), 0, 0, tiled=True)
        q, _ = lax.optimization_barrier((q, up))
        sel = jnp.concatenate([piece[rows, : tiles_here * TOPK] for piece in q]).astype(jnp.int32)
        forwards = lax.axis_index("lev") == 2
        last_up = [
            lax.ppermute(jnp.where(forwards, a, b), "lev", [(2, 3), (1, 2)])
            for a, b in zip(up, halves)
        ]

        def at(level, *which):
            base = jnp.int32(NONE)
            for here, holds in which:
                base = jnp.where(level == here, holds * level_blocks, base)
            return base

        def in_halves(base):
            return (base, base + level_blocks // 2)

        def early(level):
            return (
                level * level_blocks,
                *in_halves(at(level, (2, 0), (3, 2))),
                at(level, (1, 0), (3, 1)),
            )

        def late(level):
            return in_halves(at(level, (2, 1), (3, 0)))

        def whole_range(level):
            return early(level) + late(level)

        far, near = everyone[subs // 2 :], everyone[: subs // 2]
        state = attention(
            "far_early", True, False, far, early, q, sel, (own, *up, p2), ()
        )
        out_far = ()
        for k in far:
            out_far += attention(
                "far_late", False, True, (k,), late, q, sel, tuple(last_up), state, far[0]
            )
        q_near, _ = lax.optimization_barrier((q[: subs // 2], out_far))
        q = tuple(q_near) + tuple(q[subs // 2 :])
        out_near = attention(
            "near", True, True, near, whole_range, q, sel, (own, *up, p2, *last_up), ()
        )
        out_near, out_far = exchange(out_near, near), exchange(out_far, far)
        begun = unpack_output("unpack_most", subs, (*out_far, out_near[0]), (*far, 0), ())
        return unpack_output("unpack_rest", subs, out_near[1:], near[1:], (begun,))
    sel = jnp.concatenate([piece[rows, : tiles_here * TOPK] for piece in q]).astype(jnp.int32)
    whole = lax.all_gather(own, "lev", axis=0, tiled=True)
    out = attention("all", True, True, everyone, lambda level: (0,), q, sel, (whole,), ())
    if subs == 1:
        return out[0]
    return unpack_output("unpack", subs, exchange(out, everyone), everyone, ())


def solution(mesh):
    ctx, heads = mesh.shape["ctx"], mesh.shape["head"]
    subs = math.gcd(KVH // heads, ctx)
    if subs * heads != KVH:
        raise ValueError("unsupported mesh")
    levels = ctx // subs
    split = Mesh(mesh.devices.reshape(levels, subs, heads), ("lev", "sub", "head"))
    placed = (
        P(("lev", "sub"), "head"),
        P(("lev", "sub", "head"), None),
        P(("lev", "sub", "head"), None),
        P(("lev", "sub"), "head", None),
    )
    return jax.shard_map(
        functools.partial(body, levels, subs, heads),
        mesh=split,
        in_specs=placed,
        out_specs=P(("lev", "sub"), "head"),
        check_vma=False,
    )
```

```python
import functools
import math

import jax
import jax.numpy as jnp
from jax import lax
from jax.experimental import pallas as pl
from jax.experimental.pallas import tpu as pltpu
from jax.sharding import Mesh, PartitionSpec as P

HD = 128
QH = 32
KVH = 8
BLK = 512
TILE = 128
TOPK = 3
PER = QH // KVH
QW = PER * HD
EXTRA = 16
TOGETHER = 2

FLOOR = -1e30
SCALE = HD ** -0.5 * math.log2(math.e)
NONE = -100000
F32 = jnp.float32
BF16 = jnp.bfloat16
VMEM = pl.BlockSpec(memory_space=pltpu.VMEM)
SMEM = pl.BlockSpec(memory_space=pltpu.SMEM)
ANY = pl.BlockSpec(memory_space=pl.ANY)
MIB = 1024 * 1024


def dot_nt(a, b):
    return lax.dot_general(a, b, (((1,), (1,)), ((), ())), preferred_element_type=F32)


def dot_nn(a, b):
    return lax.dot_general(a, b, (((1,), (0,)), ((), ())), preferred_element_type=F32)


def copy_cost(bytes_moved):
    return pl.CostEstimate(flops=0, transcendentals=0, bytes_accessed=bytes_moved)


def pack_keys_values(subs, heads, keys, values):
    r = keys.shape[0]

    def kernel(k_ref, v_ref, out_ref):
        for sub in range(subs):
            for head in range(heads):
                at = (head * subs + sub) * HD
                out_ref[sub * heads + head, 0] = k_ref[:, at : at + HD]
                out_ref[sub * heads + head, 1] = v_ref[:, at : at + HD]

    return pl.pallas_call(
        kernel,
        in_specs=[VMEM, VMEM],
        out_specs=VMEM,
        out_shape=jax.ShapeDtypeStruct((subs * heads, 2, r, HD), BF16),
        cost_estimate=copy_cost(4 * keys.size * 2),
        name="pack_kv",
    )(keys, values)


def pack_queries(subs, queries, selected):
    rows = queries.shape[0]
    tiles_here = selected.shape[0]

    def kernel(sel_ref, q_ref, *outs):
        sub = lax.axis_index("sub") if subs > 1 else 0
        lane = lax.broadcasted_iota(jnp.int32, (EXTRA, QW), 1)
        for k, out_ref in enumerate(outs):
            head = sub ^ k
            out_ref[:rows] = q_ref[:, pl.ds(pl.multiple_of(head * QW, QW), QW)]
            row = jnp.zeros((EXTRA, QW), jnp.int32)
            for t in range(tiles_here):
                for e in range(TOPK):
                    row = jnp.where(lane == t * TOPK + e, sel_ref[t, head, e], row)
            out_ref[rows:] = row.astype(F32).astype(BF16)

    return pl.pallas_call(
        kernel,
        in_specs=[SMEM, VMEM],
        out_specs=(VMEM,) * subs,
        out_shape=(jax.ShapeDtypeStruct((rows + EXTRA, QW), BF16),) * subs,
        cost_estimate=copy_cost(2 * queries.size * 2),
        compiler_params=pltpu.CompilerParams(vmem_limit_bytes=8 * MIB),
        name="pack_q",
    )(selected, queries)


def unpack_output(name, subs, pieces, ks, begun):
    rows = pieces[0].shape[0]
    n = len(pieces)

    def kernel(*refs):
        out_ref, sems = refs[-2:]
        sub = lax.axis_index("sub")
        copies = []
        for i, k in enumerate(ks):
            at = pl.ds(pl.multiple_of((sub ^ k) * QW, QW), QW)
            copies.append(pltpu.make_async_copy(refs[i], out_ref.at[:, at], sems.at[i]))
        for copy in copies:
            copy.start()
        for copy in copies:
            copy.wait()

    return pl.pallas_call(
        kernel,
        in_specs=[VMEM] * n + [ANY] * len(begun),
        out_specs=ANY,
        out_shape=jax.ShapeDtypeStruct((rows, subs * QW), BF16),
        scratch_shapes=[pltpu.SemaphoreType.DMA((n,))],
        input_output_aliases={n: 0} if begun else {},
        cost_estimate=copy_cost(4 * n * rows * QW),
        compiler_params=pltpu.CompilerParams(vmem_limit_bytes=8 * MIB),
        name=name,
    )(*pieces, *begun)


def attention(
    name, first, last, partners, bases_of, queries, sel, sources, state, state_from=0
):
    parts, rows = len(queries), queries[0].shape[0] - EXTRA
    tiles_in_part = rows // TILE
    tiles_here = len(partners) * tiles_in_part
    r = sources[0].shape[2]
    per_block = BLK // r
    n_src = len(sources)
    slots = [src.shape[0] // per_block for src in sources]
    most = min(TOPK, sum(slots))
    n_q = len(partners)
    n_out = len(partners) if last else 2
    in_block = BLK // TILE
    one_block = parts > 1 and len(partners) * rows == BLK

    def kernel(*refs):
        sel_ref, q_refs = refs[0], refs[1 : 1 + n_q]
        src = refs[1 + n_q : 1 + n_q + n_src]
        rest = refs[1 + n_q + n_src :]
        m_in, acc_in = (None, None) if first else rest[:2]
        rest = rest if first else rest[2:]
        outs, k_buf, v_buf, m_tmp, acc_tmp, q_buf = rest[:n_out], *rest[n_out:]
        level = lax.axis_index("lev")
        sub = lax.axis_index("sub") if parts > 1 else 0
        for i, q_ref in enumerate(q_refs):
            q_buf[i] = q_ref[:rows]
        bases = bases_of(level)

        v_buf[:, HD:] = jnp.ones((sum(slots) * BLK, HD), BF16)
        start = 0
        for ref, base, n in zip(src, bases, slots):

            def fill(ref=ref, start=start, n=n):
                if n * per_block <= 8:
                    k_buf[start * BLK : (start + n) * BLK] = ref[:, 0].reshape(n * BLK, HD)
                    v_buf[start * BLK : (start + n) * BLK, :HD] = ref[:, 1].reshape(n * BLK, HD)
                else:

                    def chunk(i, carry):
                        at = pl.ds(pl.multiple_of(start * BLK + i * r, r), r)
                        k_buf[at] = ref[i, 0]
                        v_buf[at, :HD] = ref[i, 1]
                        return carry

                    lax.fori_loop(0, n * per_block, chunk, 0)

            if isinstance(base, int):
                fill()
            else:
                pl.when(base >= 0)(fill)
            start += n

        def own_part(t, part, at, slot, own, pieces):
            count = pieces * TILE
            keys_at = pl.ds(pl.multiple_of((own - bases[0]) * BLK, BLK), count)
            q_rows = pl.ds(pl.multiple_of(at, TILE), TILE)
            key_at = lax.broadcasted_iota(jnp.int32, (TILE, TILE), 1)
            query_at = lax.broadcasted_iota(jnp.int32, (TILE, TILE), 0)
            for j in range(PER):
                here = slice(j * TILE, (j + 1) * TILE)
                s = dot_nt(q_buf[part, q_rows, j * HD : (j + 1) * HD], k_buf[keys_at])
                edge = jnp.where(key_at <= query_at, s[:, count - TILE :], FLOOR)
                s = jnp.concatenate([s[:, : count - TILE], edge], axis=1) if pieces > 1 else edge
                m = jnp.max(s, axis=1, keepdims=True)
                p = jnp.exp2((s - m) * SCALE).astype(BF16)
                m_tmp[slot, here] = jnp.broadcast_to(m, (TILE, HD))
                acc_tmp[slot, here] = dot_nn(p, v_buf[keys_at])

        if first and one_block:
            first_part = level * parts
            own = (first_part + (sub ^ partners[0])) * tiles_in_part // in_block
            for i in range(in_block):
                part = own * (in_block // tiles_in_part) + i // tiles_in_part - first_part
                local = (part ^ sub) - partners[0]
                t = local * tiles_in_part + i % tiles_in_part
                own_part(t, local, i % tiles_in_part * TILE, t, own, i + 1)

        def one_tile(k, part, i, out_ref, out_at):
            t = part * tiles_in_part + i
            tile = (level * parts + (sub ^ k)) * tiles_in_part + i
            own = tile // in_block
            q_rows = pl.ds(pl.multiple_of(i * TILE, TILE), TILE)
            if first:
                m_old, acc_old, at_old = m_tmp, acc_tmp, t if one_block else 0
            else:
                m_old, acc_old, at_old = m_in, acc_in, t + (partners[0] - state_from) * tiles_in_part

            def finish(j, acc):
                out_ref[out_at, j * HD : (j + 1) * HD] = (acc[:, :HD] / acc[:, HD:]).astype(BF16)

            def keep(j, m, acc):
                outs[0][t, j * TILE : (j + 1) * TILE] = m
                outs[1][t, j * TILE : (j + 1) * TILE] = acc

            if first and not one_block:
                for pieces in range(1, in_block + 1):
                    pl.when(lax.rem(tile, in_block) == pieces - 1)(
                        functools.partial(own_part, t, part, i * TILE, 0, own, pieces)
                    )

            found = jnp.int32(0)
            where = [jnp.int32(0)] * most
            for e in range(TOPK):
                block = sel_ref[(k * tiles_in_part + i) * TOPK + e]
                start = 0
                for base, n in zip(bases, slots):
                    hit = (block != own) & (block >= base) & (block < base + n)
                    where = [
                        jnp.where(hit & (found == i), start + block - base, w)
                        for i, w in enumerate(where)
                    ]
                    found = found + hit.astype(jnp.int32)
                    start += n

            def others(n):
                at = [pl.ds(pl.multiple_of(w * BLK, BLK), BLK) for w in where[:n]]

                def scores(c):
                    heads = range(c * TOGETHER, (c + 1) * TOGETHER)
                    q = [q_buf[part, q_rows, j * HD : (j + 1) * HD] for j in heads]
                    q = jnp.concatenate(q, axis=0)
                    s = [dot_nt(q, k_buf[a]) for a in at]
                    return jnp.concatenate(s, axis=1) if n > 1 else s[0]

                chains = range(PER // TOGETHER)
                ready = [scores(c) for c in chains] if n else None
                for c in chains:
                    here = slice(c * TOGETHER * TILE, (c + 1) * TOGETHER * TILE)
                    m = m_old[at_old, here]
                    acc = acc_old[at_old, here]
                    if n:
                        old, s = m, ready[c]
                        m = jnp.maximum(old, jnp.max(s, axis=1, keepdims=True))
                        p = jnp.exp2((s - jnp.tile(m, (1, n * BLK // HD))) * SCALE).astype(BF16)
                        acc = acc * jnp.tile(jnp.exp2((old - m) * SCALE), (1, 2))
                        for i, a in enumerate(at):
                            acc = acc + dot_nn(p[:, i * BLK : (i + 1) * BLK], v_buf[a])
                    for i in range(TOGETHER):
                        j, rows_of = c * TOGETHER + i, slice(i * TILE, (i + 1) * TILE)
                        if last:
                            finish(j, acc[rows_of])
                        else:
                            keep(j, m[rows_of], acc[rows_of])

            for n in range(most + 1):
                pl.when(found == n)(functools.partial(others, n))

        if last:
            for part, (out_ref, k) in enumerate(zip(outs, partners)):

                def step(i, carry, out_ref=out_ref, k=k, part=part):
                    out_at = pl.ds(pl.multiple_of(i * TILE, TILE), TILE)
                    one_tile(k, part, i, out_ref, out_at)
                    return carry

                lax.fori_loop(0, tiles_in_part, step, 0)
        else:

            def step(t, carry):
                part = t // tiles_in_part
                one_tile(partners[0] + part, part, lax.rem(t, tiles_in_part), None, None)
                return carry

            lax.fori_loop(0, tiles_here, step, 0)

    if last:
        out_shape = tuple(jax.ShapeDtypeStruct((rows, QW), BF16) for _ in partners)
    else:
        out_shape = (
            jax.ShapeDtypeStruct((tiles_here, QW, HD), F32),
            jax.ShapeDtypeStruct((tiles_here, QW, 2 * HD), F32),
        )
    work = tiles_here * QW * BLK * 3 // 2
    return pl.pallas_call(
        kernel,
        in_specs=[SMEM] + [VMEM] * (n_q + n_src + len(state)),
        out_shape=out_shape,
        out_specs=(VMEM,) * n_out,
        scratch_shapes=[
            pltpu.VMEM((sum(slots) * BLK, HD), BF16),
            pltpu.VMEM((sum(slots) * BLK, 2 * HD), BF16),
            pltpu.VMEM((tiles_here if one_block else 1, QW, HD), F32),
            pltpu.VMEM((tiles_here if one_block else 1, QW, 2 * HD), F32),
            pltpu.VMEM((n_q, rows, QW), BF16),
        ],
        compiler_params=pltpu.CompilerParams(
            vmem_limit_bytes=(24 if sum(slots) <= 16 else 56) * MIB
        ),
        cost_estimate=pl.CostEstimate(
            flops=8 * work * HD, transcendentals=work, bytes_accessed=4 * MIB
        ),
        name=name,
    )(sel, *[queries[k] for k in partners], *sources, *state)


def body(levels, subs, heads, queries, keys, values, selected):
    rows = queries.shape[0]
    tiles_here = selected.shape[0]
    level_blocks = subs * rows // BLK
    by_levels = levels == 4 and subs >= 4 and subs * rows % (2 * BLK) == 0

    def exchange(pieces, ks):
        return tuple(
            lax.ppermute(piece, "sub", [(i, i ^ k) for i in range(subs)]) if k else piece
            for k, piece in zip(ks, pieces)
        )

    everyone = tuple(range(subs))
    packed = pack_keys_values(subs, heads, keys, values)
    if by_levels:
        raw = lax.ppermute(packed, "lev", [(1, 3), (0, 1)])
    own = lax.all_to_all(packed, ("sub", "head"), 0, 0, tiled=True)
    q = pack_queries(subs, queries, selected)
    hop = subs // 2
    if hop > 1:
        over = exchange(q[hop:], [hop] * hop)
        q = exchange(q[:hop], range(hop)) + exchange(over, range(hop))
    else:
        q = exchange(q, everyone)
    if by_levels:
        half = own.shape[0] // 2
        halves = lax.optimization_barrier((own[:half], own[half:]))
        up = [lax.ppermute(piece, "lev", [(0, 2), (2, 3)]) for piece in halves]
        p2 = lax.all_to_all(raw, ("sub", "head"), 0, 0, tiled=True)
        q, _ = lax.optimization_barrier((q, up))
        sel = jnp.concatenate([piece[rows, : tiles_here * TOPK] for piece in q]).astype(jnp.int32)
        forwards = lax.axis_index("lev") == 2
        last_up = [
            lax.ppermute(jnp.where(forwards, a, b), "lev", [(2, 3), (1, 2)])
            for a, b in zip(up, halves)
        ]

        def at(level, *which):
            base = jnp.int32(NONE)
            for here, holds in which:
                base = jnp.where(level == here, holds * level_blocks, base)
            return base

        def in_halves(base):
            return (base, base + level_blocks // 2)

        def early(level):
            return (
                level * level_blocks,
                *in_halves(at(level, (2, 0), (3, 2))),
                at(level, (1, 0), (3, 1)),
            )

        def late(level):
            return in_halves(at(level, (2, 1), (3, 0)))

        def whole_range(level):
            return early(level) + late(level)

        far, near = everyone[subs // 2 :], everyone[: subs // 2]
        state = attention(
            "far_early", True, False, far, early, q, sel, (own, *up, p2), ()
        )
        out_far = ()
        for k in far:
            out_far += attention(
                "far_late", False, True, (k,), late, q, sel, tuple(last_up), state, far[0]
            )
        q_near, _ = lax.optimization_barrier((q[: subs // 2], out_far))
        q = tuple(q_near) + tuple(q[subs // 2 :])
        out_near = attention(
            "near", True, True, near, whole_range, q, sel, (own, *up, p2, *last_up), ()
        )
        out_near, out_far = exchange(out_near, near), exchange(out_far, far)
        begun = unpack_output("unpack_most", subs, (*out_far, out_near[0]), (*far, 0), ())
        return unpack_output("unpack_rest", subs, out_near[1:], near[1:], (begun,))
    sel = jnp.concatenate([piece[rows, : tiles_here * TOPK] for piece in q]).astype(jnp.int32)
    whole = lax.all_gather(own, "lev", axis=0, tiled=True)
    out = attention("all", True, True, everyone, lambda level: (0,), q, sel, (whole,), ())
    if subs == 1:
        return out[0]
    return unpack_output("unpack", subs, exchange(out, everyone), everyone, ())


def solution(mesh):
    ctx, heads = mesh.shape["ctx"], mesh.shape["head"]
    subs = math.gcd(KVH // heads, ctx)
    if subs * heads != KVH:
        raise ValueError("unsupported mesh")
    levels = ctx // subs
    split = Mesh(mesh.devices.reshape(levels, subs, heads), ("lev", "sub", "head"))
    placed = (
        P(("lev", "sub"), "head"),
        P(("lev", "sub", "head"), None),
        P(("lev", "sub", "head"), None),
        P(("lev", "sub"), "head", None),
    )
    return jax.shard_map(
        functools.partial(body, levels, subs, heads),
        mesh=split,
        in_specs=placed,
        out_specs=P(("lev", "sub"), "head"),
        check_vma=False,
    )
```

```python
import functools
import math

import jax
import jax.numpy as jnp
from jax import lax
from jax.experimental import pallas as pl
from jax.experimental.pallas import tpu as pltpu
from jax.sharding import Mesh, PartitionSpec as P

HD = 128
QH = 32
KVH = 8
BLK = 512
TILE = 128
TOPK = 3
PER = QH // KVH
QW = PER * HD
EXTRA = 16
TOGETHER = 2

FLOOR = -1e30
SCALE = HD ** -0.5 * math.log2(math.e)
NONE = -100000
F32 = jnp.float32
BF16 = jnp.bfloat16
VMEM = pl.BlockSpec(memory_space=pltpu.VMEM)
SMEM = pl.BlockSpec(memory_space=pltpu.SMEM)
ANY = pl.BlockSpec(memory_space=pl.ANY)
MIB = 1024 * 1024


def dot_nt(a, b):
    return lax.dot_general(a, b, (((1,), (1,)), ((), ())), preferred_element_type=F32)


def dot_nn(a, b):
    return lax.dot_general(a, b, (((1,), (0,)), ((), ())), preferred_element_type=F32)


def copy_cost(bytes_moved):
    return pl.CostEstimate(flops=0, transcendentals=0, bytes_accessed=bytes_moved)


def pack_keys_values(subs, heads, keys, values):
    r = keys.shape[0]

    def kernel(k_ref, v_ref, out_ref):
        for sub in range(subs):
            for head in range(heads):
                at = (head * subs + sub) * HD
                out_ref[sub * heads + head, 0] = k_ref[:, at : at + HD]
                out_ref[sub * heads + head, 1] = v_ref[:, at : at + HD]

    return pl.pallas_call(
        kernel,
        in_specs=[VMEM, VMEM],
        out_specs=VMEM,
        out_shape=jax.ShapeDtypeStruct((subs * heads, 2, r, HD), BF16),
        cost_estimate=copy_cost(4 * keys.size * 2),
        name="pack_kv",
    )(keys, values)


def pack_queries(subs, queries, selected):
    rows = queries.shape[0]
    tiles_here = selected.shape[0]

    def kernel(sel_ref, q_ref, *outs):
        sub = lax.axis_index("sub") if subs > 1 else 0
        lane = lax.broadcasted_iota(jnp.int32, (EXTRA, QW), 1)
        for k, out_ref in enumerate(outs):
            head = sub ^ k
            out_ref[:rows] = q_ref[:, pl.ds(pl.multiple_of(head * QW, QW), QW)]
            row = jnp.zeros((EXTRA, QW), jnp.int32)
            for t in range(tiles_here):
                for e in range(TOPK):
                    row = jnp.where(lane == t * TOPK + e, sel_ref[t, head, e], row)
            out_ref[rows:] = row.astype(F32).astype(BF16)

    return pl.pallas_call(
        kernel,
        in_specs=[SMEM, VMEM],
        out_specs=(VMEM,) * subs,
        out_shape=(jax.ShapeDtypeStruct((rows + EXTRA, QW), BF16),) * subs,
        cost_estimate=copy_cost(2 * queries.size * 2),
        compiler_params=pltpu.CompilerParams(vmem_limit_bytes=8 * MIB),
        name="pack_q",
    )(selected, queries)


def unpack_output(name, subs, pieces, ks, begun):
    rows = pieces[0].shape[0]
    n = len(pieces)

    def kernel(*refs):
        out_ref, sems = refs[-2:]
        sub = lax.axis_index("sub")
        copies = []
        for i, k in enumerate(ks):
            at = pl.ds(pl.multiple_of((sub ^ k) * QW, QW), QW)
            copies.append(pltpu.make_async_copy(refs[i], out_ref.at[:, at], sems.at[i]))
        for copy in copies:
            copy.start()
        for copy in copies:
            copy.wait()

    return pl.pallas_call(
        kernel,
        in_specs=[VMEM] * n + [ANY] * len(begun),
        out_specs=ANY,
        out_shape=jax.ShapeDtypeStruct((rows, subs * QW), BF16),
        scratch_shapes=[pltpu.SemaphoreType.DMA((n,))],
        input_output_aliases={n: 0} if begun else {},
        cost_estimate=copy_cost(4 * n * rows * QW),
        compiler_params=pltpu.CompilerParams(vmem_limit_bytes=8 * MIB),
        name=name,
    )(*pieces, *begun)


def attention(
    name, first, last, partners, bases_of, queries, sel, sources, state, state_from=0
):
    parts, rows = len(queries), queries[0].shape[0] - EXTRA
    tiles_in_part = rows // TILE
    tiles_here = len(partners) * tiles_in_part
    r = sources[0].shape[2]
    per_block = BLK // r
    n_src = len(sources)
    slots = [src.shape[0] // per_block for src in sources]
    most = min(TOPK, sum(slots))
    n_q = len(partners)
    n_out = len(partners) if last else 2
    in_block = BLK // TILE
    one_block = parts > 1 and len(partners) * rows == BLK

    def kernel(*refs):
        sel_ref, q_refs = refs[0], refs[1 : 1 + n_q]
        src = refs[1 + n_q : 1 + n_q + n_src]
        rest = refs[1 + n_q + n_src :]
        m_in, acc_in = (None, None) if first else rest[:2]
        rest = rest if first else rest[2:]
        outs, k_buf, v_buf, m_tmp, acc_tmp, q_buf = rest[:n_out], *rest[n_out:]
        level = lax.axis_index("lev")
        sub = lax.axis_index("sub") if parts > 1 else 0
        for i, q_ref in enumerate(q_refs):
            q_buf[i] = q_ref[:rows]
        bases = bases_of(level)

        v_buf[:, HD:] = jnp.ones((sum(slots) * BLK, HD), BF16)
        start = 0
        for ref, base, n in zip(src, bases, slots):

            def fill(ref=ref, start=start, n=n):
                if n * per_block <= 8:
                    k_buf[start * BLK : (start + n) * BLK] = ref[:, 0].reshape(n * BLK, HD)
                    v_buf[start * BLK : (start + n) * BLK, :HD] = ref[:, 1].reshape(n * BLK, HD)
                else:

                    def chunk(i, carry):
                        at = pl.ds(pl.multiple_of(start * BLK + i * r, r), r)
                        k_buf[at] = ref[i, 0]
                        v_buf[at, :HD] = ref[i, 1]
                        return carry

                    lax.fori_loop(0, n * per_block, chunk, 0)

            if isinstance(base, int):
                fill()
            else:
                pl.when(base >= 0)(fill)
            start += n

        def own_part(t, part, at, slot, own, pieces):
            count = pieces * TILE
            keys_at = pl.ds(pl.multiple_of((own - bases[0]) * BLK, BLK), count)
            q_rows = pl.ds(pl.multiple_of(at, TILE), TILE)
            together = PER if pieces <= 2 else TOGETHER
            edge_shape = (together * TILE, TILE)
            key_at = lax.broadcasted_iota(jnp.int32, edge_shape, 1)
            query_at = lax.broadcasted_iota(jnp.int32, edge_shape, 0) & (TILE - 1)

            def scores(c):
                heads = range(c * together, (c + 1) * together)
                q = [q_buf[part, q_rows, j * HD : (j + 1) * HD] for j in heads]
                s = dot_nt(jnp.concatenate(q, axis=0), k_buf[keys_at])
                edge = jnp.where(key_at <= query_at, s[:, count - TILE :], FLOOR)
                if pieces == 1:
                    return edge
                return jnp.concatenate([s[:, : count - TILE], edge], axis=1)

            ready = [scores(c) for c in range(PER // together)]
            for c, s in enumerate(ready):
                here = slice(c * together * TILE, (c + 1) * together * TILE)
                m = jnp.max(s, axis=1, keepdims=True)
                p = jnp.exp2((s - m) * SCALE).astype(BF16)
                m_tmp[slot, here] = jnp.broadcast_to(m, (together * TILE, HD))
                acc_tmp[slot, here] = dot_nn(p, v_buf[keys_at])

        if first and one_block:
            first_part = level * parts
            own = (first_part + (sub ^ partners[0])) * tiles_in_part // in_block
            for i in range(in_block):
                part = own * (in_block // tiles_in_part) + i // tiles_in_part - first_part
                local = (part ^ sub) - partners[0]
                t = local * tiles_in_part + i % tiles_in_part
                own_part(t, local, i % tiles_in_part * TILE, t, own, i + 1)

        def one_tile(k, part, i, out_ref, out_at):
            t = part * tiles_in_part + i
            tile = (level * parts + (sub ^ k)) * tiles_in_part + i
            own = tile // in_block
            q_rows = pl.ds(pl.multiple_of(i * TILE, TILE), TILE)
            if first:
                m_old, acc_old, at_old = m_tmp, acc_tmp, t if one_block else 0
            else:
                m_old, acc_old, at_old = m_in, acc_in, t + (partners[0] - state_from) * tiles_in_part

            def finish(j, acc):
                out_ref[out_at, j * HD : (j + 1) * HD] = (acc[:, :HD] / acc[:, HD:]).astype(BF16)

            def keep(j, m, acc):
                outs[0][t, j * TILE : (j + 1) * TILE] = m
                outs[1][t, j * TILE : (j + 1) * TILE] = acc

            if first and not one_block:
                for pieces in range(1, in_block + 1):
                    pl.when(lax.rem(tile, in_block) == pieces - 1)(
                        functools.partial(own_part, t, part, i * TILE, 0, own, pieces)
                    )

            found = jnp.int32(0)
            where = [jnp.int32(0)] * most
            for e in range(TOPK):
                block = sel_ref[(k * tiles_in_part + i) * TOPK + e]
                start = 0
                for base, n in zip(bases, slots):
                    hit = (block != own) & (block >= base) & (block < base + n)
                    where = [
                        jnp.where(hit & (found == i), start + block - base, w)
                        for i, w in enumerate(where)
                    ]
                    found = found + hit.astype(jnp.int32)
                    start += n

            def others(n):
                at = [pl.ds(pl.multiple_of(w * BLK, BLK), BLK) for w in where[:n]]

                def scores(c):
                    heads = range(c * TOGETHER, (c + 1) * TOGETHER)
                    q = [q_buf[part, q_rows, j * HD : (j + 1) * HD] for j in heads]
                    q = jnp.concatenate(q, axis=0)
                    s = [dot_nt(q, k_buf[a]) for a in at]
                    return jnp.concatenate(s, axis=1) if n > 1 else s[0]

                chains = range(PER // TOGETHER)
                ready = [scores(c) for c in chains] if n else None
                for c in chains:
                    here = slice(c * TOGETHER * TILE, (c + 1) * TOGETHER * TILE)
                    m = m_old[at_old, here]
                    acc = acc_old[at_old, here]
                    if n:
                        old, s = m, ready[c]
                        m = jnp.maximum(old, jnp.max(s, axis=1, keepdims=True))
                        p = jnp.exp2((s - jnp.tile(m, (1, n * BLK // HD))) * SCALE).astype(BF16)
                        acc = acc * jnp.tile(jnp.exp2((old - m) * SCALE), (1, 2))
                        for i, a in enumerate(at):
                            acc = acc + dot_nn(p[:, i * BLK : (i + 1) * BLK], v_buf[a])
                    for i in range(TOGETHER):
                        j, rows_of = c * TOGETHER + i, slice(i * TILE, (i + 1) * TILE)
                        if last:
                            finish(j, acc[rows_of])
                        else:
                            keep(j, m[rows_of], acc[rows_of])

            for n in range(most + 1):
                pl.when(found == n)(functools.partial(others, n))

        if last:
            for part, (out_ref, k) in enumerate(zip(outs, partners)):

                def step(i, carry, out_ref=out_ref, k=k, part=part):
                    out_at = pl.ds(pl.multiple_of(i * TILE, TILE), TILE)
                    one_tile(k, part, i, out_ref, out_at)
                    return carry

                lax.fori_loop(0, tiles_in_part, step, 0)
        else:

            def step(t, carry):
                part = t // tiles_in_part
                one_tile(partners[0] + part, part, lax.rem(t, tiles_in_part), None, None)
                return carry

            lax.fori_loop(0, tiles_here, step, 0)

    if last:
        out_shape = tuple(jax.ShapeDtypeStruct((rows, QW), BF16) for _ in partners)
    else:
        out_shape = (
            jax.ShapeDtypeStruct((tiles_here, QW, HD), F32),
            jax.ShapeDtypeStruct((tiles_here, QW, 2 * HD), F32),
        )
    work = tiles_here * QW * BLK * 3 // 2
    return pl.pallas_call(
        kernel,
        in_specs=[SMEM] + [VMEM] * (n_q + n_src + len(state)),
        out_shape=out_shape,
        out_specs=(VMEM,) * n_out,
        scratch_shapes=[
            pltpu.VMEM((sum(slots) * BLK, HD), BF16),
            pltpu.VMEM((sum(slots) * BLK, 2 * HD), BF16),
            pltpu.VMEM((tiles_here if one_block else 1, QW, HD), F32),
            pltpu.VMEM((tiles_here if one_block else 1, QW, 2 * HD), F32),
            pltpu.VMEM((n_q, rows, QW), BF16),
        ],
        compiler_params=pltpu.CompilerParams(
            vmem_limit_bytes=(24 if sum(slots) <= 16 else 56) * MIB
        ),
        cost_estimate=pl.CostEstimate(
            flops=8 * work * HD, transcendentals=work, bytes_accessed=4 * MIB
        ),
        name=name,
    )(sel, *[queries[k] for k in partners], *sources, *state)


def body(levels, subs, heads, queries, keys, values, selected):
    rows = queries.shape[0]
    tiles_here = selected.shape[0]
    level_blocks = subs * rows // BLK
    by_levels = levels == 4 and subs >= 4 and subs * rows % (2 * BLK) == 0

    def exchange(pieces, ks):
        return tuple(
            lax.ppermute(piece, "sub", [(i, i ^ k) for i in range(subs)]) if k else piece
            for k, piece in zip(ks, pieces)
        )

    everyone = tuple(range(subs))
    packed = pack_keys_values(subs, heads, keys, values)
    if by_levels:
        raw = lax.ppermute(packed, "lev", [(1, 3), (0, 1)])
    own = lax.all_to_all(packed, ("sub", "head"), 0, 0, tiled=True)
    q = pack_queries(subs, queries, selected)
    hop = subs // 2
    if hop > 1:
        over = exchange(q[hop:], [hop] * hop)
        q = exchange(q[:hop], range(hop)) + exchange(over, range(hop))
    else:
        q = exchange(q, everyone)
    if by_levels:
        own, raw = lax.optimization_barrier((own, raw))
        half = own.shape[0] // 2
        halves = lax.optimization_barrier((own[:half], own[half:]))
        up = [lax.ppermute(piece, "lev", [(0, 2), (2, 3)]) for piece in halves]
        p2 = lax.all_to_all(raw, ("sub", "head"), 0, 0, tiled=True)
        q, _ = lax.optimization_barrier((q, up))
        sel = jnp.concatenate([piece[rows, : tiles_here * TOPK] for piece in q]).astype(jnp.int32)
        forwards = lax.axis_index("lev") == 2
        last_up = [
            lax.ppermute(jnp.where(forwards, a, b), "lev", [(2, 3), (1, 2)])
            for a, b in zip(up, halves)
        ]

        def at(level, *which):
            base = jnp.int32(NONE)
            for here, holds in which:
                base = jnp.where(level == here, holds * level_blocks, base)
            return base

        def in_halves(base):
            return (base, base + level_blocks // 2)

        def early(level):
            return (
                level * level_blocks,
                *in_halves(at(level, (2, 0), (3, 2))),
                at(level, (1, 0), (3, 1)),
            )

        def late(level):
            return in_halves(at(level, (2, 1), (3, 0)))

        def whole_range(level):
            return early(level) + late(level)

        far, near = everyone[subs // 2 :], everyone[: subs // 2]
        state = attention(
            "far_early", True, False, far, early, q, sel, (own, *up, p2), ()
        )
        out_far = ()
        for k in far:
            out_far += attention(
                "far_late", False, True, (k,), late, q, sel, tuple(last_up), state, far[0]
            )
        q_near, _ = lax.optimization_barrier((q[: subs // 2], out_far))
        q = tuple(q_near) + tuple(q[subs // 2 :])
        out_near = attention(
            "near", True, True, near, whole_range, q, sel, (own, *up, p2, *last_up), ()
        )
        out_near, out_far = exchange(out_near, near), exchange(out_far, far)
        begun = unpack_output("unpack_most", subs, (*out_far, out_near[0]), (*far, 0), ())
        return unpack_output("unpack_rest", subs, out_near[1:], near[1:], (begun,))
    sel = jnp.concatenate([piece[rows, : tiles_here * TOPK] for piece in q]).astype(jnp.int32)
    whole = lax.all_gather(own, "lev", axis=0, tiled=True)
    out = attention("all", True, True, everyone, lambda level: (0,), q, sel, (whole,), ())
    if subs == 1:
        return out[0]
    return unpack_output("unpack", subs, exchange(out, everyone), everyone, ())


def solution(mesh):
    ctx, heads = mesh.shape["ctx"], mesh.shape["head"]
    subs = math.gcd(KVH // heads, ctx)
    if subs * heads != KVH:
        raise ValueError("unsupported mesh")
    levels = ctx // subs
    split = Mesh(mesh.devices.reshape(levels, subs, heads), ("lev", "sub", "head"))
    placed = (
        P(("lev", "sub"), "head"),
        P(("lev", "sub", "head"), None),
        P(("lev", "sub", "head"), None),
        P(("lev", "sub"), "head", None),
    )
    return jax.shard_map(
        functools.partial(body, levels, subs, heads),
        mesh=split,
        in_specs=placed,
        out_specs=P(("lev", "sub"), "head"),
        check_vma=False,
    )
```

```python
import functools
import math

import jax
import jax.numpy as jnp
from jax import lax
from jax.experimental import pallas as pl
from jax.experimental.pallas import tpu as pltpu
from jax.sharding import Mesh, PartitionSpec as P

HD = 128
QH = 32
KVH = 8
BLK = 512
TILE = 128
TOPK = 3
PER = QH // KVH
QW = PER * HD
EXTRA = 16
TOGETHER = 2

FLOOR = -1e30
SCALE = HD ** -0.5 * math.log2(math.e)
NONE = -100000
F32 = jnp.float32
BF16 = jnp.bfloat16
VMEM = pl.BlockSpec(memory_space=pltpu.VMEM)
SMEM = pl.BlockSpec(memory_space=pltpu.SMEM)
ANY = pl.BlockSpec(memory_space=pl.ANY)
MIB = 1024 * 1024


def dot_nt(a, b):
    return lax.dot_general(a, b, (((1,), (1,)), ((), ())), preferred_element_type=F32)


def dot_nn(a, b):
    return lax.dot_general(a, b, (((1,), (0,)), ((), ())), preferred_element_type=F32)


def copy_cost(bytes_moved):
    return pl.CostEstimate(flops=0, transcendentals=0, bytes_accessed=bytes_moved)


def pack_keys_values(subs, heads, keys, values):
    r = keys.shape[0]

    def kernel(k_ref, v_ref, out_ref):
        for sub in range(subs):
            for head in range(heads):
                at = (head * subs + sub) * HD
                out_ref[sub * heads + head, 0] = k_ref[:, at : at + HD]
                out_ref[sub * heads + head, 1] = v_ref[:, at : at + HD]

    return pl.pallas_call(
        kernel,
        in_specs=[VMEM, VMEM],
        out_specs=VMEM,
        out_shape=jax.ShapeDtypeStruct((subs * heads, 2, r, HD), BF16),
        cost_estimate=copy_cost(4 * keys.size * 2),
        name="pack_kv",
    )(keys, values)


def pack_queries(subs, queries, selected):
    rows = queries.shape[0]
    tiles_here = selected.shape[0]

    def kernel(sel_ref, q_ref, *outs):
        sub = lax.axis_index("sub") if subs > 1 else 0
        lane = lax.broadcasted_iota(jnp.int32, (EXTRA, QW), 1)
        for k, out_ref in enumerate(outs):
            head = sub ^ k
            out_ref[:rows] = q_ref[:, pl.ds(pl.multiple_of(head * QW, QW), QW)]
            row = jnp.zeros((EXTRA, QW), jnp.int32)
            for t in range(tiles_here):
                for e in range(TOPK):
                    row = jnp.where(lane == t * TOPK + e, sel_ref[t, head, e], row)
            out_ref[rows:] = row.astype(F32).astype(BF16)

    return pl.pallas_call(
        kernel,
        in_specs=[SMEM, VMEM],
        out_specs=(VMEM,) * subs,
        out_shape=(jax.ShapeDtypeStruct((rows + EXTRA, QW), BF16),) * subs,
        cost_estimate=copy_cost(2 * queries.size * 2),
        compiler_params=pltpu.CompilerParams(vmem_limit_bytes=8 * MIB),
        name="pack_q",
    )(selected, queries)


def unpack_output(name, subs, pieces, ks, begun):
    rows = pieces[0].shape[0]
    n = len(pieces)

    def kernel(*refs):
        out_ref, sems = refs[-2:]
        sub = lax.axis_index("sub")
        copies = []
        for i, k in enumerate(ks):
            at = pl.ds(pl.multiple_of((sub ^ k) * QW, QW), QW)
            copies.append(pltpu.make_async_copy(refs[i], out_ref.at[:, at], sems.at[i]))
        for copy in copies:
            copy.start()
        for copy in copies:
            copy.wait()

    return pl.pallas_call(
        kernel,
        in_specs=[VMEM] * n + [ANY] * len(begun),
        out_specs=ANY,
        out_shape=jax.ShapeDtypeStruct((rows, subs * QW), BF16),
        scratch_shapes=[pltpu.SemaphoreType.DMA((n,))],
        input_output_aliases={n: 0} if begun else {},
        cost_estimate=copy_cost(4 * n * rows * QW),
        compiler_params=pltpu.CompilerParams(vmem_limit_bytes=8 * MIB),
        name=name,
    )(*pieces, *begun)


def in_place(*pieces):
    n = len(pieces)

    def kernel(*refs):
        pass

    return pl.pallas_call(
        kernel,
        in_specs=[ANY] * n,
        out_specs=(ANY,) * n,
        out_shape=tuple(jax.ShapeDtypeStruct(piece.shape, piece.dtype) for piece in pieces),
        input_output_aliases={i: i for i in range(n)},
        cost_estimate=copy_cost(4 * n * pieces[0].size),
        compiler_params=pltpu.CompilerParams(vmem_limit_bytes=8 * MIB),
        name="landed",
    )(*pieces)


def attention(
    name, first, last, partners, bases_of, queries, sel, sources, state, state_from=0
):
    parts, rows = len(queries), queries[0].shape[0] - EXTRA
    tiles_in_part = rows // TILE
    tiles_here = len(partners) * tiles_in_part
    r = sources[0].shape[2]
    per_block = BLK // r
    n_src = len(sources)
    slots = [src.shape[0] // per_block for src in sources]
    most = min(TOPK, sum(slots))
    n_q = len(partners)
    n_out = len(partners) if last else 2
    in_block = BLK // TILE
    one_block = parts > 1 and len(partners) * rows == BLK

    def kernel(*refs):
        sel_ref, q_refs = refs[0], refs[1 : 1 + n_q]
        src = refs[1 + n_q : 1 + n_q + n_src]
        rest = refs[1 + n_q + n_src :]
        m_in, acc_in = (None, None) if first else rest[:2]
        rest = rest if first else rest[2:]
        outs, k_buf, v_buf, m_tmp, acc_tmp, q_buf = rest[:n_out], *rest[n_out:]
        level = lax.axis_index("lev")
        sub = lax.axis_index("sub") if parts > 1 else 0
        for i, q_ref in enumerate(q_refs):
            q_buf[i] = q_ref[:rows]
        bases = bases_of(level)

        v_buf[:, HD:] = jnp.ones((sum(slots) * BLK, HD), BF16)
        start = 0
        for ref, base, n in zip(src, bases, slots):

            def fill(ref=ref, start=start, n=n):
                if n * per_block <= 8:
                    k_buf[start * BLK : (start + n) * BLK] = ref[:, 0].reshape(n * BLK, HD)
                    v_buf[start * BLK : (start + n) * BLK, :HD] = ref[:, 1].reshape(n * BLK, HD)
                else:

                    def chunk(i, carry):
                        at = pl.ds(pl.multiple_of(start * BLK + i * r, r), r)
                        k_buf[at] = ref[i, 0]
                        v_buf[at, :HD] = ref[i, 1]
                        return carry

                    lax.fori_loop(0, n * per_block, chunk, 0)

            if isinstance(base, int):
                fill()
            else:
                pl.when(base >= 0)(fill)
            start += n

        def own_part(t, part, at, slot, own, pieces):
            count = pieces * TILE
            keys_at = pl.ds(pl.multiple_of((own - bases[0]) * BLK, BLK), count)
            q_rows = pl.ds(pl.multiple_of(at, TILE), TILE)
            together = PER if pieces <= 2 else TOGETHER
            edge_shape = (together * TILE, TILE)
            key_at = lax.broadcasted_iota(jnp.int32, edge_shape, 1)
            query_at = lax.broadcasted_iota(jnp.int32, edge_shape, 0) & (TILE - 1)

            def scores(c):
                heads = range(c * together, (c + 1) * together)
                q = [q_buf[part, q_rows, j * HD : (j + 1) * HD] for j in heads]
                s = dot_nt(jnp.concatenate(q, axis=0), k_buf[keys_at])
                edge = jnp.where(key_at <= query_at, s[:, count - TILE :], FLOOR)
                if pieces == 1:
                    return edge
                return jnp.concatenate([s[:, : count - TILE], edge], axis=1)

            ready = [scores(c) for c in range(PER // together)]
            for c, s in enumerate(ready):
                here = slice(c * together * TILE, (c + 1) * together * TILE)
                m = jnp.max(s, axis=1, keepdims=True)
                p = jnp.exp2((s - m) * SCALE).astype(BF16)
                m_tmp[slot, here] = jnp.broadcast_to(m, (together * TILE, HD))
                acc_tmp[slot, here] = dot_nn(p, v_buf[keys_at])

        if first and one_block:
            first_part = level * parts
            own = (first_part + (sub ^ partners[0])) * tiles_in_part // in_block
            for i in range(in_block):
                part = own * (in_block // tiles_in_part) + i // tiles_in_part - first_part
                local = (part ^ sub) - partners[0]
                t = local * tiles_in_part + i % tiles_in_part
                own_part(t, local, i % tiles_in_part * TILE, t, own, i + 1)

        def one_tile(k, part, i, out_ref, out_at):
            t = part * tiles_in_part + i
            tile = (level * parts + (sub ^ k)) * tiles_in_part + i
            own = tile // in_block
            q_rows = pl.ds(pl.multiple_of(i * TILE, TILE), TILE)
            if first:
                m_old, acc_old, at_old = m_tmp, acc_tmp, t if one_block else 0
            else:
                m_old, acc_old, at_old = m_in, acc_in, t + (partners[0] - state_from) * tiles_in_part

            def finish(j, acc):
                out_ref[out_at, j * HD : (j + 1) * HD] = (acc[:, :HD] / acc[:, HD:]).astype(BF16)

            def keep(j, m, acc):
                outs[0][t, j * TILE : (j + 1) * TILE] = m
                outs[1][t, j * TILE : (j + 1) * TILE] = acc

            if first and not one_block:
                for pieces in range(1, in_block + 1):
                    pl.when(lax.rem(tile, in_block) == pieces - 1)(
                        functools.partial(own_part, t, part, i * TILE, 0, own, pieces)
                    )

            found = jnp.int32(0)
            where = [jnp.int32(0)] * most
            for e in range(TOPK):
                block = sel_ref[(k * tiles_in_part + i) * TOPK + e]
                start = 0
                for base, n in zip(bases, slots):
                    hit = (block != own) & (block >= base) & (block < base + n)
                    where = [
                        jnp.where(hit & (found == i), start + block - base, w)
                        for i, w in enumerate(where)
                    ]
                    found = found + hit.astype(jnp.int32)
                    start += n

            def others(n):
                at = [pl.ds(pl.multiple_of(w * BLK, BLK), BLK) for w in where[:n]]

                def scores(c):
                    heads = range(c * TOGETHER, (c + 1) * TOGETHER)
                    q = [q_buf[part, q_rows, j * HD : (j + 1) * HD] for j in heads]
                    q = jnp.concatenate(q, axis=0)
                    s = [dot_nt(q, k_buf[a]) for a in at]
                    return jnp.concatenate(s, axis=1) if n > 1 else s[0]

                chains = range(PER // TOGETHER)
                ready = [scores(c) for c in chains] if n else None
                for c in chains:
                    here = slice(c * TOGETHER * TILE, (c + 1) * TOGETHER * TILE)
                    m = m_old[at_old, here]
                    acc = acc_old[at_old, here]
                    if n:
                        old, s = m, ready[c]
                        m = jnp.maximum(old, jnp.max(s, axis=1, keepdims=True))
                        p = jnp.exp2((s - jnp.tile(m, (1, n * BLK // HD))) * SCALE).astype(BF16)
                        acc = acc * jnp.tile(jnp.exp2((old - m) * SCALE), (1, 2))
                        for i, a in enumerate(at):
                            acc = acc + dot_nn(p[:, i * BLK : (i + 1) * BLK], v_buf[a])
                    for i in range(TOGETHER):
                        j, rows_of = c * TOGETHER + i, slice(i * TILE, (i + 1) * TILE)
                        if last:
                            finish(j, acc[rows_of])
                        else:
                            keep(j, m[rows_of], acc[rows_of])

            for n in range(most + 1):
                pl.when(found == n)(functools.partial(others, n))

        if last:
            for part, (out_ref, k) in enumerate(zip(outs, partners)):

                def step(i, carry, out_ref=out_ref, k=k, part=part):
                    out_at = pl.ds(pl.multiple_of(i * TILE, TILE), TILE)
                    one_tile(k, part, i, out_ref, out_at)
                    return carry

                lax.fori_loop(0, tiles_in_part, step, 0)
        else:

            def step(t, carry):
                part = t // tiles_in_part
                one_tile(partners[0] + part, part, lax.rem(t, tiles_in_part), None, None)
                return carry

            lax.fori_loop(0, tiles_here, step, 0)

    if last:
        out_shape = tuple(jax.ShapeDtypeStruct((rows, QW), BF16) for _ in partners)
    else:
        out_shape = (
            jax.ShapeDtypeStruct((tiles_here, QW, HD), F32),
            jax.ShapeDtypeStruct((tiles_here, QW, 2 * HD), F32),
        )
    work = tiles_here * QW * BLK * 3 // 2
    return pl.pallas_call(
        kernel,
        in_specs=[SMEM] + [VMEM] * (n_q + n_src + len(state)),
        out_shape=out_shape,
        out_specs=(VMEM,) * n_out,
        scratch_shapes=[
            pltpu.VMEM((sum(slots) * BLK, HD), BF16),
            pltpu.VMEM((sum(slots) * BLK, 2 * HD), BF16),
            pltpu.VMEM((tiles_here if one_block else 1, QW, HD), F32),
            pltpu.VMEM((tiles_here if one_block else 1, QW, 2 * HD), F32),
            pltpu.VMEM((n_q, rows, QW), BF16),
        ],
        compiler_params=pltpu.CompilerParams(
            vmem_limit_bytes=(24 if sum(slots) <= 16 else 56) * MIB
        ),
        cost_estimate=pl.CostEstimate(
            flops=8 * work * HD, transcendentals=work, bytes_accessed=4 * MIB
        ),
        name=name,
    )(sel, *[queries[k] for k in partners], *sources, *state)


def body(levels, subs, heads, queries, keys, values, selected):
    rows = queries.shape[0]
    tiles_here = selected.shape[0]
    level_blocks = subs * rows // BLK
    by_levels = levels == 4 and subs >= 4 and subs * rows % (2 * BLK) == 0

    def exchange(pieces, ks):
        return tuple(
            lax.ppermute(piece, "sub", [(i, i ^ k) for i in range(subs)]) if k else piece
            for k, piece in zip(ks, pieces)
        )

    everyone = tuple(range(subs))
    packed = pack_keys_values(subs, heads, keys, values)
    if by_levels:
        raw = lax.ppermute(packed, "lev", [(1, 3), (0, 1)])
    own = lax.all_to_all(packed, ("sub", "head"), 0, 0, tiled=True)
    q = pack_queries(subs, queries, selected)
    hop = subs // 2
    if hop > 1:
        over = exchange(q[hop:], [hop] * hop)
        q = exchange(q[:hop], range(hop)) + exchange(over, range(hop))
    else:
        q = exchange(q, everyone)
    if by_levels:
        own, raw = lax.optimization_barrier((own, raw))
        half = own.shape[0] // 2
        halves = lax.optimization_barrier((own[:half], own[half:]))
        up = [lax.ppermute(piece, "lev", [(0, 2), (2, 3)]) for piece in halves]
        p2 = lax.all_to_all(raw, ("sub", "head"), 0, 0, tiled=True)
        q, _ = lax.optimization_barrier((q, up))
        sel = jnp.concatenate([piece[rows, : tiles_here * TOPK] for piece in q]).astype(jnp.int32)
        forwards = lax.axis_index("lev") == 2
        last_up = [
            lax.ppermute(jnp.where(forwards, a, b), "lev", [(2, 3), (1, 2)])
            for a, b in zip(up, halves)
        ]

        def at(level, *which):
            base = jnp.int32(NONE)
            for here, holds in which:
                base = jnp.where(level == here, holds * level_blocks, base)
            return base

        def in_halves(base):
            return (base, base + level_blocks // 2)

        def early(level):
            return (
                level * level_blocks,
                *in_halves(at(level, (2, 0), (3, 2))),
                at(level, (1, 0), (3, 1)),
            )

        def late(level):
            return in_halves(at(level, (2, 1), (3, 0)))

        def whole_range(level):
            return early(level) + late(level)

        far, near = everyone[subs // 2 :], everyone[: subs // 2]
        state = attention(
            "far_early", True, False, far, early, q, sel, (own, *up, p2), ()
        )
        out_far = ()
        for k in far:
            out_far += attention(
                "far_late", False, True, (k,), late, q, sel, tuple(last_up), state, far[0]
            )
        q_near, _ = lax.optimization_barrier((q[: subs // 2], out_far))
        q = tuple(q_near) + tuple(q[subs // 2 :])
        out_near = attention(
            "near", True, True, near, whole_range, q, sel, (own, *up, p2, *last_up), ()
        )
        out_near, out_far = exchange(out_near, near), exchange(out_far, far)
        landed = in_place(*out_far)
        return unpack_output("unpack", subs, (*landed, *out_near), (*far, *near), ())
    sel = jnp.concatenate([piece[rows, : tiles_here * TOPK] for piece in q]).astype(jnp.int32)
    whole = lax.all_gather(own, "lev", axis=0, tiled=True)
    out = attention("all", True, True, everyone, lambda level: (0,), q, sel, (whole,), ())
    if subs == 1:
        return out[0]
    return unpack_output("unpack", subs, exchange(out, everyone), everyone, ())


def solution(mesh):
    ctx, heads = mesh.shape["ctx"], mesh.shape["head"]
    subs = math.gcd(KVH // heads, ctx)
    if subs * heads != KVH:
        raise ValueError("unsupported mesh")
    levels = ctx // subs
    split = Mesh(mesh.devices.reshape(levels, subs, heads), ("lev", "sub", "head"))
    placed = (
        P(("lev", "sub"), "head"),
        P(("lev", "sub", "head"), None),
        P(("lev", "sub", "head"), None),
        P(("lev", "sub"), "head", None),
    )
    return jax.shard_map(
        functools.partial(body, levels, subs, heads),
        mesh=split,
        in_specs=placed,
        out_specs=P(("lev", "sub"), "head"),
        check_vma=False,
    )
```

```python
import functools
import math

import jax
import jax.numpy as jnp
from jax import lax
from jax.experimental import pallas as pl
from jax.experimental.pallas import tpu as pltpu
from jax.sharding import Mesh, PartitionSpec as P

HD = 128
QH = 32
KVH = 8
BLK = 512
TILE = 128
TOPK = 3
PER = QH // KVH
QW = PER * HD
EXTRA = 16
TOGETHER = 2

FLOOR = -1e30
SCALE = HD ** -0.5 * math.log2(math.e)
NONE = -100000
F32 = jnp.float32
BF16 = jnp.bfloat16
VMEM = pl.BlockSpec(memory_space=pltpu.VMEM)
SMEM = pl.BlockSpec(memory_space=pltpu.SMEM)
ANY = pl.BlockSpec(memory_space=pl.ANY)
MIB = 1024 * 1024


def dot_nt(a, b):
    return lax.dot_general(a, b, (((1,), (1,)), ((), ())), preferred_element_type=F32)


def dot_nn(a, b):
    return lax.dot_general(a, b, (((1,), (0,)), ((), ())), preferred_element_type=F32)


def copy_cost(bytes_moved):
    return pl.CostEstimate(flops=0, transcendentals=0, bytes_accessed=bytes_moved)


def pack_keys_values(subs, heads, keys, values):
    r = keys.shape[0]

    def kernel(k_ref, v_ref, out_ref):
        for sub in range(subs):
            for head in range(heads):
                at = (head * subs + sub) * HD
                out_ref[sub * heads + head, 0] = k_ref[:, at : at + HD]
                out_ref[sub * heads + head, 1] = v_ref[:, at : at + HD]

    return pl.pallas_call(
        kernel,
        in_specs=[VMEM, VMEM],
        out_specs=VMEM,
        out_shape=jax.ShapeDtypeStruct((subs * heads, 2, r, HD), BF16),
        cost_estimate=copy_cost(4 * keys.size * 2),
        name="pack_kv",
    )(keys, values)


def pack_queries(subs, queries, selected):
    rows = queries.shape[0]
    tiles_here = selected.shape[0]

    def kernel(sel_ref, q_ref, *outs):
        sub = lax.axis_index("sub") if subs > 1 else 0
        lane = lax.broadcasted_iota(jnp.int32, (EXTRA, QW), 1)
        for k, out_ref in enumerate(outs):
            head = sub ^ k
            out_ref[:rows] = q_ref[:, pl.ds(pl.multiple_of(head * QW, QW), QW)]
            row = jnp.zeros((EXTRA, QW), jnp.int32)
            for t in range(tiles_here):
                for e in range(TOPK):
                    row = jnp.where(lane == t * TOPK + e, sel_ref[t, head, e], row)
            out_ref[rows:] = row.astype(F32).astype(BF16)

    return pl.pallas_call(
        kernel,
        in_specs=[SMEM, VMEM],
        out_specs=(VMEM,) * subs,
        out_shape=(jax.ShapeDtypeStruct((rows + EXTRA, QW), BF16),) * subs,
        cost_estimate=copy_cost(2 * queries.size * 2),
        compiler_params=pltpu.CompilerParams(vmem_limit_bytes=8 * MIB),
        name="pack_q",
    )(selected, queries)


def unpack_output(name, subs, pieces, ks, begun):
    rows = pieces[0].shape[0]
    n = len(pieces)

    def kernel(*refs):
        out_ref, sems = refs[-2:]
        sub = lax.axis_index("sub")
        copies = []
        for i, k in enumerate(ks):
            at = pl.ds(pl.multiple_of((sub ^ k) * QW, QW), QW)
            copies.append(pltpu.make_async_copy(refs[i], out_ref.at[:, at], sems.at[i]))
        for copy in copies:
            copy.start()
        for copy in copies:
            copy.wait()

    return pl.pallas_call(
        kernel,
        in_specs=[VMEM] * n + [ANY] * len(begun),
        out_specs=ANY,
        out_shape=jax.ShapeDtypeStruct((rows, subs * QW), BF16),
        scratch_shapes=[pltpu.SemaphoreType.DMA((n,))],
        input_output_aliases={n: 0} if begun else {},
        cost_estimate=copy_cost(4 * n * rows * QW),
        compiler_params=pltpu.CompilerParams(vmem_limit_bytes=8 * MIB),
        name=name,
    )(*pieces, *begun)


def in_place(*pieces):
    n = len(pieces)

    def kernel(*refs):
        pass

    return pl.pallas_call(
        kernel,
        in_specs=[ANY] * n,
        out_specs=(ANY,) * n,
        out_shape=tuple(jax.ShapeDtypeStruct(piece.shape, piece.dtype) for piece in pieces),
        input_output_aliases={i: i for i in range(n)},
        cost_estimate=copy_cost(4 * n * pieces[0].size),
        compiler_params=pltpu.CompilerParams(vmem_limit_bytes=8 * MIB),
        name="landed",
    )(*pieces)


def attention(
    name, first, last, partners, bases_of, queries, sel, sources, state, state_from=0
):
    parts, rows = len(queries), queries[0].shape[0] - EXTRA
    tiles_in_part = rows // TILE
    tiles_here = len(partners) * tiles_in_part
    r = sources[0].shape[2]
    per_block = BLK // r
    n_src = len(sources)
    slots = [src.shape[0] // per_block for src in sources]
    most = min(TOPK, sum(slots))
    n_q = len(partners)
    n_out = len(partners) if last else 2
    in_block = BLK // TILE
    one_block = parts > 1 and len(partners) * rows == BLK

    def kernel(*refs):
        sel_ref, q_refs = refs[0], refs[1 : 1 + n_q]
        src = refs[1 + n_q : 1 + n_q + n_src]
        rest = refs[1 + n_q + n_src :]
        m_in, acc_in = (None, None) if first else rest[:2]
        rest = rest if first else rest[2:]
        outs, k_buf, v_buf, m_tmp, acc_tmp, q_buf = rest[:n_out], *rest[n_out:]
        level = lax.axis_index("lev")
        sub = lax.axis_index("sub") if parts > 1 else 0
        for i, q_ref in enumerate(q_refs):
            q_buf[i] = q_ref[:rows]
        bases = bases_of(level)

        v_buf[:, HD:] = jnp.ones((sum(slots) * BLK, HD), BF16)
        start = 0
        for ref, base, n in zip(src, bases, slots):

            def fill(ref=ref, start=start, n=n):
                if n * per_block <= 8:
                    k_buf[start * BLK : (start + n) * BLK] = ref[:, 0].reshape(n * BLK, HD)
                    v_buf[start * BLK : (start + n) * BLK, :HD] = ref[:, 1].reshape(n * BLK, HD)
                else:

                    def chunk(i, carry):
                        at = pl.ds(pl.multiple_of(start * BLK + i * r, r), r)
                        k_buf[at] = ref[i, 0]
                        v_buf[at, :HD] = ref[i, 1]
                        return carry

                    lax.fori_loop(0, n * per_block, chunk, 0)

            if isinstance(base, int):
                fill()
            else:
                pl.when(base >= 0)(fill)
            start += n

        def own_part(t, part, at, slot, own, pieces):
            count = pieces * TILE
            keys_at = pl.ds(pl.multiple_of((own - bases[0]) * BLK, BLK), count)
            q_rows = pl.ds(pl.multiple_of(at, TILE), TILE)
            together = PER if pieces <= 2 else TOGETHER
            edge_shape = (together * TILE, TILE)
            key_at = lax.broadcasted_iota(jnp.int32, edge_shape, 1)
            query_at = lax.broadcasted_iota(jnp.int32, edge_shape, 0) & (TILE - 1)

            def scores(c):
                heads = range(c * together, (c + 1) * together)
                q = [q_buf[part, q_rows, j * HD : (j + 1) * HD] for j in heads]
                s = dot_nt(jnp.concatenate(q, axis=0), k_buf[keys_at])
                edge = jnp.where(key_at <= query_at, s[:, count - TILE :], FLOOR)
                if pieces == 1:
                    return edge
                return jnp.concatenate([s[:, : count - TILE], edge], axis=1)

            ready = [scores(c) for c in range(PER // together)]
            for c, s in enumerate(ready):
                here = slice(c * together * TILE, (c + 1) * together * TILE)
                m = jnp.max(s, axis=1, keepdims=True)
                p = jnp.exp2((s - m) * SCALE).astype(BF16)
                m_tmp[slot, here] = jnp.broadcast_to(m, (together * TILE, HD))
                acc_tmp[slot, here] = dot_nn(p, v_buf[keys_at])

        if first and one_block:
            first_part = level * parts
            own = (first_part + (sub ^ partners[0])) * tiles_in_part // in_block
            for i in range(in_block):
                part = own * (in_block // tiles_in_part) + i // tiles_in_part - first_part
                local = (part ^ sub) - partners[0]
                t = local * tiles_in_part + i % tiles_in_part
                own_part(t, local, i % tiles_in_part * TILE, t, own, i + 1)

        def one_tile(k, part, i, out_ref, out_at):
            t = part * tiles_in_part + i
            tile = (level * parts + (sub ^ k)) * tiles_in_part + i
            own = tile // in_block
            q_rows = pl.ds(pl.multiple_of(i * TILE, TILE), TILE)
            if first:
                m_old, acc_old, at_old = m_tmp, acc_tmp, t if one_block else 0
            else:
                m_old, acc_old, at_old = m_in, acc_in, t + (partners[0] - state_from) * tiles_in_part

            def finish(j, acc):
                out_ref[out_at, j * HD : (j + 1) * HD] = (acc[:, :HD] / acc[:, HD:]).astype(BF16)

            def keep(j, m, acc):
                outs[0][t, j * TILE : (j + 1) * TILE] = m
                outs[1][t, j * TILE : (j + 1) * TILE] = acc

            if first and not one_block:
                for pieces in range(1, in_block + 1):
                    pl.when(lax.rem(tile, in_block) == pieces - 1)(
                        functools.partial(own_part, t, part, i * TILE, 0, own, pieces)
                    )

            found = jnp.int32(0)
            where = [jnp.int32(0)] * most
            for e in range(TOPK):
                block = sel_ref[(k * tiles_in_part + i) * TOPK + e]
                start = 0
                for base, n in zip(bases, slots):
                    hit = (block != own) & (block >= base) & (block < base + n)
                    where = [
                        jnp.where(hit & (found == i), start + block - base, w)
                        for i, w in enumerate(where)
                    ]
                    found = found + hit.astype(jnp.int32)
                    start += n

            def others(n):
                together = PER if n <= 1 else TOGETHER
                at = [pl.ds(pl.multiple_of(w * BLK, BLK), BLK) for w in where[:n]]

                def scores(c):
                    heads = range(c * together, (c + 1) * together)
                    q = [q_buf[part, q_rows, j * HD : (j + 1) * HD] for j in heads]
                    q = jnp.concatenate(q, axis=0)
                    s = [dot_nt(q, k_buf[a]) for a in at]
                    return jnp.concatenate(s, axis=1) if n > 1 else s[0]

                chains = range(PER // together)
                ready = [scores(c) for c in chains] if n else None
                for c in chains:
                    here = slice(c * together * TILE, (c + 1) * together * TILE)
                    m = m_old[at_old, here]
                    acc = acc_old[at_old, here]
                    if n:
                        old, s = m, ready[c]
                        m = jnp.maximum(old, jnp.max(s, axis=1, keepdims=True))
                        p = jnp.exp2((s - jnp.tile(m, (1, n * BLK // HD))) * SCALE).astype(BF16)
                        acc = acc * jnp.tile(jnp.exp2((old - m) * SCALE), (1, 2))
                        for i, a in enumerate(at):
                            acc = acc + dot_nn(p[:, i * BLK : (i + 1) * BLK], v_buf[a])
                    for i in range(together):
                        j, rows_of = c * together + i, slice(i * TILE, (i + 1) * TILE)
                        if last:
                            finish(j, acc[rows_of])
                        else:
                            keep(j, m[rows_of], acc[rows_of])

            for n in range(most + 1):
                pl.when(found == n)(functools.partial(others, n))

        if last:
            for part, (out_ref, k) in enumerate(zip(outs, partners)):

                def step(i, carry, out_ref=out_ref, k=k, part=part):
                    out_at = pl.ds(pl.multiple_of(i * TILE, TILE), TILE)
                    one_tile(k, part, i, out_ref, out_at)
                    return carry

                lax.fori_loop(0, tiles_in_part, step, 0)
        else:

            def step(t, carry):
                part = t // tiles_in_part
                one_tile(partners[0] + part, part, lax.rem(t, tiles_in_part), None, None)
                return carry

            lax.fori_loop(0, tiles_here, step, 0)

    if last:
        out_shape = tuple(jax.ShapeDtypeStruct((rows, QW), BF16) for _ in partners)
    else:
        out_shape = (
            jax.ShapeDtypeStruct((tiles_here, QW, HD), F32),
            jax.ShapeDtypeStruct((tiles_here, QW, 2 * HD), F32),
        )
    work = tiles_here * QW * BLK * 3 // 2
    return pl.pallas_call(
        kernel,
        in_specs=[SMEM] + [VMEM] * (n_q + n_src + len(state)),
        out_shape=out_shape,
        out_specs=(VMEM,) * n_out,
        scratch_shapes=[
            pltpu.VMEM((sum(slots) * BLK, HD), BF16),
            pltpu.VMEM((sum(slots) * BLK, 2 * HD), BF16),
            pltpu.VMEM((tiles_here if one_block else 1, QW, HD), F32),
            pltpu.VMEM((tiles_here if one_block else 1, QW, 2 * HD), F32),
            pltpu.VMEM((n_q, rows, QW), BF16),
        ],
        compiler_params=pltpu.CompilerParams(
            vmem_limit_bytes=(24 if sum(slots) <= 16 else 56) * MIB
        ),
        cost_estimate=pl.CostEstimate(
            flops=8 * work * HD, transcendentals=work, bytes_accessed=4 * MIB
        ),
        name=name,
    )(sel, *[queries[k] for k in partners], *sources, *state)


def body(levels, subs, heads, queries, keys, values, selected):
    rows = queries.shape[0]
    tiles_here = selected.shape[0]
    level_blocks = subs * rows // BLK
    by_levels = levels == 4 and subs >= 4 and subs * rows % (2 * BLK) == 0

    def exchange(pieces, ks):
        return tuple(
            lax.ppermute(piece, "sub", [(i, i ^ k) for i in range(subs)]) if k else piece
            for k, piece in zip(ks, pieces)
        )

    everyone = tuple(range(subs))
    packed = pack_keys_values(subs, heads, keys, values)
    if by_levels:
        raw = lax.ppermute(packed, "lev", [(1, 3), (0, 1)])
    own = lax.all_to_all(packed, ("sub", "head"), 0, 0, tiled=True)
    q = pack_queries(subs, queries, selected)
    hop = subs // 2
    if hop > 1:
        over = exchange(q[hop:], [hop] * hop)
        q = exchange(q[:hop], range(hop)) + exchange(over, range(hop))
    else:
        q = exchange(q, everyone)
    if by_levels:
        own, raw = lax.optimization_barrier((own, raw))
        half = own.shape[0] // 2
        halves = lax.optimization_barrier((own[:half], own[half:]))
        up = [lax.ppermute(piece, "lev", [(0, 2), (2, 3)]) for piece in halves]
        p2 = lax.all_to_all(raw, ("sub", "head"), 0, 0, tiled=True)
        q, _ = lax.optimization_barrier((q, up))
        sel = jnp.concatenate([piece[rows, : tiles_here * TOPK] for piece in q]).astype(jnp.int32)
        forwards = lax.axis_index("lev") == 2
        last_up = [
            lax.ppermute(jnp.where(forwards, a, b), "lev", [(2, 3), (1, 2)])
            for a, b in zip(up, halves)
        ]

        def at(level, *which):
            base = jnp.int32(NONE)
            for here, holds in which:
                base = jnp.where(level == here, holds * level_blocks, base)
            return base

        def in_halves(base):
            return (base, base + level_blocks // 2)

        def early(level):
            return (
                level * level_blocks,
                *in_halves(at(level, (2, 0), (3, 2))),
                at(level, (1, 0), (3, 1)),
            )

        def late(level):
            return in_halves(at(level, (2, 1), (3, 0)))

        def whole_range(level):
            return early(level) + late(level)

        far, near = everyone[subs // 2 :], everyone[: subs // 2]
        state = attention(
            "far_early", True, False, far, early, q, sel, (own, *up, p2), ()
        )
        out_far = ()
        for k in far:
            out_far += attention(
                "far_late", False, True, (k,), late, q, sel, tuple(last_up), state, far[0]
            )
        q_near, _ = lax.optimization_barrier((q[: subs // 2], out_far))
        q = tuple(q_near) + tuple(q[subs // 2 :])
        out_near = attention(
            "near", True, True, near, whole_range, q, sel, (own, *up, p2, *last_up), ()
        )
        out_near, out_far = exchange(out_near, near), exchange(out_far, far)
        landed = in_place(*out_far)
        return unpack_output("unpack", subs, (*landed, *out_near), (*far, *near), ())
    sel = jnp.concatenate([piece[rows, : tiles_here * TOPK] for piece in q]).astype(jnp.int32)
    whole = lax.all_gather(own, "lev", axis=0, tiled=True)
    out = attention("all", True, True, everyone, lambda level: (0,), q, sel, (whole,), ())
    if subs == 1:
        return out[0]
    return unpack_output("unpack", subs, exchange(out, everyone), everyone, ())


def solution(mesh):
    ctx, heads = mesh.shape["ctx"], mesh.shape["head"]
    subs = math.gcd(KVH // heads, ctx)
    if subs * heads != KVH:
        raise ValueError("unsupported mesh")
    levels = ctx // subs
    split = Mesh(mesh.devices.reshape(levels, subs, heads), ("lev", "sub", "head"))
    placed = (
        P(("lev", "sub"), "head"),
        P(("lev", "sub", "head"), None),
        P(("lev", "sub", "head"), None),
        P(("lev", "sub"), "head", None),
    )
    return jax.shard_map(
        functools.partial(body, levels, subs, heads),
        mesh=split,
        in_specs=placed,
        out_specs=P(("lev", "sub"), "head"),
        check_vma=False,
    )
```

```python
import functools
import math

import jax
import jax.numpy as jnp
from jax import lax
from jax.experimental import pallas as pl
from jax.experimental.pallas import tpu as pltpu
from jax.sharding import Mesh, PartitionSpec as P

HD = 128
QH = 32
KVH = 8
BLK = 512
TILE = 128
TOPK = 3
PER = QH // KVH
QW = PER * HD
EXTRA = 16
TOGETHER = 2

FLOOR = -1e30
SCALE = HD ** -0.5 * math.log2(math.e)
NONE = -100000
F32 = jnp.float32
BF16 = jnp.bfloat16
VMEM = pl.BlockSpec(memory_space=pltpu.VMEM)
SMEM = pl.BlockSpec(memory_space=pltpu.SMEM)
ANY = pl.BlockSpec(memory_space=pl.ANY)
MIB = 1024 * 1024


def dot_nt(a, b):
    return lax.dot_general(a, b, (((1,), (1,)), ((), ())), preferred_element_type=F32)


def dot_nn(a, b):
    return lax.dot_general(a, b, (((1,), (0,)), ((), ())), preferred_element_type=F32)


def copy_cost(bytes_moved):
    return pl.CostEstimate(flops=0, transcendentals=0, bytes_accessed=bytes_moved)


def pack_keys_values(subs, heads, keys, values):
    r = keys.shape[0]

    def kernel(k_ref, v_ref, out_ref):
        for sub in range(subs):
            for head in range(heads):
                at = (head * subs + sub) * HD
                out_ref[sub * heads + head, 0] = k_ref[:, at : at + HD]
                out_ref[sub * heads + head, 1] = v_ref[:, at : at + HD]

    return pl.pallas_call(
        kernel,
        in_specs=[VMEM, VMEM],
        out_specs=VMEM,
        out_shape=jax.ShapeDtypeStruct((subs * heads, 2, r, HD), BF16),
        cost_estimate=copy_cost(4 * keys.size * 2),
        name="pack_kv",
    )(keys, values)


def pack_queries(subs, queries, selected):
    rows = queries.shape[0]
    tiles_here = selected.shape[0]

    def kernel(sel_ref, q_ref, *outs):
        sub = lax.axis_index("sub") if subs > 1 else 0
        lane = lax.broadcasted_iota(jnp.int32, (EXTRA, QW), 1)
        for k, out_ref in enumerate(outs):
            head = sub ^ k
            out_ref[:rows] = q_ref[:, pl.ds(pl.multiple_of(head * QW, QW), QW)]
            row = jnp.zeros((EXTRA, QW), jnp.int32)
            for t in range(tiles_here):
                for e in range(TOPK):
                    row = jnp.where(lane == t * TOPK + e, sel_ref[t, head, e], row)
            out_ref[rows:] = row.astype(F32).astype(BF16)

    return pl.pallas_call(
        kernel,
        in_specs=[SMEM, VMEM],
        out_specs=(VMEM,) * subs,
        out_shape=(jax.ShapeDtypeStruct((rows + EXTRA, QW), BF16),) * subs,
        cost_estimate=copy_cost(2 * queries.size * 2),
        compiler_params=pltpu.CompilerParams(vmem_limit_bytes=8 * MIB),
        name="pack_q",
    )(selected, queries)


def unpack_output(name, subs, pieces, ks, begun):
    rows = pieces[0].shape[0]
    n = len(pieces)

    def kernel(*refs):
        out_ref, sems = refs[-2:]
        sub = lax.axis_index("sub")
        copies = []
        for i, k in enumerate(ks):
            at = pl.ds(pl.multiple_of((sub ^ k) * QW, QW), QW)
            copies.append(pltpu.make_async_copy(refs[i], out_ref.at[:, at], sems.at[i]))
        for copy in copies:
            copy.start()
        for copy in copies:
            copy.wait()

    return pl.pallas_call(
        kernel,
        in_specs=[VMEM] * n + [ANY] * len(begun),
        out_specs=ANY,
        out_shape=jax.ShapeDtypeStruct((rows, subs * QW), BF16),
        scratch_shapes=[pltpu.SemaphoreType.DMA((n,))],
        input_output_aliases={n: 0} if begun else {},
        cost_estimate=copy_cost(4 * n * rows * QW),
        compiler_params=pltpu.CompilerParams(vmem_limit_bytes=8 * MIB),
        name=name,
    )(*pieces, *begun)


def in_place(*pieces):
    n = len(pieces)

    def kernel(*refs):
        pass

    return pl.pallas_call(
        kernel,
        in_specs=[ANY] * n,
        out_specs=(ANY,) * n,
        out_shape=tuple(jax.ShapeDtypeStruct(piece.shape, piece.dtype) for piece in pieces),
        input_output_aliases={i: i for i in range(n)},
        cost_estimate=copy_cost(4 * n * pieces[0].size),
        compiler_params=pltpu.CompilerParams(vmem_limit_bytes=8 * MIB),
        name="landed",
    )(*pieces)


def attention(
    name, first, last, partners, bases_of, queries, sel, sources, state, state_from=0
):
    parts, rows = len(queries), queries[0].shape[0] - EXTRA
    tiles_in_part = rows // TILE
    tiles_here = len(partners) * tiles_in_part
    r = sources[0].shape[2]
    per_block = BLK // r
    n_src = len(sources)
    slots = [src.shape[0] // per_block for src in sources]
    most = min(TOPK, sum(slots))
    n_q = len(partners)
    n_out = len(partners) if last else 2
    in_block = BLK // TILE
    one_block = parts > 1 and len(partners) * rows == BLK

    def kernel(*refs):
        sel_ref, q_refs = refs[0], refs[1 : 1 + n_q]
        src = refs[1 + n_q : 1 + n_q + n_src]
        rest = refs[1 + n_q + n_src :]
        m_in, acc_in = (None, None) if first else rest[:2]
        rest = rest if first else rest[2:]
        outs, k_buf, v_buf, m_tmp, acc_tmp, q_buf = rest[:n_out], *rest[n_out:]
        level = lax.axis_index("lev")
        sub = lax.axis_index("sub") if parts > 1 else 0
        for i, q_ref in enumerate(q_refs):
            q_buf[i] = q_ref[:rows]
        bases = bases_of(level)

        v_buf[:, HD:] = jnp.ones((sum(slots) * BLK, HD), BF16)
        start = 0
        for ref, base, n in zip(src, bases, slots):

            def fill(ref=ref, start=start, n=n):
                if n * per_block <= 8:
                    k_buf[start * BLK : (start + n) * BLK] = ref[:, 0].reshape(n * BLK, HD)
                    v_buf[start * BLK : (start + n) * BLK, :HD] = ref[:, 1].reshape(n * BLK, HD)
                else:

                    def chunk(i, carry):
                        at = pl.ds(pl.multiple_of(start * BLK + i * r, r), r)
                        k_buf[at] = ref[i, 0]
                        v_buf[at, :HD] = ref[i, 1]
                        return carry

                    lax.fori_loop(0, n * per_block, chunk, 0)

            if isinstance(base, int):
                fill()
            else:
                pl.when(base >= 0)(fill)
            start += n

        def own_part(t, part, at, slot, own, pieces):
            count = pieces * TILE
            keys_at = pl.ds(pl.multiple_of((own - bases[0]) * BLK, BLK), count)
            q_rows = pl.ds(pl.multiple_of(at, TILE), TILE)
            together = PER if pieces <= 2 else TOGETHER
            edge_shape = (together * TILE, TILE)
            key_at = lax.broadcasted_iota(jnp.int32, edge_shape, 1)
            query_at = lax.broadcasted_iota(jnp.int32, edge_shape, 0) & (TILE - 1)

            def scores(c):
                heads = range(c * together, (c + 1) * together)
                q = [q_buf[part, q_rows, j * HD : (j + 1) * HD] for j in heads]
                s = dot_nt(jnp.concatenate(q, axis=0), k_buf[keys_at])
                edge = jnp.where(key_at <= query_at, s[:, count - TILE :], FLOOR)
                if pieces == 1:
                    return edge
                return jnp.concatenate([s[:, : count - TILE], edge], axis=1)

            ready = [scores(c) for c in range(PER // together)]
            for c, s in enumerate(ready):
                here = slice(c * together * TILE, (c + 1) * together * TILE)
                m = jnp.max(s, axis=1, keepdims=True)
                p = jnp.exp2((s - m) * SCALE).astype(BF16)
                m_tmp[slot, here] = jnp.broadcast_to(m, (together * TILE, HD))
                acc_tmp[slot, here] = dot_nn(p, v_buf[keys_at])

        if first and one_block:
            first_part = level * parts
            own = (first_part + (sub ^ partners[0])) * tiles_in_part // in_block
            for i in range(in_block):
                part = own * (in_block // tiles_in_part) + i // tiles_in_part - first_part
                local = (part ^ sub) - partners[0]
                t = local * tiles_in_part + i % tiles_in_part
                own_part(t, local, i % tiles_in_part * TILE, t, own, i + 1)

        def one_tile(k, part, i, out_ref, out_at):
            t = part * tiles_in_part + i
            tile = (level * parts + (sub ^ k)) * tiles_in_part + i
            own = tile // in_block
            q_rows = pl.ds(pl.multiple_of(i * TILE, TILE), TILE)
            if first:
                m_old, acc_old, at_old = m_tmp, acc_tmp, t if one_block else 0
            else:
                m_old, acc_old, at_old = m_in, acc_in, t + (partners[0] - state_from) * tiles_in_part

            def finish(j, acc):
                out_ref[out_at, j * HD : (j + 1) * HD] = (acc[:, :HD] * pl.reciprocal(acc[:, HD:])).astype(BF16)

            def keep(j, m, acc):
                outs[0][t, j * TILE : (j + 1) * TILE] = m
                outs[1][t, j * TILE : (j + 1) * TILE] = acc

            if first and not one_block:
                for pieces in range(1, in_block + 1):
                    pl.when(lax.rem(tile, in_block) == pieces - 1)(
                        functools.partial(own_part, t, part, i * TILE, 0, own, pieces)
                    )

            found = jnp.int32(0)
            where = [jnp.int32(0)] * most
            for e in range(TOPK):
                block = sel_ref[(k * tiles_in_part + i) * TOPK + e]
                start = 0
                for base, n in zip(bases, slots):
                    hit = (block != own) & (block >= base) & (block < base + n)
                    where = [
                        jnp.where(hit & (found == i), start + block - base, w)
                        for i, w in enumerate(where)
                    ]
                    found = found + hit.astype(jnp.int32)
                    start += n

            def others(n):
                at = [pl.ds(pl.multiple_of(w * BLK, BLK), BLK) for w in where[:n]]

                def scores(c):
                    heads = range(c * TOGETHER, (c + 1) * TOGETHER)
                    q = [q_buf[part, q_rows, j * HD : (j + 1) * HD] for j in heads]
                    q = jnp.concatenate(q, axis=0)
                    s = [dot_nt(q, k_buf[a]) for a in at]
                    return jnp.concatenate(s, axis=1) if n > 1 else s[0]

                chains = range(PER // TOGETHER)
                ready = [scores(c) for c in chains] if n else None
                for c in chains:
                    here = slice(c * TOGETHER * TILE, (c + 1) * TOGETHER * TILE)
                    m = m_old[at_old, here]
                    acc = acc_old[at_old, here]
                    if n:
                        old, s = m, ready[c]
                        m = jnp.maximum(old, jnp.max(s, axis=1, keepdims=True))
                        p = jnp.exp2((s - jnp.tile(m, (1, n * BLK // HD))) * SCALE).astype(BF16)
                        acc = acc * jnp.tile(jnp.exp2((old - m) * SCALE), (1, 2))
                        for i, a in enumerate(at):
                            acc = acc + dot_nn(p[:, i * BLK : (i + 1) * BLK], v_buf[a])
                    for i in range(TOGETHER):
                        j, rows_of = c * TOGETHER + i, slice(i * TILE, (i + 1) * TILE)
                        if last:
                            finish(j, acc[rows_of])
                        else:
                            keep(j, m[rows_of], acc[rows_of])

            for n in range(most + 1):
                pl.when(found == n)(functools.partial(others, n))

        if last:
            for part, (out_ref, k) in enumerate(zip(outs, partners)):

                def step(i, carry, out_ref=out_ref, k=k, part=part):
                    out_at = pl.ds(pl.multiple_of(i * TILE, TILE), TILE)
                    one_tile(k, part, i, out_ref, out_at)
                    return carry

                lax.fori_loop(0, tiles_in_part, step, 0)
        else:

            def step(t, carry):
                part = t // tiles_in_part
                one_tile(partners[0] + part, part, lax.rem(t, tiles_in_part), None, None)
                return carry

            lax.fori_loop(0, tiles_here, step, 0)

    if last:
        out_shape = tuple(jax.ShapeDtypeStruct((rows, QW), BF16) for _ in partners)
    else:
        out_shape = (
            jax.ShapeDtypeStruct((tiles_here, QW, HD), F32),
            jax.ShapeDtypeStruct((tiles_here, QW, 2 * HD), F32),
        )
    work = tiles_here * QW * BLK * 3 // 2
    return pl.pallas_call(
        kernel,
        in_specs=[SMEM] + [VMEM] * (n_q + n_src + len(state)),
        out_shape=out_shape,
        out_specs=(VMEM,) * n_out,
        scratch_shapes=[
            pltpu.VMEM((sum(slots) * BLK, HD), BF16),
            pltpu.VMEM((sum(slots) * BLK, 2 * HD), BF16),
            pltpu.VMEM((tiles_here if one_block else 1, QW, HD), F32),
            pltpu.VMEM((tiles_here if one_block else 1, QW, 2 * HD), F32),
            pltpu.VMEM((n_q, rows, QW), BF16),
        ],
        compiler_params=pltpu.CompilerParams(
            vmem_limit_bytes=(24 if sum(slots) <= 16 else 56) * MIB
        ),
        cost_estimate=pl.CostEstimate(
            flops=8 * work * HD, transcendentals=work, bytes_accessed=4 * MIB
        ),
        name=name,
    )(sel, *[queries[k] for k in partners], *sources, *state)


def body(levels, subs, heads, queries, keys, values, selected):
    rows = queries.shape[0]
    tiles_here = selected.shape[0]
    level_blocks = subs * rows // BLK
    by_levels = levels == 4 and subs >= 4 and subs * rows % (2 * BLK) == 0

    def exchange(pieces, ks):
        return tuple(
            lax.ppermute(piece, "sub", [(i, i ^ k) for i in range(subs)]) if k else piece
            for k, piece in zip(ks, pieces)
        )

    everyone = tuple(range(subs))
    packed = pack_keys_values(subs, heads, keys, values)
    if by_levels:
        raw = lax.ppermute(packed, "lev", [(1, 3), (0, 1)])
    own = lax.all_to_all(packed, ("sub", "head"), 0, 0, tiled=True)
    q = pack_queries(subs, queries, selected)
    hop = subs // 2
    if hop > 1:
        over = exchange(q[hop:], [hop] * hop)
        q = exchange(q[:hop], range(hop)) + exchange(over, range(hop))
    else:
        q = exchange(q, everyone)
    if by_levels:
        own, raw = lax.optimization_barrier((own, raw))
        half = own.shape[0] // 2
        halves = lax.optimization_barrier((own[:half], own[half:]))
        up = [lax.ppermute(piece, "lev", [(0, 2), (2, 3)]) for piece in halves]
        p2 = lax.all_to_all(raw, ("sub", "head"), 0, 0, tiled=True)
        q, _ = lax.optimization_barrier((q, up))
        sel = jnp.concatenate([piece[rows, : tiles_here * TOPK] for piece in q]).astype(jnp.int32)
        forwards = lax.axis_index("lev") == 2
        last_up = [
            lax.ppermute(jnp.where(forwards, a, b), "lev", [(2, 3), (1, 2)])
            for a, b in zip(up, halves)
        ]

        def at(level, *which):
            base = jnp.int32(NONE)
            for here, holds in which:
                base = jnp.where(level == here, holds * level_blocks, base)
            return base

        def in_halves(base):
            return (base, base + level_blocks // 2)

        def early(level):
            return (
                level * level_blocks,
                *in_halves(at(level, (2, 0), (3, 2))),
                at(level, (1, 0), (3, 1)),
            )

        def late(level):
            return in_halves(at(level, (2, 1), (3, 0)))

        def whole_range(level):
            return early(level) + late(level)

        far, near = everyone[subs // 2 :], everyone[: subs // 2]
        state = attention(
            "far_early", True, False, far, early, q, sel, (own, *up, p2), ()
        )
        out_far = ()
        for k in far:
            out_far += attention(
                "far_late", False, True, (k,), late, q, sel, tuple(last_up), state, far[0]
            )
        q_near, _ = lax.optimization_barrier((q[: subs // 2], out_far))
        q = tuple(q_near) + tuple(q[subs // 2 :])
        out_near = attention(
            "near", True, True, near, whole_range, q, sel, (own, *up, p2, *last_up), ()
        )
        out_near, out_far = exchange(out_near, near), exchange(out_far, far)
        landed = in_place(*out_far)
        return unpack_output("unpack", subs, (*landed, *out_near), (*far, *near), ())
    sel = jnp.concatenate([piece[rows, : tiles_here * TOPK] for piece in q]).astype(jnp.int32)
    whole = lax.all_gather(own, "lev", axis=0, tiled=True)
    out = attention("all", True, True, everyone, lambda level: (0,), q, sel, (whole,), ())
    if subs == 1:
        return out[0]
    return unpack_output("unpack", subs, exchange(out, everyone), everyone, ())


def solution(mesh):
    ctx, heads = mesh.shape["ctx"], mesh.shape["head"]
    subs = math.gcd(KVH // heads, ctx)
    if subs * heads != KVH:
        raise ValueError("unsupported mesh")
    levels = ctx // subs
    split = Mesh(mesh.devices.reshape(levels, subs, heads), ("lev", "sub", "head"))
    placed = (
        P(("lev", "sub"), "head"),
        P(("lev", "sub", "head"), None),
        P(("lev", "sub", "head"), None),
        P(("lev", "sub"), "head", None),
    )
    return jax.shard_map(
        functools.partial(body, levels, subs, heads),
        mesh=split,
        in_specs=placed,
        out_specs=P(("lev", "sub"), "head"),
        check_vma=False,
    )
```
